256 devices in a mesh: lon: 64 (over z, y_hi, x), lat: 4 (over y_lo, core).
Axes of the slice: x: 4, y: 4 (y_hi: 2, y_lo: 2; y = y_hi * 2 + y_lo), z: 8, core: 2. Of those that a mesh axis runs over, the one named last changes fastest.
Arguments:
- thermal_anomaly: float32 [32, 512, 512], P(None, 'lon', 'lat'), may hold values from -5 to 5
- saltiness_anomaly: float32 [32, 512, 512], P(None, 'lon', 'lat'), may hold values from -5 to 5
- zonal_flow: float32 [32, 512, 512], P(None, 'lon', 'lat'), may hold values from -1.2 to 1.2
- meridional_flow: float32 [32, 512, 512], P(None, 'lon', 'lat'), may hold values from -1.2 to 1.2
- submerged_strata_number: int32 [512, 512], P('lon', 'lat'), may hold values from 1 to 32
- sea_indicator: int32 [512, 512], P('lon', 'lat'), may hold values 0 or 1
- strata_thickness: float32 [32], replicated, may hold values from 0.5 to 2
- earlier_sea_elevation: float32 [512, 512], P('lon', 'lat'), may hold values from -3 to 3
- sea_drive_term: float32 [512, 512], P('lon', 'lat'), may hold values from -10 to 10
Outputs:
- new_temperature: float32 [32, 512, 512], P(None, 'lon', 'lat')
- new_salinity: float32 [32, 512, 512], P(None, 'lon', 'lat')
- new_u_velocity: float32 [32, 512, 512], P(None, 'lon', 'lat')
- new_v_velocity: float32 [32, 512, 512], P(None, 'lon', 'lat')
- new_surface: float32 [512, 512], P('lon', 'lat')
- residual_rms: float32 [], replicated
The draws below stay inside these ranges and needn't reach their ends.
All inputs are finite; a program needn't handle non-finite values. No bound on the sum of `sea_indicator` on one device may be relied on, other than what follows from the above.
Results may differ from the reference program's by a relative error of at most 0.0003.
Values sent between devices are 32-bit elements; how exact they have to be, the bound alone decides.
No kernel may reach another device: no remote copies, remote signals or barrier semaphores. Data moves between devices by JAX's collectives and lax.ppermute only.
A program may use at most 128 MiB of HBM per device.

```python
import math
import jax
import jax.numpy as jnp
from jax import lax

STRATA_TOTAL = 32
CLON = 8
ITERS = 4
ZONAL_POINTS = 512
MERIDIAN_ROWS = 512
N_LON = 64


def draw_sea_drive_term(key, part):
    key_rough = jax.random.fold_in(jax.random.fold_in(key, 11), 0)
    growth = 1.0 + 2.0 * jnp.arange(ZONAL_POINTS, dtype=jnp.float32)[:, None] / (ZONAL_POINTS - 1)
    random_part = jnp.clip(jax.random.normal(key_rough, (ZONAL_POINTS, MERIDIAN_ROWS), jnp.float32), -4.0, 4.0)
    return 0.5 * growth * random_part


def touch_ends(result, key, smallest, top_value):
    shape = result.shape
    spot = [jax.random.randint(jax.random.fold_in(key, axis), (), 0, shape[axis]) for axis in range(len(shape))]
    result = result.at[tuple(spot)].set(smallest)
    longest = shape.index(max(shape))
    spot[longest] = (spot[longest] + 1) % shape[longest]
    return result.at[tuple(spot)].set(top_value)


def block_scale(key, shape, pieces, low, high):
    gain, own = 1.0, jax.random.fold_in(key, 6)
    for axis_at, shards_of in pieces:
        steps = jnp.exp(jax.random.uniform(jax.random.fold_in(own, axis_at), (shards_of,), jnp.float32, low / len(pieces), high / len(pieces)))
        gain = gain * jnp.repeat(steps, shape[axis_at] // shards_of).reshape([-1 if axis == axis_at else 1 for axis in range(len(shape))])
    return gain


def normal_values(rng, dims, scale, limit, shards=(), kind=jnp.bfloat16):
    entries = scale * jax.random.normal(rng, dims, jnp.float32)
    if shards:
        entries = entries * block_scale(rng, dims, shards, -0.22, 0.18)
    return jnp.clip(entries, -limit, limit).astype(kind)


def setup_inputs(seed: int = 0) -> dict:
    streams_of = jax.random.split(jax.random.key(seed), 10)
    return {
        "thermal_anomaly": normal_values(streams_of[0], (STRATA_TOTAL, ZONAL_POINTS, MERIDIAN_ROWS), 1.0, 5.0, ((1, 64), (2, 4)), jnp.float32),
        "saltiness_anomaly": normal_values(streams_of[1], (STRATA_TOTAL, ZONAL_POINTS, MERIDIAN_ROWS), 1.0, 5.0, ((1, 64), (2, 4)), jnp.float32),
        "zonal_flow": normal_values(streams_of[2], (STRATA_TOTAL, ZONAL_POINTS, MERIDIAN_ROWS), 0.3, 1.2, ((1, 64), (2, 4)), jnp.float32),
        "meridional_flow": normal_values(streams_of[3], (STRATA_TOTAL, ZONAL_POINTS, MERIDIAN_ROWS), 0.3, 1.2, ((1, 64), (2, 4)), jnp.float32),
        "submerged_strata_number": touch_ends(jax.random.randint(streams_of[4], (ZONAL_POINTS, MERIDIAN_ROWS), 1, STRATA_TOTAL + 1), jax.random.fold_in(streams_of[4], 1), 1, STRATA_TOTAL).astype(jnp.int32),
        "sea_indicator": touch_ends((jax.random.randint(streams_of[5], (ZONAL_POINTS, MERIDIAN_ROWS), 0, 5) < 4).astype(jnp.int32), jax.random.fold_in(streams_of[5], 1), 0, 1),
        "strata_thickness": jnp.clip(jnp.exp(jax.random.uniform(streams_of[6], (STRATA_TOTAL,), jnp.float32, math.log(0.5), math.log(2.0))), 0.5, 2.0),
        "earlier_sea_elevation": normal_values(streams_of[7], (ZONAL_POINTS, MERIDIAN_ROWS), 0.5, 3.0, ((0, 64), (1, 4)), jnp.float32),
        "sea_drive_term": draw_sea_drive_term(jax.random.fold_in(streams_of[9], 71), 0),
    }


DIFFUSION = 0.15
MIXING = 0.1
EXPANSION = 0.2
CONTRACTION = 0.15
PRESSURE_SCALE = 0.02
CORIOLIS = 0.5
FRICTION = 0.01
DIVERGENCE = 0.3
STORAGE = 0.1
SPECTRUM_LOW = 0.1
SPECTRUM_HIGH = 1.9
GRAVITY = 0.3
EPSILON = 1e-06

def extend(field, sign_rows, width):
    folded = jnp.flip(field[:, :, MERIDIAN_ROWS - width:], (1, 2)) * sign_rows[:, None, None]
    southern = jnp.zeros((field.shape[0], ZONAL_POINTS, width), field.dtype)
    padded = jnp.concatenate([southern, field, folded], axis=2)
    return jnp.concatenate([padded[:, ZONAL_POINTS - width:], padded, padded[:, :width]], axis=1)

def center(field):
    return field[:, 1:-1, 1:-1]

def to_east(field):
    return field[:, 2:, 1:-1]

def to_west(field):
    return field[:, :-2, 1:-1]

def to_north(field):
    return field[:, 1:-1, 2:]

def to_south(field):
    return field[:, 1:-1, :-2]

def shrink(field):
    return field[:, 1:-1, 1:-1]

def level_mask(strata_bottoms, strata_indices):
    level_index = jnp.arange(strata_indices).astype(strata_bottoms.dtype)[:, None, None]
    return jnp.where(level_index + 0.5 < strata_bottoms, 1.0, 0.0).astype(strata_bottoms.dtype)

def laplace(field, mask):
    middle = center(field)
    total = to_east(mask) * (to_east(field) - middle) + to_west(mask) * (to_west(field) - middle)
    total = total + to_north(mask) * (to_north(field) - middle) + to_south(mask) * (to_south(field) - middle)
    return center(mask) * total

def tracer_step(tracer, u_field, v_field, mask, thickness):
    middle = center(tracer)
    wet_mid = center(mask)
    u_mid = center(u_field)
    v_mid = center(v_field)
    flux_east = wet_mid * to_east(mask) * (0.5 * (u_mid + to_east(u_field)) * 0.5 * (middle + to_east(tracer)) - DIFFUSION * (to_east(tracer) - middle))
    flux_west = wet_mid * to_west(mask) * (0.5 * (to_west(u_field) + u_mid) * 0.5 * (to_west(tracer) + middle) - DIFFUSION * (middle - to_west(tracer)))
    flux_north = wet_mid * to_north(mask) * (0.5 * (v_mid + to_north(v_field)) * 0.5 * (middle + to_north(tracer)) - DIFFUSION * (to_north(tracer) - middle))
    flux_south = wet_mid * to_south(mask) * (0.5 * (to_south(v_field) + v_mid) * 0.5 * (to_south(tracer) + middle) - DIFFUSION * (middle - to_south(tracer)))
    horizontal = flux_west - flux_east + flux_south - flux_north
    spacing = 0.5 * (thickness[1:] + thickness[:-1])
    vflux = wet_mid[1:] * wet_mid[:-1] * (middle[1:] - middle[:-1]) / spacing[:, None, None]
    zero_plane = jnp.zeros_like(middle[:1])
    upper_flux = jnp.concatenate([vflux, zero_plane], axis=0)
    lower_flux = jnp.concatenate([zero_plane, vflux], axis=0)
    vertical = MIXING * (upper_flux - lower_flux) / thickness[:, None, None]
    return wet_mid * (middle + horizontal + vertical)

def pressure_gradients(temp_rim, salt_rim, mask, thickness):
    density = (CONTRACTION * salt_rim - EXPANSION * temp_rim) * thickness[:, None, None] * mask
    pressure = jnp.cumsum(density, axis=0)
    middle = center(pressure)
    wet_mid = center(mask)
    grad_x = 0.5 * wet_mid * (to_east(mask) * (to_east(pressure) - middle) + to_west(mask) * (middle - to_west(pressure)))
    grad_y = 0.5 * wet_mid * (to_north(mask) * (to_north(pressure) - middle) + to_south(mask) * (middle - to_south(pressure)))
    return (grad_x, grad_y)

def baroclinic(narrow, mask_narrow, lap_u, lap_v, thickness, coriolis, strata_indices):
    temp_rim = narrow[:strata_indices]
    salt_rim = narrow[strata_indices:2 * strata_indices]
    u_rim = narrow[2 * strata_indices:3 * strata_indices]
    v_rim = narrow[3 * strata_indices:4 * strata_indices]
    new_temp = tracer_step(temp_rim, u_rim, v_rim, mask_narrow, thickness)
    new_salt = tracer_step(salt_rim, u_rim, v_rim, mask_narrow, thickness)
    grad_x, grad_y = pressure_gradients(temp_rim, salt_rim, mask_narrow, thickness)
    friction_u = laplace(lap_u, mask_narrow)
    friction_v = laplace(lap_v, mask_narrow)
    wet_mid = center(mask_narrow)
    u_mid = center(u_rim)
    v_mid = center(v_rim)
    u_star = wet_mid * (u_mid + coriolis * v_mid - PRESSURE_SCALE * grad_x - FRICTION * friction_u)
    v_star = wet_mid * (v_mid - coriolis * u_mid - PRESSURE_SCALE * grad_y - FRICTION * friction_v)
    height = lax.optimization_barrier(jnp.sum(thickness[:, None, None] * mask_narrow, axis=0, keepdims=True))
    return (new_temp, new_salt, u_star, v_star, height, wet_mid)

def solver_weights(height, strata_indices):
    middle = center(height)
    w_east = jnp.minimum(middle, to_east(height)) / strata_indices
    w_west = jnp.minimum(middle, to_west(height)) / strata_indices
    w_north = jnp.minimum(middle, to_north(height)) / strata_indices
    w_south = jnp.minimum(middle, to_south(height)) / strata_indices
    diagonal = STORAGE + w_east + w_west + w_north + w_south
    return (w_east, w_west, w_north, w_south, diagonal)

def apply_operator(weights, field_rim):
    w_east, w_west, w_north, w_south, diagonal = weights
    coupled = w_east * to_east(field_rim) + w_west * to_west(field_rim) + w_north * to_north(field_rim) + w_south * to_south(field_rim)
    return diagonal * center(field_rim) - coupled

def line_factor(w_west, w_east, diagonal):
    count = diagonal.shape[0]
    position = jnp.arange(count).reshape((count,) + (1,) * (diagonal.ndim - 1))
    lower_band = jnp.where(position > 0, -w_west, 0.0)
    upper_band = jnp.where(position < count - 1, -w_east, 0.0)

    def forward(previous, inputs):
        lower_row, diag_row, upper_row = inputs
        inverse = 1.0 / (diag_row - lower_row * previous)
        factor = upper_row * inverse
        return (factor, (factor, inverse))
    _, (factors, pivots) = lax.scan(forward, jnp.zeros_like(diagonal[0]), (lower_band, diagonal, upper_band))
    return (lower_band, factors, pivots)

def line_solve(lower_band, factors, pivots, values):

    def forward(previous, inputs):
        lower_row, inverse, value_row = inputs
        current = (value_row - lower_row * previous) * inverse
        return (current, current)
    _, partial_rows = lax.scan(forward, jnp.zeros_like(values[0]), (lower_band, pivots, values))

    def backward(following, inputs):
        factor, partial_row = inputs
        current = partial_row - factor * following
        return (current, current)
    _, solved = lax.scan(backward, jnp.zeros_like(values[0]), (factors, partial_rows), reverse=True)
    return solved

def to_lines(field):
    return jnp.transpose(field.reshape(N_LON, CLON, MERIDIAN_ROWS), (1, 0, 2))

def from_lines(field):
    return jnp.transpose(field, (1, 0, 2)).reshape(ZONAL_POINTS, MERIDIAN_ROWS)

def reference(thermal_anomaly, saltiness_anomaly, zonal_flow, meridional_flow, submerged_strata_number, sea_indicator, strata_thickness, earlier_sea_elevation, sea_drive_term):
    strata_indices = thermal_anomaly.shape[0]
    real_number_kind = thermal_anomaly.dtype
    wet_surface = sea_indicator.astype(real_number_kind)
    strata_bottoms = (submerged_strata_number * sea_indicator).astype(real_number_kind)[None]
    joined_tracers = jnp.concatenate([thermal_anomaly, saltiness_anomaly, zonal_flow, meridional_flow, strata_bottoms], axis=0)
    sign_rows = jnp.concatenate([jnp.ones(2 * strata_indices, real_number_kind), -jnp.ones(2 * strata_indices, real_number_kind), jnp.ones(1, real_number_kind)])
    wide_rim = extend(joined_tracers, sign_rows, 2)
    mask_wide = level_mask(wide_rim[4 * strata_indices:], strata_indices)
    narrow = shrink(wide_rim)
    mask_narrow = shrink(mask_wide)
    lap_u = laplace(wide_rim[2 * strata_indices:3 * strata_indices], mask_wide)
    lap_v = laplace(wide_rim[3 * strata_indices:4 * strata_indices], mask_wide)
    lat_index = jnp.arange(MERIDIAN_ROWS).astype(real_number_kind)
    coriolis = CORIOLIS * (2.0 * (lat_index + 0.5) / MERIDIAN_ROWS - 1.0)
    new_temp, new_salt, u_star, v_star, height, wet_mid = baroclinic(narrow, mask_narrow, lap_u, lap_v, strata_thickness, coriolis, strata_indices)
    weights = solver_weights(height, strata_indices)
    lower_band, factors, pivots = line_factor(to_lines(weights[1][0]), to_lines(weights[0][0]), to_lines(weights[4][0]))

    def precondition(values):
        return from_lines(line_solve(lower_band, factors, pivots, to_lines(values[0])))[None]
    transport_u = lax.optimization_barrier(jnp.sum(strata_thickness[:, None, None] * u_star, axis=0, keepdims=True))
    transport_v = lax.optimization_barrier(jnp.sum(strata_thickness[:, None, None] * v_star, axis=0, keepdims=True))
    start_field = (wet_surface * earlier_sea_elevation)[None]
    surface_signs = jnp.array([-1.0, -1.0, 1.0], real_number_kind)
    plus_one = jnp.ones(1, real_number_kind)
    moved = extend(jnp.concatenate([transport_u, transport_v, start_field], axis=0), surface_signs, 1)
    divergence = 0.5 * (to_east(moved[0:1]) - to_west(moved[0:1])) + 0.5 * (to_north(moved[1:2]) - to_south(moved[1:2]))
    right_side = wet_surface[None] * (sea_drive_term[None] - DIVERGENCE * divergence)
    solution = center(moved[2:3])
    residual = right_side - apply_operator(weights, moved[2:3])
    spectrum_mid = 0.5 * (SPECTRUM_HIGH + SPECTRUM_LOW)
    spectrum_half = 0.5 * (SPECTRUM_HIGH - SPECTRUM_LOW)
    spectrum_ratio = spectrum_mid / spectrum_half
    direction = precondition(residual) / spectrum_mid
    cheby_rho = 1.0 / spectrum_ratio
    for step_index in range(ITERS):
        solution = solution + direction
        if step_index + 1 < ITERS:
            residual = residual - apply_operator(weights, extend(direction, plus_one, 1))
            rho_next = 1.0 / (2.0 * spectrum_ratio - cheby_rho)
            direction = rho_next * cheby_rho * direction + 2.0 * rho_next / spectrum_half * precondition(residual)
            cheby_rho = rho_next
    final_rim = extend(solution, plus_one, 1)
    final_residual = right_side - apply_operator(weights, final_rim)
    residual_rms = jnp.sqrt(jnp.sum(final_residual * final_residual) / (ZONAL_POINTS * MERIDIAN_ROWS) + EPSILON)
    slope_x = 0.5 * (to_east(final_rim) - to_west(final_rim))
    slope_y = 0.5 * (to_north(final_rim) - to_south(final_rim))
    new_u = wet_mid * (u_star - GRAVITY * slope_x)
    new_v = wet_mid * (v_star - GRAVITY * slope_y)
    return (new_temp, new_salt, new_u, new_v, solution[0], residual_rms)
```

```python
import functools

import jax
import jax.numpy as jnp
from jax import lax
from jax.experimental import pallas as pl
from jax.experimental.pallas import tpu as pltpu
from jax.sharding import PartitionSpec as P

DIFFUSION = 0.15
MIXING = 0.1
EXPANSION = 0.2
CONTRACTION = 0.15
PRESSURE_SCALE = 0.02
CORIOLIS = 0.5
FRICTION = 0.01
DIVERGENCE = 0.3
STORAGE = 0.1
SPECTRUM_LOW = 0.1
SPECTRUM_HIGH = 1.9
GRAVITY = 0.3
EPSILON = 1e-06
ITERS = 4
F32 = jnp.float32

VMEM = pl.BlockSpec(memory_space=pltpu.VMEM)
SMEM = pl.BlockSpec(memory_space=pltpu.SMEM)


def lanes(shape=(8, 128)):
    return lax.broadcasted_iota(jnp.int32, shape, 1)


def subs(shape=(8, 128)):
    return lax.broadcasted_iota(jnp.int32, shape, 0)


def roll_lane(x, shift):
    return pltpu.roll(x, shift % x.shape[1], 1)


def roll_sub(x, shift):
    return pltpu.roll(x, shift % x.shape[0], 0)


def north(x, ghost):
    return roll_lane(jnp.where(lanes() == 0, ghost, x), -1)


def south(x, ghost):
    return roll_lane(jnp.where(lanes() == 127, ghost, x), 1)


def east(x, ghost):
    return roll_sub(jnp.where(subs() == 0, ghost, x), -1)


def west(x, ghost):
    return roll_sub(jnp.where(subs() == 7, ghost, x), 1)


def around(x, lat_ghost, lon_ghost):
    return (east(x, lon_ghost), west(x, lon_ghost), north(x, lat_ghost), south(x, lat_ghost))


def one_of(index, values):
    found = index == values[0]
    for value in values[1:]:
        found = found | (index == value)
    return found


def lat_pack_kernel(t_ref, s_ref, u_ref, v_ref, d_ref, m_ref, z_ref, out_ref):
    levels = t_ref.shape[0]
    lane = lanes()
    is_v = (lane >= 2) & (lane <= 5)
    is_t = (lane == 7) | (lane == 8)
    is_s = (lane == 9) | (lane == 10)
    for k in range(levels):
        x = jnp.where(is_v, roll_lane(v_ref[k], 4), u_ref[k])
        x = jnp.where(is_t, roll_lane(t_ref[k], 8), x)
        out_ref[k] = jnp.where(is_s, roll_lane(s_ref[k], 10), x)
    sea = m_ref[...].astype(F32)
    out_ref[levels] = (d_ref[...] * m_ref[...]).astype(F32)
    out_ref[levels + 1] = sea * z_ref[...]


def lon_pack_kernel(info_ref, t_ref, s_ref, u_ref, v_ref, d_ref, m_ref, z_ref, a_ref, b_ref, g_ref, w_ref, e_ref):
    levels = t_ref.shape[0]
    lane, sub = lanes(), subs()
    is_even, is_top = info_ref[0], info_ref[1]
    from_north = one_of(lane, (0, 1, 4, 5, 8, 10))
    second = one_of(lane, (1, 5))
    flow_sign = jnp.where(lane < 6, -1.0, 1.0).astype(F32)

    @pl.when(is_even == 1)
    def _():
        for k in range(levels + 2):
            g_ref[k] = jnp.where(from_north, a_ref[k], b_ref[k])

    @pl.when((is_even == 0) & (is_top == 0))
    def _():
        for k in range(levels + 2):
            g_ref[k] = jnp.where(from_north, b_ref[k], a_ref[k])

    @pl.when(is_top == 1)
    def _():
        for k in range(levels + 2):
            turned = jnp.concatenate([b_ref[k, 7 - i : 8 - i, :] for i in range(8)], axis=0)
            turned = jnp.where(second, roll_lane(turned, 3), roll_lane(turned, 1))
            if k < levels:
                turned = turned * flow_sign
            g_ref[k] = jnp.where(from_north, turned, a_ref[k])

    for k in range(levels):
        u, v, t, s, g = u_ref[k], v_ref[k], t_ref[k], s_ref[k], g_ref[k]
        v4, t2, s6 = roll_sub(v, 4), roll_sub(t, 2), roll_sub(s, 6)
        x = jnp.where((sub >= 4) & (sub <= 5), v4, u)
        x = jnp.where(sub == 2, t2, x)
        x = jnp.where(sub == 6, s6, x)
        w_ref[k] = jnp.where(sub == 3, roll_sub(g, 3), x)
        x = jnp.where((sub >= 2) & (sub <= 3), v4, u)
        x = jnp.where(sub == 1, t2, x)
        x = jnp.where(sub == 5, s6, x)
        e_ref[k] = jnp.where(sub == 0, roll_sub(g, 1), x)
    depth = (d_ref[...] * m_ref[...]).astype(F32)
    start = m_ref[...].astype(F32) * z_ref[...]
    for k, x in ((levels, depth), (levels + 1, start)):
        w_ref[k] = jnp.where(sub == 3, roll_sub(g_ref[k], 3), x)
        e_ref[k] = jnp.where(sub == 0, roll_sub(g_ref[k], 1), x)


def lon_ghost(e, w, sub):
    return jnp.where(one_of(sub, (0, 1, 4, 5)), e, w)


def corner_ghost(e, w, sub):
    return jnp.where(sub == 0, roll_sub(e, -3), roll_sub(w, -1))


def lap(x, near, masks):
    total = jnp.where(masks[0], near[0] - x, 0.0)
    for i in range(1, 4):
        total = total + jnp.where(masks[i], near[i] - x, 0.0)
    return total


def floats(i):
    return i.astype(F32)


def momentum_kernel(
    info_ref, th_ref, t_ref, s_ref, u_ref, v_ref, d_ref, m_ref, z_ref, f_ref, g_ref, e_ref, w_ref, us_ref, vs_ref, flat_ref, st_ref
):
    levels = t_ref.shape[0]
    lane, sub = lanes(), subs()
    depth = (d_ref[...] * m_ref[...]).astype(F32)
    depth_g = g_ref[levels]
    depth_h = lon_ghost(e_ref[levels], w_ref[levels], sub)
    depth_c = corner_ghost(e_ref[levels], w_ref[levels], sub)
    low_x = [jnp.minimum(depth, n) for n in around(depth, depth_g, depth_h)]
    low_g = [jnp.minimum(depth_g, n) for n in around(depth_g, depth, depth_c)]
    low_h = [jnp.minimum(depth_h, n) for n in around(depth_h, depth_c, depth)]
    lat_index = (lane + info_ref[2] * 128).astype(F32)
    coriolis = CORIOLIS * (2.0 * (lat_index + 0.5) / (128.0 * info_ref[4].astype(F32)) - 1.0)
    zero = jnp.zeros((8, 128), F32)

    def level(k, carry):
        p, p_g, p_h, h, h_g, h_h, tu, tv = carry
        th = th_ref[k]
        kf = floats(k) + 0.5
        u, v, t, s = u_ref[k], v_ref[k], t_ref[k], s_ref[k]
        g, e, w = g_ref[k], e_ref[k], w_ref[k]
        u_h = lon_ghost(e, w, sub)
        v_h = roll_sub(u_h, 4)
        t_h = roll_sub(jnp.where(sub == 2, e, w), -2)
        s_h = roll_sub(jnp.where(sub == 6, e, w), -6)
        u_c = corner_ghost(e, w, sub)
        v_c = roll_lane(u_c, -4)
        v_g, t_g, s_g = roll_lane(g, -4), roll_lane(g, -8), roll_lane(g, -10)
        m_x = [x > kf for x in low_x]
        m_g = [x > kf for x in low_g]
        m_h = [x > kf for x in low_h]
        wet, wet_g, wet_h = depth > kf, depth_g > kf, depth_h > kf
        drags = []
        for x, x_g, x_h, x_c in ((u, g, u_h, u_c), (v, v_g, v_h, v_c)):
            l = lap(x, around(x, x_g, x_h), m_x)
            l_g = lap(x_g, around(x_g, x, x_c), m_g)
            l_h = lap(x_h, around(x_h, x_c, x), m_h)
            drags.append(lap(l, around(l, l_g, l_h), m_x))
        p = p + jnp.where(wet, (CONTRACTION * s - EXPANSION * t) * th, 0.0)
        p_g = p_g + jnp.where(wet_g, (CONTRACTION * s_g - EXPANSION * t_g) * th, 0.0)
        p_h = p_h + jnp.where(wet_h, (CONTRACTION * s_h - EXPANSION * t_h) * th, 0.0)
        p_e, p_w, p_n, p_s = around(p, p_g, p_h)
        grad_x = 0.5 * (jnp.where(m_x[0], p_e - p, 0.0) + jnp.where(m_x[1], p - p_w, 0.0))
        grad_y = 0.5 * (jnp.where(m_x[2], p_n - p, 0.0) + jnp.where(m_x[3], p - p_s, 0.0))
        us = jnp.where(wet, u + coriolis * v - PRESSURE_SCALE * grad_x - FRICTION * drags[0], 0.0)
        vs = jnp.where(wet, v - coriolis * u - PRESSURE_SCALE * grad_y - FRICTION * drags[1], 0.0)
        us_ref[k] = us
        vs_ref[k] = vs
        h = h + jnp.where(wet, th, 0.0)
        h_g = h_g + jnp.where(wet_g, th, 0.0)
        h_h = h_h + jnp.where(wet_h, th, 0.0)
        return (p, p_g, p_h, h, h_g, h_h, tu + th * us, tv + th * vs)

    _, _, _, h, h_g, h_h, tu, tv = lax.fori_loop(0, levels, level, (zero,) * 8)
    sea = m_ref[...].astype(F32)
    start = sea * z_ref[...]
    start_g = g_ref[levels + 1]
    start_h = lon_ghost(e_ref[levels + 1], w_ref[levels + 1], sub)
    diag, coupled = STORAGE + zero, zero
    for n, x in zip(around(h, h_g, h_h), around(start, start_g, start_h)):
        weight = jnp.minimum(h, n) * (1.0 / levels)
        diag = diag + weight
        coupled = coupled + weight * x
    flat_ref[0] = h
    flat_ref[1] = sea * f_ref[...] - (diag * start - coupled)
    flat_ref[2] = tu
    flat_ref[3] = tv
    st_ref[0] = start
    st_ref[1] = start_g
    st_ref[2] = start_h


def tracer_kernel(th_ref, t_ref, s_ref, u_ref, v_ref, d_ref, m_ref, g_ref, e_ref, w_ref, nt_ref, ns_ref):
    levels = t_ref.shape[0]
    lane, sub = lanes(), subs()
    depth = (d_ref[...] * m_ref[...]).astype(F32)
    depth_g = g_ref[levels]
    depth_h = lon_ghost(e_ref[levels], w_ref[levels], sub)
    low = [jnp.minimum(depth, n) for n in around(depth, depth_g, depth_h)]
    zero = jnp.zeros((8, 128), F32)

    def level(k, carry):
        above_t, above_s = carry
        kf = floats(k) + 0.5
        below = jnp.minimum(k + 1, levels - 1)
        th, th_below = th_ref[k], th_ref[below]
        u, v, t, s = u_ref[k], v_ref[k], t_ref[k], s_ref[k]
        g, e, w = g_ref[k], e_ref[k], w_ref[k]
        u_h = lon_ghost(e, w, sub)
        v_g = roll_lane(g, -4)
        wet = depth > kf
        wet_below = (depth > kf + 1.0) & (k + 1 < levels)
        inv_space = 1.0 / jnp.full((8, 128), 0.5 * (th + th_below), F32)
        inv_th = MIXING / jnp.full((8, 128), th, F32)
        flow = [0.25 * x for x in (u + east(u, u_h), west(u, u_h) + u, v + north(v, v_g), south(v, v_g) + v)]
        masks = [x > kf for x in low]
        fluxes = []
        for q, q_g, q_h, q_ref, above, out_ref in (
            (t, roll_lane(g, -8), roll_sub(jnp.where(sub == 2, e, w), -2), t_ref, above_t, nt_ref),
            (s, roll_lane(g, -10), roll_sub(jnp.where(sub == 6, e, w), -6), s_ref, above_s, ns_ref),
        ):
            q_e, q_w, q_n, q_s = around(q, q_g, q_h)
            f_e = jnp.where(masks[0], flow[0] * (q + q_e) - DIFFUSION * (q_e - q), 0.0)
            f_w = jnp.where(masks[1], flow[1] * (q_w + q) - DIFFUSION * (q - q_w), 0.0)
            f_n = jnp.where(masks[2], flow[2] * (q + q_n) - DIFFUSION * (q_n - q), 0.0)
            f_s = jnp.where(masks[3], flow[3] * (q_s + q) - DIFFUSION * (q - q_s), 0.0)
            vflux = jnp.where(wet_below, (q_ref[below] - q) * inv_space, 0.0)
            vertical = (vflux - above) * inv_th
            out_ref[k] = jnp.where(wet, q + (f_w - f_e + f_s - f_n) + vertical, 0.0)
            fluxes.append(vflux)
        return tuple(fluxes)

    lax.fori_loop(0, levels, level, (zero, zero))


def turn(x, cells):
    lane = lanes()
    x = jnp.concatenate([x[7 - i : 8 - i] for i in range(8)], axis=0)
    out = roll_lane(x, 1)
    for j in range(1, cells):
        out = jnp.where(lane == j, roll_lane(x, 1 + 2 * j), out)
    return out


def chunk_kernel(info_ref, flat_ref, a_ref, b_ref, out_ref):
    lane, sub = lanes(), subs()
    even = jnp.full((8, 128), info_ref[0], jnp.int32) == 1
    top = jnp.full((8, 128), info_ref[1], jnp.int32) == 1
    own, ghost = [], []
    for f in range(4):
        a, b = a_ref[f], b_ref[f]
        turned = turn(b, 5)
        if f >= 2:
            turned = -turned
        n = jnp.where(even, a, jnp.where(top, turned, b))
        s = jnp.where(even, b, a)
        own.append(flat_ref[f])
        ghost.append(jnp.where(lane < 64, n, s))
    rights = []
    for x, other in ((own, ghost), (ghost, own)):
        h, base, tu, tv = x
        tu_e = jnp.where(sub == 7, 0.0, roll_sub(tu, -1))
        tu_w = jnp.where(sub == 0, 0.0, roll_sub(tu, 1))
        tv_n, tv_s = north(tv, other[3]), south(tv, other[3])
        rights.append(base - jnp.where(h > 0.0, (0.5 * DIVERGENCE) * ((tu_e - tu_w) + (tv_n - tv_s)), 0.0))
    halo = jnp.where(lane < 16, roll_lane(ghost[0], 8), jnp.where(lane < 32, roll_lane(rights[1], 24), roll_lane(ghost[2], 40)))
    halo = jnp.where(lane < 64, halo, roll_lane(roll_sub(halo, 4), 64))
    halo = jnp.where(sub < 4, halo, jnp.where(sub == 4, roll_sub(own[2], 4), roll_sub(own[2], -2)))
    out_ref[0] = own[0]
    out_ref[1] = rights[0]
    out_ref[2] = halo


def slab_kernel(info_ref, in_ref, st_ref, sum_ref, surf_ref, slope_ref, h_s, we_s, wn_s, ws_s, dg_s, fac_s, inv_s, r_s, d_s, z_s):
    blocks = in_ref.shape[0] // 24
    inv_levels = info_ref[5].astype(F32)
    inv_levels = 1.0 / jnp.full((8, 128), inv_levels, F32)[0:1, 0:1]

    def rows(i):
        return in_ref[pl.ds(i, blocks, stride=24), :]

    tu = [None] * 8
    for p in range(8):
        packed = rows(16 + p % 4)
        at = 64 * (p // 4)
        h_s[p, :, 0:128] = rows(p)
        h_s[p, :, 128:256] = roll_lane(packed, -8 - at)
        r_s[p, :, 0:128] = rows(8 + p)
        r_s[p, :, 128:256] = roll_lane(packed, -24 - at)
        if p in (0, 7):
            tu[p] = jnp.concatenate([rows(20 if p == 0 else 21), roll_lane(packed, -40 - at)], axis=1)
    r_s[0] = r_s[0] + jnp.where(h_s[0] > 0.0, (0.5 * DIVERGENCE) * roll_sub(tu[7], 1), 0.0)
    r_s[7] = r_s[7] - jnp.where(h_s[7] > 0.0, (0.5 * DIVERGENCE) * roll_sub(tu[0], -1), 0.0)
    for p in range(8):
        h = h_s[p]
        h_e = h_s[p + 1] if p < 7 else roll_sub(h_s[0], -1)
        we_s[p] = jnp.minimum(h, h_e) * inv_levels
        wn = jnp.minimum(h, roll_lane(h, -1)) * inv_levels
        wn_s[p] = wn
        ws_s[p] = roll_lane(wn, 1)
    for p in range(8):
        w_w = we_s[p - 1] if p > 0 else roll_sub(we_s[7], 1)
        diag = STORAGE + we_s[p] + w_w + wn_s[p] + ws_s[p]
        dg_s[p] = diag
        if p > 0:
            diag = diag + we_s[p - 1] * fac_s[p - 1]
        inv = 1.0 / diag
        inv_s[p] = inv
        fac_s[p] = -we_s[p] * inv

    mid = 0.5 * (SPECTRUM_HIGH + SPECTRUM_LOW)
    half = 0.5 * (SPECTRUM_HIGH - SPECTRUM_LOW)
    ratio = mid / half

    def solve(scale_old, scale_new, first):
        y = [None] * 8
        y[0] = r_s[0] * inv_s[0]
        for p in range(1, 8):
            y[p] = (r_s[p] + we_s[p - 1] * y[p - 1]) * inv_s[p]
        x = None
        for p in range(7, -1, -1):
            x = y[p] if x is None else y[p] - fac_s[p] * x
            if first:
                d = x * scale_new
                z_s[p] = d
            else:
                d = scale_old * d_s[p] + scale_new * x
                z_s[p] = z_s[p] + d
            d_s[p] = d

    def subtract():
        for p in range(8):
            d = d_s[p]
            d_e = d_s[p + 1] if p < 7 else roll_sub(d_s[0], -1)
            d_w = d_s[p - 1] if p > 0 else roll_sub(d_s[7], 1)
            w_w = we_s[p - 1] if p > 0 else roll_sub(we_s[7], 1)
            coupled = we_s[p] * d_e + w_w * d_w + wn_s[p] * roll_lane(d, -1) + ws_s[p] * roll_lane(d, 1)
            r_s[p] = r_s[p] - (dg_s[p] * d - coupled)

    solve(0.0, 1.0 / mid, True)
    rho = 1.0 / ratio
    for _ in range(ITERS - 1):
        subtract()
        rho_next = 1.0 / (2.0 * ratio - rho)
        solve(rho_next * rho, 2.0 * rho_next / half, False)
        rho = rho_next
    subtract()
    total = jnp.zeros((blocks, 128), F32)
    for p in range(8):
        x = r_s[p, :, 0:128]
        total = total + x * x
    sum_ref[...] = jnp.sum(jnp.sum(total, axis=0, keepdims=True), axis=1, keepdims=True) + jnp.zeros((1, 128), F32)

    here = info_ref[3]
    right = jnp.where(here + 1 == blocks, 0, here + 1)
    left = jnp.where(here == 0, blocks - 1, here - 1)
    both = jnp.concatenate([z_s[p, pl.ds(here, 1), :] for p in range(8)], axis=0)
    x, x_g = both[:, 0:128], both[:, 128:256]
    sub = subs()
    x_e = jnp.broadcast_to(z_s[0, pl.ds(right, 1), :][:, 0:128], (8, 128))
    x_w = jnp.broadcast_to(z_s[7, pl.ds(left, 1), :][:, 0:128], (8, 128))
    x_h = jnp.where(sub < 4, x_e, x_w)
    x, x_g, x_h = x + st_ref[0], x_g + st_ref[1], x_h + st_ref[2]
    e, w, n, s = around(x, x_g, x_h)
    surf_ref[...] = x
    slope_ref[0] = (0.5 * GRAVITY) * (e - w)
    slope_ref[1] = (0.5 * GRAVITY) * (n - s)


def velocity_kernel(us_ref, vs_ref, d_ref, m_ref, slope_ref, nu_ref, nv_ref):
    depth = (d_ref[...] * m_ref[...]).astype(F32)
    slope_x, slope_y = slope_ref[0], slope_ref[1]
    for k in range(us_ref.shape[0]):
        wet = depth > k + 0.5
        nu_ref[k] = jnp.where(wet, us_ref[k] - slope_x, 0.0)
        nv_ref[k] = jnp.where(wet, vs_ref[k] - slope_y, 0.0)


def call(kernel, name, outs, in_specs, scratch=()):
    return pl.pallas_call(
        kernel,
        name=name,
        out_shape=outs,
        in_specs=in_specs,
        out_specs=jax.tree.map(lambda _: VMEM, outs),
        scratch_shapes=list(scratch),
        compiler_params=pltpu.CompilerParams(vmem_limit_bytes=48 << 20),
    )


def per_device(lon_size, lat_size, temp, salt, u, v, strata, sea, thickness, elevation, drive):
    levels = temp.shape[0]
    lon, lat = lax.axis_index("lon"), lax.axis_index("lat")
    top = lat_size - 1
    info = jnp.stack(
        [1 - lat % 2, (lat == top).astype(jnp.int32), lat, lon, jnp.int32(lat_size), jnp.int32(levels)]
    ).astype(jnp.int32)
    pairs_a = [(i, i ^ 1) for i in range(lat_size)]
    pairs_b = []
    for a in range(lon_size):
        for i in range(1, top, 2):
            pairs_b += [(a * lat_size + i, a * lat_size + i + 1), (a * lat_size + i + 1, a * lat_size + i)]
        pairs_b.append((a * lat_size + top, (lon_size - 1 - a) * lat_size + top))
    up = [(i, (i + 1) % lon_size) for i in range(lon_size)]
    down = [(j, i) for i, j in up]

    def lat_swap(x):
        return lax.ppermute(x, "lat", pairs_a), lax.ppermute(x, ("lon", "lat"), pairs_b)

    field = jax.ShapeDtypeStruct((levels, 8, 128), F32)
    message = jax.ShapeDtypeStruct((levels + 2, 8, 128), F32)

    def tiles(n):
        return jax.ShapeDtypeStruct((n, 8, 128), F32)

    packed = call(lat_pack_kernel, "lat_pack", message, [VMEM] * 7)(temp, salt, u, v, strata, sea, elevation)
    got_a, got_b = lat_swap(packed)
    ghost, westward, eastward = call(lon_pack_kernel, "lon_pack", (message,) * 3, [SMEM] + [VMEM] * 9)(
        info, temp, salt, u, v, strata, sea, elevation, got_a, got_b
    )
    from_east = lax.ppermute(westward, "lon", down)
    from_west = lax.ppermute(eastward, "lon", up)
    u_star, v_star, flat, start = call(
        momentum_kernel, "momentum", (field, field, tiles(4), tiles(3)), [SMEM, SMEM] + [VMEM] * 11
    )(info, thickness, temp, salt, u, v, strata, sea, elevation, drive, ghost, from_east, from_west)
    flat_a, flat_b = lat_swap(flat)
    chunk = call(chunk_kernel, "chunk", tiles(3), [SMEM] + [VMEM] * 3)(info, flat, flat_a, flat_b)
    copies = jnp.broadcast_to(chunk[None], (lon_size, 3, 8, 128))
    ring = lax.all_to_all(copies, "lon", 0, 0, tiled=True).reshape(lon_size * 24, 128)
    new_temp, new_salt = call(tracer_kernel, "tracers", (field, field), [SMEM] + [VMEM] * 9)(
        thickness, temp, salt, u, v, strata, sea, ghost, from_east, from_west
    )
    total, surface, slope = call(
        slab_kernel,
        "slab",
        (jax.ShapeDtypeStruct((1, 128), F32), jax.ShapeDtypeStruct((8, 128), F32), tiles(2)),
        [SMEM, VMEM, VMEM],
        [pltpu.VMEM((8, lon_size, 256), F32)] * 10,
    )(info, ring, start)
    total = total + lax.ppermute(total, "lat", pairs_a)
    gap = 2
    while gap < lat_size:
        total = total + lax.ppermute(total, "lat", [(i, i ^ gap) for i in range(lat_size)])
        gap *= 2
    cells = lon_size * 8 * lat_size * 128
    rms = jnp.sqrt(total[0, 0] / cells + EPSILON)
    new_u, new_v = call(velocity_kernel, "velocity", (field, field), [VMEM] * 5)(u_star, v_star, strata, sea, slope)
    return (new_temp, new_salt, new_u, new_v, surface, rms)


def solution(mesh):
    cube, flat = P(None, "lon", "lat"), P("lon", "lat")
    return jax.shard_map(
        functools.partial(per_device, mesh.shape["lon"], mesh.shape["lat"]),
        mesh=mesh,
        in_specs=(cube, cube, cube, cube, flat, flat, P(), flat, flat),
        out_specs=(cube, cube, cube, cube, flat, P()),
        check_vma=False,
    )
```

```python
import functools

import jax
import jax.numpy as jnp
from jax import lax
from jax.experimental import pallas as pl
from jax.experimental.pallas import tpu as pltpu
from jax.sharding import PartitionSpec as P

DIFFUSION = 0.15
MIXING = 0.1
EXPANSION = 0.2
CONTRACTION = 0.15
PRESSURE_SCALE = 0.02
CORIOLIS = 0.5
FRICTION = 0.01
DIVERGENCE = 0.3
STORAGE = 0.1
SPECTRUM_LOW = 0.1
SPECTRUM_HIGH = 1.9
GRAVITY = 0.3
EPSILON = 1e-06
ITERS = 4
TILES_PER_STEP = 2
F32 = jnp.float32

VMEM = pl.BlockSpec(memory_space=pltpu.VMEM)
SMEM = pl.BlockSpec(memory_space=pltpu.SMEM)


def lanes(shape=(8, 128)):
    return lax.broadcasted_iota(jnp.int32, shape, 1)


def subs(shape=(8, 128)):
    return lax.broadcasted_iota(jnp.int32, shape, 0)


def roll_lane(x, shift):
    return pltpu.roll(x, shift % x.shape[1], 1)


def roll_sub(x, shift):
    return pltpu.roll(x, shift % x.shape[0], 0)


def north(x, ghost):
    return roll_lane(jnp.where(lanes() == 0, ghost, x), -1)


def south(x, ghost):
    return roll_lane(jnp.where(lanes() == 127, ghost, x), 1)


def east(x, ghost):
    return roll_sub(jnp.where(subs() == 0, ghost, x), -1)


def west(x, ghost):
    return roll_sub(jnp.where(subs() == 7, ghost, x), 1)


def around(x, lat_ghost, lon_ghost):
    return (east(x, lon_ghost), west(x, lon_ghost), north(x, lat_ghost), south(x, lat_ghost))


def one_of(index, values):
    found = index == values[0]
    for value in values[1:]:
        found = found | (index == value)
    return found


def lat_field(x, f, odd):
    return roll_lane(x, 16 * f + 8 + 64 * odd)


def from_lat_group(x, f, odd):
    return roll_lane(x, -(16 * f + 8 + 64 * odd))


def group_of(lane):
    return lane // 16


def lat_pack_kernel(t_hbm, s_hbm, u_hbm, v_hbm, d_hbm, m_hbm, z_hbm, f_hbm, out_ref, t_ref, s_ref, u_ref, v_ref, d_ref, m_ref, z_ref, f_ref, sem):
    levels = t_ref.shape[0]
    pairs = (
        (t_hbm, t_ref), (s_hbm, s_ref), (u_hbm, u_ref), (v_hbm, v_ref), (d_hbm, d_ref), (m_hbm, m_ref), (z_hbm, z_ref), (f_hbm, f_ref),
    )
    copies = [pltpu.make_async_copy(src, dst, sem.at[i]) for i, (src, dst) in enumerate(pairs)]
    for copy in copies:
        copy.start()
    for copy in copies:
        copy.wait()
    group = group_of(lanes())

    def put(out, fields, odd):
        for f, x in enumerate(fields):
            out = jnp.where(group == f + 4 * odd, lat_field(x, f, odd), out)
        return out

    zero = jnp.zeros((8, 128), F32)
    for j in range(levels // 2):
        out = zero
        for odd in range(2):
            k = 2 * j + odd
            out = put(out, (u_ref[k], v_ref[k], t_ref[k], s_ref[k]), odd)
        out_ref[j] = out
    sea = m_ref[...].astype(F32)
    depth = (d_ref[...] * m_ref[...]).astype(F32)
    out_ref[levels // 2] = put(zero, (depth, sea * z_ref[...], sea * f_ref[...]), 0)


def lon_pack_kernel(info_ref, t_ref, s_ref, u_ref, v_ref, d_ref, m_ref, z_ref, f_ref, a_ref, b_ref, g_ref, q_ref, r_ref):
    levels = t_ref.shape[0]
    count = levels // 2 + 1
    lane, sub = lanes(), subs()
    is_even, is_top = info_ref[0], info_ref[1]
    from_north = lane % 16 >= 8
    flow_sign = jnp.where(group_of(lane) % 4 < 2, -1.0, 1.0).astype(F32)
    odd_lon = jnp.full((8, 128), info_ref[3] % 2, jnp.int32) == 1

    @pl.when(is_even == 1)
    def _():
        for j in range(count):
            g_ref[j] = jnp.where(from_north, a_ref[j], b_ref[j])

    @pl.when((is_even == 0) & (is_top == 0))
    def _():
        for j in range(count):
            g_ref[j] = jnp.where(from_north, b_ref[j], a_ref[j])

    @pl.when(is_top == 1)
    def _():
        for j in range(count):
            rows = jnp.concatenate([b_ref[j, 7 - i : 8 - i, :] for i in range(8)], axis=0)
            turned = roll_lane(rows, 1)
            for i in range(1, 7):
                turned = jnp.where(lane % 16 == 8 + i, roll_lane(rows, 1 + 2 * i), turned)
            if j < levels // 2:
                turned = turned * flow_sign
            g_ref[j] = jnp.where(from_north, turned, a_ref[j])

    def put(k, u, v, t, s):
        g = g_ref[k // 2]
        odd = k % 2
        v4, t2, s6 = roll_sub(v, 4), roll_sub(t, 2), roll_sub(s, 6)
        x = jnp.where((sub >= 4) & (sub <= 5), v4, u)
        x = jnp.where(sub == 2, t2, x)
        x = jnp.where(sub == 6, s6, x)
        to_west = jnp.where(sub == 3, roll_sub(g, 3 - odd), x)
        x = jnp.where((sub >= 2) & (sub <= 3), v4, u)
        x = jnp.where(sub == 1, t2, x)
        x = jnp.where(sub == 5, s6, x)
        to_east = jnp.where(sub == 0, roll_sub(g, 1 + odd), x)
        q_ref[k] = jnp.where(odd_lon, to_west, to_east)
        r_ref[k] = jnp.where(odd_lon, to_east, to_west)

    for k in range(levels):
        put(k, u_ref[k], v_ref[k], t_ref[k], s_ref[k])
    sea = m_ref[...].astype(F32)
    depth, start = (d_ref[...] * m_ref[...]).astype(F32), sea * z_ref[...]
    put(levels, depth, start, sea * f_ref[...], start)
    put(levels + 1, depth, start, start, start)


def lon_masks(info_ref):
    sub = subs()
    odd_lon = jnp.full((8, 128), info_ref[3] % 2, jnp.int32) == 1
    return [x != odd_lon for x in (one_of(sub, (0, 1, 4, 5)), sub == 2, sub == 6, sub == 3)]


def lon_ghost(q, r, masks):
    return jnp.where(masks[0], q, r)


def lon_tracers(q, r, masks):
    return roll_sub(jnp.where(masks[1], q, r), -2), roll_sub(jnp.where(masks[2], q, r), -6)


def corner_group(q_ref, r_ref, j, masks):
    sub = subs()
    x = jnp.where(masks[3], q_ref[2 * j], r_ref[2 * j])
    y = jnp.where(masks[3], q_ref[2 * j + 1], r_ref[2 * j + 1])
    return jnp.where(sub == 0, roll_sub(x, -3), jnp.where(sub == 7, roll_sub(x, -1), roll_sub(y, -2)))


LAT_PARTNER = (1, 0, 3, 2)
LON_PARTNER = (2, 3, 0, 1)


def ext_east(x):
    return [east(x[i], x[LON_PARTNER[i]]) for i in range(len(x))]


def ext_north(x):
    return [north(x[i], x[LAT_PARTNER[i]]) for i in range(len(x))]


def lap(x, mask_e, mask_n, tiles):
    f_e = [jnp.where(m, y - c, 0.0) for m, y, c in zip(mask_e, ext_east(x), x)]
    f_n = [jnp.where(m, y - c, 0.0) for m, y, c in zip(mask_n, ext_north(x), x)]
    out = []
    for i in tiles:
        out.append(f_e[i] - west(f_e[i], f_e[LON_PARTNER[i]]) + (f_n[i] - south(f_n[i], f_n[LAT_PARTNER[i]])))
    return out


def floats(i):
    return i.astype(F32)


def momentum_kernel(
    info_ref, th_ref, t_ref, s_ref, u_ref, v_ref, d_ref, m_ref, z_ref, f_ref, g_ref, q_ref, r_ref, us_ref, vs_ref, chunk_ref, st_ref
):
    levels = t_ref.shape[0]
    lane, sub = lanes(), subs()
    edges = lon_masks(info_ref)
    last = levels // 2
    sea = m_ref[...].astype(F32)
    corner = corner_group(q_ref, r_ref, last, edges)
    edge = lon_ghost(q_ref[levels], r_ref[levels], edges)
    depth = [(d_ref[...] * m_ref[...]).astype(F32), from_lat_group(g_ref[last], 0, 0), edge, from_lat_group(corner, 0, 0)]
    low_e = [jnp.minimum(x, y) for x, y in zip(depth, ext_east(depth))]
    low_n = [jnp.minimum(x, y) for x, y in zip(depth, ext_north(depth))]
    lat_index = (lane + info_ref[2] * 128).astype(F32)
    ghost_index = lat_index + jnp.where(lane < 64, 128.0, -128.0)
    lats = 128.0 * info_ref[4].astype(F32)
    ghost_index = jnp.where(ghost_index >= lats, 2.0 * lats - 1.0 - ghost_index, ghost_index)
    coriolis = [CORIOLIS * (2.0 * (x + 0.5) / lats - 1.0) for x in (lat_index, ghost_index)]
    zero = jnp.zeros((8, 128), F32)
    both = (0, 1)

    def level(k, odd, j, corners, carry):
        p, h, tu, tv = carry
        th = th_ref[k]
        kf = floats(k) + 0.5
        g, q_in, r_in = g_ref[j], q_ref[k], r_ref[k]
        u_h = lon_ghost(q_in, r_in, edges)
        t_h, s_h = lon_tracers(q_in, r_in, edges)
        u = [u_ref[k], from_lat_group(g, 0, odd), u_h, from_lat_group(corners, 0, odd)]
        v = [v_ref[k], from_lat_group(g, 1, odd), roll_sub(u_h, 4), from_lat_group(corners, 1, odd)]
        t = [t_ref[k], from_lat_group(g, 2, odd), t_h, from_lat_group(corners, 2, odd)]
        s = [s_ref[k], from_lat_group(g, 3, odd), s_h, from_lat_group(corners, 3, odd)]
        mask_e, mask_n, wet = [[x > kf for x in xs] for xs in (low_e, low_n, depth)]
        drag_u = lap(lap(u, mask_e, mask_n, range(4)), mask_e, mask_n, both)
        drag_v = lap(lap(v, mask_e, mask_n, range(4)), mask_e, mask_n, both)
        p = [c + jnp.where(m, (CONTRACTION * b - EXPANSION * a) * th, 0.0) for c, m, a, b in zip(p, wet, t, s)]
        h = [c + jnp.where(m, th, 0.0) for c, m in zip(h, wet)]
        f_e = [jnp.where(m, y - c, 0.0) for m, y, c in zip(mask_e, ext_east(p), p)]
        f_n = [jnp.where(m, y - c, 0.0) for m, y, c in zip(mask_n, ext_north(p), p)]
        us, vs = [], []
        for i in both:
            grad_x = f_e[i] + west(f_e[i], f_e[LON_PARTNER[i]])
            grad_y = f_n[i] + south(f_n[i], f_n[LAT_PARTNER[i]])
            x = u[i] + coriolis[i] * v[i] - (0.5 * PRESSURE_SCALE) * grad_x - FRICTION * drag_u[i]
            y = v[i] - coriolis[i] * u[i] - (0.5 * PRESSURE_SCALE) * grad_y - FRICTION * drag_v[i]
            us.append(jnp.where(wet[i], x, 0.0))
            vs.append(jnp.where(wet[i], y, 0.0))
        us_ref[k] = us[0]
        vs_ref[k] = vs[0]
        return (p, h, [a + th * b for a, b in zip(tu, us)], [a + th * b for a, b in zip(tv, vs)])

    def step(i, carry):
        for j in range(TILES_PER_STEP):
            at = i * TILES_PER_STEP + j
            corners = corner_group(q_ref, r_ref, at, edges)
            for odd in range(2):
                carry = level(2 * at + odd, odd, at, corners, carry)
        return carry

    _, h, tu, tv = lax.fori_loop(0, last // TILES_PER_STEP, step, ([zero] * 4, [zero] * 4, [zero] * 2, [zero] * 2))
    start = [sea * z_ref[...], from_lat_group(g_ref[last], 1, 0), roll_sub(edge, 4), from_lat_group(corner, 1, 0)]
    drive = [sea * f_ref[...], from_lat_group(g_ref[last], 2, 0)]
    weight_e = [jnp.minimum(x, y) * (1.0 / levels) for x, y in zip(h, ext_east(h))]
    weight_n = [jnp.minimum(x, y) * (1.0 / levels) for x, y in zip(h, ext_north(h))]
    flux_e = [x * (y - c) for x, y, c in zip(weight_e, ext_east(start), start)]
    flux_n = [x * (y - c) for x, y, c in zip(weight_n, ext_north(start), start)]
    rights = []
    for i in both:
        spread = flux_e[i] - west(flux_e[i], flux_e[LON_PARTNER[i]]) + (flux_n[i] - south(flux_n[i], flux_n[LAT_PARTNER[i]]))
        base = drive[i] - (STORAGE * start[i] - spread)
        tu_e = jnp.where(sub == 7, 0.0, roll_sub(tu[i], -1))
        tu_w = jnp.where(sub == 0, 0.0, roll_sub(tu[i], 1))
        tv_n, tv_s = north(tv[i], tv[1 - i]), south(tv[i], tv[1 - i])
        rights.append(base - jnp.where(h[i] > 0.0, (0.5 * DIVERGENCE) * ((tu_e - tu_w) + (tv_n - tv_s)), 0.0))
    halo = jnp.where(lane < 16, roll_lane(h[1], 8), jnp.where(lane < 32, roll_lane(rights[1], 24), roll_lane(tu[1], 40)))
    halo = jnp.where(lane < 64, halo, roll_lane(roll_sub(halo, 4), 64))
    halo = jnp.where(sub < 4, halo, jnp.where(sub == 4, roll_sub(tu[0], 4), roll_sub(tu[0], -2)))
    chunk_ref[0] = h[0]
    chunk_ref[1] = rights[0]
    chunk_ref[2] = halo
    for i in range(3):
        st_ref[i] = start[i]


def tracer_kernel(info_ref, th_ref, t_ref, s_ref, u_ref, v_ref, d_ref, m_ref, g_ref, q_ref, r_ref, after_ref, nt_ref, ns_ref):
    del after_ref
    levels = t_ref.shape[0]
    edges = lon_masks(info_ref)
    depth = (d_ref[...] * m_ref[...]).astype(F32)
    depth_g = from_lat_group(g_ref[levels // 2], 0, 0)
    depth_h = lon_ghost(q_ref[levels], r_ref[levels], edges)
    low = [jnp.minimum(depth, n) for n in around(depth, depth_g, depth_h)]
    zero = jnp.zeros((8, 128), F32)

    def level(k, odd, j, carry):
        above_t, above_s = carry
        kf = floats(k) + 0.5
        below = jnp.minimum(k + 1, levels - 1)
        th, th_below = th_ref[k], th_ref[below]
        u, v, t, s = u_ref[k], v_ref[k], t_ref[k], s_ref[k]
        g, q_in, r_in = g_ref[j], q_ref[k], r_ref[k]
        u_h = lon_ghost(q_in, r_in, edges)
        t_h, s_h = lon_tracers(q_in, r_in, edges)
        v_g = from_lat_group(g, 1, odd)
        wet = depth > kf
        wet_below = (depth > kf + 1.0) & (k + 1 < levels)
        inv_space = 1.0 / jnp.full((8, 128), 0.5 * (th + th_below), F32)
        inv_th = MIXING / jnp.full((8, 128), th, F32)
        flow = [0.25 * x for x in (u + east(u, u_h), west(u, u_h) + u, v + north(v, v_g), south(v, v_g) + v)]
        masks = [x > kf for x in low]
        fluxes = []
        for q, q_g, q_h, full_ref, above, out_ref in (
            (t, from_lat_group(g, 2, odd), t_h, t_ref, above_t, nt_ref),
            (s, from_lat_group(g, 3, odd), s_h, s_ref, above_s, ns_ref),
        ):
            q_e, q_w, q_n, q_s = around(q, q_g, q_h)
            f_e = jnp.where(masks[0], flow[0] * (q + q_e) - DIFFUSION * (q_e - q), 0.0)
            f_w = jnp.where(masks[1], flow[1] * (q_w + q) - DIFFUSION * (q - q_w), 0.0)
            f_n = jnp.where(masks[2], flow[2] * (q + q_n) - DIFFUSION * (q_n - q), 0.0)
            f_s = jnp.where(masks[3], flow[3] * (q_s + q) - DIFFUSION * (q - q_s), 0.0)
            vflux = jnp.where(wet_below, (full_ref[below] - q) * inv_space, 0.0)
            vertical = (vflux - above) * inv_th
            out_ref[k] = jnp.where(wet, q + (f_w - f_e + f_s - f_n) + vertical, 0.0)
            fluxes.append(vflux)
        return tuple(fluxes)

    def step(i, carry):
        for j in range(TILES_PER_STEP):
            at = i * TILES_PER_STEP + j
            for odd in range(2):
                carry = level(2 * at + odd, odd, at, carry)
        return carry

    lax.fori_loop(0, levels // 2 // TILES_PER_STEP, step, (zero, zero))


def slab_kernel(info_ref, in_ref, st_ref, sum_ref, surf_ref, slope_ref, h_s, we_s, wn_s, ws_s, dg_s, fac_s, inv_s, r_s, d_s, z_s):
    blocks = in_ref.shape[0] // 24
    inv_levels = info_ref[5].astype(F32)
    inv_levels = 1.0 / jnp.full((8, 128), inv_levels, F32)[0:1, 0:1]

    def rows(i):
        return in_ref[pl.ds(i, blocks, stride=24), :]

    tu = [None] * 8
    for p in range(8):
        packed = rows(16 + p % 4)
        at = 64 * (p // 4)
        h_s[p, :, 0:128] = rows(p)
        h_s[p, :, 128:256] = roll_lane(packed, -8 - at)
        r_s[p, :, 0:128] = rows(8 + p)
        r_s[p, :, 128:256] = roll_lane(packed, -24 - at)
        if p in (0, 7):
            tu[p] = jnp.concatenate([rows(20 if p == 0 else 21), roll_lane(packed, -40 - at)], axis=1)
    r_s[0] = r_s[0] + jnp.where(h_s[0] > 0.0, (0.5 * DIVERGENCE) * roll_sub(tu[7], 1), 0.0)
    r_s[7] = r_s[7] - jnp.where(h_s[7] > 0.0, (0.5 * DIVERGENCE) * roll_sub(tu[0], -1), 0.0)
    for p in range(8):
        h = h_s[p]
        h_e = h_s[p + 1] if p < 7 else roll_sub(h_s[0], -1)
        we_s[p] = jnp.minimum(h, h_e) * inv_levels
        wn = jnp.minimum(h, roll_lane(h, -1)) * inv_levels
        wn_s[p] = wn
        ws_s[p] = roll_lane(wn, 1)
    for p in range(8):
        w_w = we_s[p - 1] if p > 0 else roll_sub(we_s[7], 1)
        diag = STORAGE + we_s[p] + w_w + wn_s[p] + ws_s[p]
        dg_s[p] = diag
        if p > 0:
            diag = diag + we_s[p - 1] * fac_s[p - 1]
        inv = 1.0 / diag
        inv_s[p] = inv
        fac_s[p] = -we_s[p] * inv

    mid = 0.5 * (SPECTRUM_HIGH + SPECTRUM_LOW)
    half = 0.5 * (SPECTRUM_HIGH - SPECTRUM_LOW)
    ratio = mid / half

    def solve(scale_old, scale_new, first):
        y = [None] * 8
        y[0] = r_s[0] * inv_s[0]
        for p in range(1, 8):
            y[p] = (r_s[p] + we_s[p - 1] * y[p - 1]) * inv_s[p]
        x = None
        for p in range(7, -1, -1):
            x = y[p] if x is None else y[p] - fac_s[p] * x
            if first:
                d = x * scale_new
                z_s[p] = d
            else:
                d = scale_old * d_s[p] + scale_new * x
                z_s[p] = z_s[p] + d
            d_s[p] = d

    def subtract():
        for p in range(8):
            d = d_s[p]
            d_e = d_s[p + 1] if p < 7 else roll_sub(d_s[0], -1)
            d_w = d_s[p - 1] if p > 0 else roll_sub(d_s[7], 1)
            w_w = we_s[p - 1] if p > 0 else roll_sub(we_s[7], 1)
            coupled = we_s[p] * d_e + w_w * d_w + wn_s[p] * roll_lane(d, -1) + ws_s[p] * roll_lane(d, 1)
            r_s[p] = r_s[p] - (dg_s[p] * d - coupled)

    solve(0.0, 1.0 / mid, True)
    rho = 1.0 / ratio
    for _ in range(ITERS - 1):
        subtract()
        rho_next = 1.0 / (2.0 * ratio - rho)
        solve(rho_next * rho, 2.0 * rho_next / half, False)
        rho = rho_next
    subtract()
    total = jnp.zeros((blocks, 128), F32)
    for p in range(8):
        x = r_s[p, :, 0:128]
        total = total + x * x
    sum_ref[...] = jnp.sum(jnp.sum(total, axis=0, keepdims=True), axis=1, keepdims=True) + jnp.zeros((1, 128), F32)

    here = info_ref[3]
    right = jnp.where(here + 1 == blocks, 0, here + 1)
    left = jnp.where(here == 0, blocks - 1, here - 1)
    both = jnp.concatenate([z_s[p, pl.ds(here, 1), :] for p in range(8)], axis=0)
    x, x_g = both[:, 0:128], both[:, 128:256]
    sub = subs()
    x_e = jnp.broadcast_to(z_s[0, pl.ds(right, 1), :][:, 0:128], (8, 128))
    x_w = jnp.broadcast_to(z_s[7, pl.ds(left, 1), :][:, 0:128], (8, 128))
    x_h = jnp.where(sub < 4, x_e, x_w)
    x, x_g, x_h = x + st_ref[0], x_g + st_ref[1], x_h + st_ref[2]
    e, w, n, s = around(x, x_g, x_h)
    surf_ref[...] = x
    slope_ref[0] = (0.5 * GRAVITY) * (e - w)
    slope_ref[1] = (0.5 * GRAVITY) * (n - s)


def velocity_kernel(us_ref, vs_ref, d_ref, m_ref, slope_ref, nu_ref, nv_ref):
    depth = (d_ref[...] * m_ref[...]).astype(F32)
    slope_x, slope_y = slope_ref[0], slope_ref[1]
    for k in range(us_ref.shape[0]):
        wet = depth > k + 0.5
        nu_ref[k] = jnp.where(wet, us_ref[k] - slope_x, 0.0)
        nv_ref[k] = jnp.where(wet, vs_ref[k] - slope_y, 0.0)


def call(kernel, name, outs, in_specs, scratch=()):
    return pl.pallas_call(
        kernel,
        name=name,
        out_shape=outs,
        in_specs=in_specs,
        out_specs=jax.tree.map(lambda _: VMEM, outs),
        scratch_shapes=list(scratch),
        compiler_params=pltpu.CompilerParams(vmem_limit_bytes=48 << 20),
    )


def everywhere(tiles, size):
    copies = jnp.broadcast_to(tiles[None], (size, *tiles.shape))
    return lax.all_to_all(copies, "lon", 0, 0, tiled=True).reshape(-1, 128)


def per_device(lon_size, lat_size, temp, salt, u, v, strata, sea, thickness, elevation, drive):
    levels = temp.shape[0]
    lon, lat = lax.axis_index("lon"), lax.axis_index("lat")
    top = lat_size - 1
    info = jnp.stack(
        [1 - lat % 2, (lat == top).astype(jnp.int32), lat, lon, jnp.int32(lat_size), jnp.int32(levels)]
    ).astype(jnp.int32)
    pairs_a = [(i, i ^ 1) for i in range(lat_size)]
    pairs_b = []
    for a in range(lon_size):
        for i in range(1, top, 2):
            pairs_b += [(a * lat_size + i, a * lat_size + i + 1), (a * lat_size + i + 1, a * lat_size + i)]
        pairs_b.append((a * lat_size + top, (lon_size - 1 - a) * lat_size + top))

    def lat_swap(x):
        return lax.ppermute(x, "lat", pairs_a), lax.ppermute(x, ("lon", "lat"), pairs_b)

    def tiles(n, kind=F32):
        return jax.ShapeDtypeStruct((n, 8, 128), kind)

    field, flat = tiles(levels), (8, 128)
    message, packed = tiles(levels + 2), tiles(levels // 2 + 1)
    own = (temp, salt, u, v, strata, sea, elevation, drive)

    edges = call(
        lat_pack_kernel,
        "lat_pack",
        packed,
        [pl.BlockSpec(memory_space=pltpu.HBM)] * 8,
        [pltpu.VMEM(field.shape, F32)] * 4
        + [pltpu.VMEM(flat, jnp.int32)] * 2
        + [pltpu.VMEM(flat, F32)] * 2
        + [pltpu.SemaphoreType.DMA((8,))],
    )(*[pltpu.with_memory_space_constraint(x, pltpu.HBM) for x in own])
    got_a, got_b = lat_swap(edges)
    ghost, pair_q, pair_r = call(lon_pack_kernel, "lon_pack", (packed, message, message), [SMEM] + [VMEM] * 10)(
        info, *own, got_a, got_b
    )
    pair_q = lax.ppermute(pair_q, "lon", [(i, i ^ 1) for i in range(lon_size)])
    pair_r = lax.ppermute(pair_r, "lon", [(i, (i + 1 if i % 2 else i - 1) % lon_size) for i in range(lon_size)])
    u_star, v_star, chunk, start = call(
        momentum_kernel, "momentum", (field, field, tiles(3), tiles(3)), [SMEM, SMEM] + [VMEM] * 11
    )(info, thickness, *own, ghost, pair_q, pair_r)
    ring = everywhere(chunk, lon_size)
    new_temp, new_salt = call(tracer_kernel, "tracers", (field, field), [SMEM] * 2 + [VMEM] * 10)(
        info, thickness, temp, salt, u, v, strata, sea, ghost, pair_q, pair_r, chunk
    )
    ring, new_temp, new_salt = lax.optimization_barrier((ring, new_temp, new_salt))
    total, surface, slope = call(
        slab_kernel,
        "slab",
        (jax.ShapeDtypeStruct((1, 128), F32), jax.ShapeDtypeStruct((8, 128), F32), tiles(2)),
        [SMEM, VMEM, VMEM],
        [pltpu.VMEM((8, lon_size, 256), F32)] * 10,
    )(info, ring, start)
    total = total + lax.ppermute(total, "lat", pairs_a)
    gap = 2
    while gap < lat_size:
        total = total + lax.ppermute(total, "lat", [(i, i ^ gap) for i in range(lat_size)])
        gap *= 2
    cells = lon_size * 8 * lat_size * 128
    rms = jnp.sqrt(total[0, 0] / cells + EPSILON)
    new_u, new_v = call(velocity_kernel, "velocity", (field, field), [VMEM] * 5)(u_star, v_star, strata, sea, slope)
    return (new_temp, new_salt, new_u, new_v, surface, rms)


def solution(mesh):
    cube, flat = P(None, "lon", "lat"), P("lon", "lat")
    return jax.shard_map(
        functools.partial(per_device, mesh.shape["lon"], mesh.shape["lat"]),
        mesh=mesh,
        in_specs=(cube, cube, cube, cube, flat, flat, P(), flat, flat),
        out_specs=(cube, cube, cube, cube, flat, P()),
        check_vma=False,
    )
```

```python
import functools

import jax
import jax.numpy as jnp
from jax import lax
from jax.experimental import pallas as pl
from jax.experimental.pallas import tpu as pltpu
from jax.sharding import Mesh
from jax.sharding import PartitionSpec as P

DIFFUSION = 0.15
MIXING = 0.1
EXPANSION = 0.2
CONTRACTION = 0.15
PRESSURE_SCALE = 0.02
CORIOLIS = 0.5
FRICTION = 0.01
DIVERGENCE = 0.3
STORAGE = 0.1
SPECTRUM_LOW = 0.1
SPECTRUM_HIGH = 1.9
GRAVITY = 0.3
EPSILON = 1e-06
ITERS = 4
TILES_PER_STEP = 2
GROUP = 8
LON = ("lon_hi", "lon_lo")
F32 = jnp.float32

VMEM = pl.BlockSpec(memory_space=pltpu.VMEM)
SMEM = pl.BlockSpec(memory_space=pltpu.SMEM)


def lanes(shape=(8, 128)):
    return lax.broadcasted_iota(jnp.int32, shape, 1)


def subs(shape=(8, 128)):
    return lax.broadcasted_iota(jnp.int32, shape, 0)


def roll_lane(x, shift):
    return pltpu.roll(x, shift % x.shape[1], 1)


def roll_sub(x, shift):
    return pltpu.roll(x, shift % x.shape[0], 0)


def north(x, ghost):
    return roll_lane(jnp.where(lanes() == 0, ghost, x), -1)


def south(x, ghost):
    return roll_lane(jnp.where(lanes() == 127, ghost, x), 1)


def east(x, ghost):
    return roll_sub(jnp.where(subs() == 0, ghost, x), -1)


def west(x, ghost):
    return roll_sub(jnp.where(subs() == 7, ghost, x), 1)


def around(x, lat_ghost, lon_ghost):
    return (east(x, lon_ghost), west(x, lon_ghost), north(x, lat_ghost), south(x, lat_ghost))


def one_of(index, values):
    found = index == values[0]
    for value in values[1:]:
        found = found | (index == value)
    return found


def lat_field(x, f, odd):
    return roll_lane(x, 16 * f + 8 + 64 * odd)


def from_lat_group(x, f, odd):
    return roll_lane(x, -(16 * f + 8 + 64 * odd))


def group_of(lane):
    return lane // 16


def lat_pack_kernel(t_hbm, s_hbm, u_hbm, v_hbm, d_hbm, m_hbm, z_hbm, f_hbm, out_ref, t_ref, s_ref, u_ref, v_ref, d_ref, m_ref, z_ref, f_ref, sem):
    levels = t_ref.shape[0]
    pairs = (
        (t_hbm, t_ref), (s_hbm, s_ref), (u_hbm, u_ref), (v_hbm, v_ref), (d_hbm, d_ref), (m_hbm, m_ref), (z_hbm, z_ref), (f_hbm, f_ref),
    )
    copies = [pltpu.make_async_copy(src, dst, sem.at[i]) for i, (src, dst) in enumerate(pairs)]
    for copy in copies:
        copy.start()
    for copy in copies:
        copy.wait()
    group = group_of(lanes())

    def put(out, fields, odd):
        for f, x in enumerate(fields):
            out = jnp.where(group == f + 4 * odd, lat_field(x, f, odd), out)
        return out

    zero = jnp.zeros((8, 128), F32)
    for j in range(levels // 2):
        out = zero
        for odd in range(2):
            k = 2 * j + odd
            out = put(out, (u_ref[k], v_ref[k], t_ref[k], s_ref[k]), odd)
        out_ref[j] = out
    sea = m_ref[...].astype(F32)
    depth = (d_ref[...] * m_ref[...]).astype(F32)
    out_ref[levels // 2] = put(zero, (depth, sea * z_ref[...], sea * f_ref[...]), 0)


def lon_pack_kernel(info_ref, t_ref, s_ref, u_ref, v_ref, d_ref, m_ref, z_ref, f_ref, a_ref, b_ref, g_ref, q_ref, r_ref):
    levels = t_ref.shape[0]
    count = levels // 2 + 1
    lane, sub = lanes(), subs()
    is_even, is_top = info_ref[0], info_ref[1]
    from_north = lane % 16 >= 8
    flow_sign = jnp.where(group_of(lane) % 4 < 2, -1.0, 1.0).astype(F32)
    odd_lon = jnp.full((8, 128), info_ref[3] % 2, jnp.int32) == 1

    @pl.when(is_even == 1)
    def _():
        for j in range(count):
            g_ref[j] = jnp.where(from_north, a_ref[j], b_ref[j])

    @pl.when((is_even == 0) & (is_top == 0))
    def _():
        for j in range(count):
            g_ref[j] = jnp.where(from_north, b_ref[j], a_ref[j])

    @pl.when(is_top == 1)
    def _():
        for j in range(count):
            rows = jnp.concatenate([b_ref[j, 7 - i : 8 - i, :] for i in range(8)], axis=0)
            turned = roll_lane(rows, 1)
            for i in range(1, 7):
                turned = jnp.where(lane % 16 == 8 + i, roll_lane(rows, 1 + 2 * i), turned)
            if j < levels // 2:
                turned = turned * flow_sign
            g_ref[j] = jnp.where(from_north, turned, a_ref[j])

    def put(k, u, v, t, s):
        g = g_ref[k // 2]
        odd = k % 2
        v4, t2, s6 = roll_sub(v, 4), roll_sub(t, 2), roll_sub(s, 6)
        x = jnp.where((sub >= 4) & (sub <= 5), v4, u)
        x = jnp.where(sub == 2, t2, x)
        x = jnp.where(sub == 6, s6, x)
        to_west = jnp.where(sub == 3, roll_sub(g, 3 - odd), x)
        x = jnp.where((sub >= 2) & (sub <= 3), v4, u)
        x = jnp.where(sub == 1, t2, x)
        x = jnp.where(sub == 5, s6, x)
        to_east = jnp.where(sub == 0, roll_sub(g, 1 + odd), x)
        q_ref[k] = jnp.where(odd_lon, to_west, to_east)
        r_ref[k] = jnp.where(odd_lon, to_east, to_west)

    for k in range(levels):
        put(k, u_ref[k], v_ref[k], t_ref[k], s_ref[k])
    sea = m_ref[...].astype(F32)
    depth, start = (d_ref[...] * m_ref[...]).astype(F32), sea * z_ref[...]
    put(levels, depth, start, sea * f_ref[...], start)
    put(levels + 1, depth, start, start, start)


def lon_masks(info_ref):
    sub = subs()
    odd_lon = jnp.full((8, 128), info_ref[3] % 2, jnp.int32) == 1
    return [x != odd_lon for x in (one_of(sub, (0, 1, 4, 5)), sub == 2, sub == 6, sub == 3)]


def lon_ghost(q, r, masks):
    return jnp.where(masks[0], q, r)


def lon_tracers(q, r, masks):
    return roll_sub(jnp.where(masks[1], q, r), -2), roll_sub(jnp.where(masks[2], q, r), -6)


def corner_group(q_ref, r_ref, j, masks):
    sub = subs()
    x = jnp.where(masks[3], q_ref[2 * j], r_ref[2 * j])
    y = jnp.where(masks[3], q_ref[2 * j + 1], r_ref[2 * j + 1])
    return jnp.where(sub == 0, roll_sub(x, -3), jnp.where(sub == 7, roll_sub(x, -1), roll_sub(y, -2)))


LAT_PARTNER = (1, 0, 3, 2)
LON_PARTNER = (2, 3, 0, 1)


def ext_east(x):
    return [east(x[i], x[LON_PARTNER[i]]) for i in range(len(x))]


def ext_north(x):
    return [north(x[i], x[LAT_PARTNER[i]]) for i in range(len(x))]


def lap(x, mask_e, mask_n, tiles):
    f_e = [jnp.where(m, y - c, 0.0) for m, y, c in zip(mask_e, ext_east(x), x)]
    f_n = [jnp.where(m, y - c, 0.0) for m, y, c in zip(mask_n, ext_north(x), x)]
    out = []
    for i in tiles:
        out.append(f_e[i] - west(f_e[i], f_e[LON_PARTNER[i]]) + (f_n[i] - south(f_n[i], f_n[LAT_PARTNER[i]])))
    return out


def floats(i):
    return i.astype(F32)


def momentum_kernel(
    info_ref, th_ref, t_ref, s_ref, u_ref, v_ref, d_ref, m_ref, z_ref, f_ref, g_ref, q_ref, r_ref, us_ref, vs_ref, chunk_ref, st_ref
):
    levels = t_ref.shape[0]
    lane, sub = lanes(), subs()
    edges = lon_masks(info_ref)
    last = levels // 2
    sea = m_ref[...].astype(F32)
    corner = corner_group(q_ref, r_ref, last, edges)
    edge = lon_ghost(q_ref[levels], r_ref[levels], edges)
    depth = [(d_ref[...] * m_ref[...]).astype(F32), from_lat_group(g_ref[last], 0, 0), edge, from_lat_group(corner, 0, 0)]
    low_e = [jnp.minimum(x, y) for x, y in zip(depth, ext_east(depth))]
    low_n = [jnp.minimum(x, y) for x, y in zip(depth, ext_north(depth))]
    lat_index = (lane + info_ref[2] * 128).astype(F32)
    ghost_index = lat_index + jnp.where(lane < 64, 128.0, -128.0)
    lats = 128.0 * info_ref[4].astype(F32)
    ghost_index = jnp.where(ghost_index >= lats, 2.0 * lats - 1.0 - ghost_index, ghost_index)
    coriolis = [CORIOLIS * (2.0 * (x + 0.5) / lats - 1.0) for x in (lat_index, ghost_index)]
    zero = jnp.zeros((8, 128), F32)
    both = (0, 1)

    def level(k, odd, j, corners, carry):
        p, h, tu, tv = carry
        th = th_ref[k]
        kf = floats(k) + 0.5
        g, q_in, r_in = g_ref[j], q_ref[k], r_ref[k]
        u_h = lon_ghost(q_in, r_in, edges)
        t_h, s_h = lon_tracers(q_in, r_in, edges)
        u = [u_ref[k], from_lat_group(g, 0, odd), u_h, from_lat_group(corners, 0, odd)]
        v = [v_ref[k], from_lat_group(g, 1, odd), roll_sub(u_h, 4), from_lat_group(corners, 1, odd)]
        t = [t_ref[k], from_lat_group(g, 2, odd), t_h, from_lat_group(corners, 2, odd)]
        s = [s_ref[k], from_lat_group(g, 3, odd), s_h, from_lat_group(corners, 3, odd)]
        mask_e, mask_n, wet = [[x > kf for x in xs] for xs in (low_e, low_n, depth)]
        drag_u = lap(lap(u, mask_e, mask_n, range(4)), mask_e, mask_n, both)
        drag_v = lap(lap(v, mask_e, mask_n, range(4)), mask_e, mask_n, both)
        p = [c + jnp.where(m, (CONTRACTION * b - EXPANSION * a) * th, 0.0) for c, m, a, b in zip(p, wet, t, s)]
        h = [c + jnp.where(m, th, 0.0) for c, m in zip(h, wet)]
        f_e = [jnp.where(m, y - c, 0.0) for m, y, c in zip(mask_e, ext_east(p), p)]
        f_n = [jnp.where(m, y - c, 0.0) for m, y, c in zip(mask_n, ext_north(p), p)]
        us, vs = [], []
        for i in both:
            grad_x = f_e[i] + west(f_e[i], f_e[LON_PARTNER[i]])
            grad_y = f_n[i] + south(f_n[i], f_n[LAT_PARTNER[i]])
            x = u[i] + coriolis[i] * v[i] - (0.5 * PRESSURE_SCALE) * grad_x - FRICTION * drag_u[i]
            y = v[i] - coriolis[i] * u[i] - (0.5 * PRESSURE_SCALE) * grad_y - FRICTION * drag_v[i]
            us.append(jnp.where(wet[i], x, 0.0))
            vs.append(jnp.where(wet[i], y, 0.0))
        us_ref[k] = us[0]
        vs_ref[k] = vs[0]
        return (p, h, [a + th * b for a, b in zip(tu, us)], [a + th * b for a, b in zip(tv, vs)])

    def step(i, carry):
        for j in range(TILES_PER_STEP):
            at = i * TILES_PER_STEP + j
            corners = corner_group(q_ref, r_ref, at, edges)
            for odd in range(2):
                carry = level(2 * at + odd, odd, at, corners, carry)
        return carry

    _, h, tu, tv = lax.fori_loop(0, last // TILES_PER_STEP, step, ([zero] * 4, [zero] * 4, [zero] * 2, [zero] * 2))
    start = [sea * z_ref[...], from_lat_group(g_ref[last], 1, 0), roll_sub(edge, 4), from_lat_group(corner, 1, 0)]
    drive = [sea * f_ref[...], from_lat_group(g_ref[last], 2, 0)]
    weight_e = [jnp.minimum(x, y) * (1.0 / levels) for x, y in zip(h, ext_east(h))]
    weight_n = [jnp.minimum(x, y) * (1.0 / levels) for x, y in zip(h, ext_north(h))]
    flux_e = [x * (y - c) for x, y, c in zip(weight_e, ext_east(start), start)]
    flux_n = [x * (y - c) for x, y, c in zip(weight_n, ext_north(start), start)]
    rights = []
    for i in both:
        spread = flux_e[i] - west(flux_e[i], flux_e[LON_PARTNER[i]]) + (flux_n[i] - south(flux_n[i], flux_n[LAT_PARTNER[i]]))
        base = drive[i] - (STORAGE * start[i] - spread)
        tu_e = jnp.where(sub == 7, 0.0, roll_sub(tu[i], -1))
        tu_w = jnp.where(sub == 0, 0.0, roll_sub(tu[i], 1))
        tv_n, tv_s = north(tv[i], tv[1 - i]), south(tv[i], tv[1 - i])
        rights.append(base - jnp.where(h[i] > 0.0, (0.5 * DIVERGENCE) * ((tu_e - tu_w) + (tv_n - tv_s)), 0.0))
    halo = jnp.where(lane < 16, roll_lane(h[1], 8), jnp.where(lane < 32, roll_lane(rights[1], 24), roll_lane(tu[1], 40)))
    halo = jnp.where(lane < 64, halo, roll_lane(roll_sub(halo, 4), 64))
    halo = jnp.where(sub < 4, halo, jnp.where(sub == 4, roll_sub(tu[0], 4), roll_sub(tu[0], -2)))
    chunk_ref[0] = h[0]
    chunk_ref[1] = rights[0]
    chunk_ref[2] = halo
    for i in range(3):
        st_ref[i] = start[i]


def tracer_kernel(info_ref, th_ref, t_ref, s_ref, u_ref, v_ref, d_ref, m_ref, g_ref, q_ref, r_ref, after_ref, nt_ref, ns_ref):
    del after_ref
    levels = t_ref.shape[0]
    edges = lon_masks(info_ref)
    depth = (d_ref[...] * m_ref[...]).astype(F32)
    depth_g = from_lat_group(g_ref[levels // 2], 0, 0)
    depth_h = lon_ghost(q_ref[levels], r_ref[levels], edges)
    low = [jnp.minimum(depth, n) for n in around(depth, depth_g, depth_h)]
    zero = jnp.zeros((8, 128), F32)

    def level(k, odd, j, carry):
        above_t, above_s = carry
        kf = floats(k) + 0.5
        below = jnp.minimum(k + 1, levels - 1)
        th, th_below = th_ref[k], th_ref[below]
        u, v, t, s = u_ref[k], v_ref[k], t_ref[k], s_ref[k]
        g, q_in, r_in = g_ref[j], q_ref[k], r_ref[k]
        u_h = lon_ghost(q_in, r_in, edges)
        t_h, s_h = lon_tracers(q_in, r_in, edges)
        v_g = from_lat_group(g, 1, odd)
        wet = depth > kf
        wet_below = (depth > kf + 1.0) & (k + 1 < levels)
        inv_space = 1.0 / jnp.full((8, 128), 0.5 * (th + th_below), F32)
        inv_th = MIXING / jnp.full((8, 128), th, F32)
        flow = [0.25 * x for x in (u + east(u, u_h), west(u, u_h) + u, v + north(v, v_g), south(v, v_g) + v)]
        masks = [x > kf for x in low]
        fluxes = []
        for q, q_g, q_h, full_ref, above, out_ref in (
            (t, from_lat_group(g, 2, odd), t_h, t_ref, above_t, nt_ref),
            (s, from_lat_group(g, 3, odd), s_h, s_ref, above_s, ns_ref),
        ):
            q_e, q_w, q_n, q_s = around(q, q_g, q_h)
            f_e = jnp.where(masks[0], flow[0] * (q + q_e) - DIFFUSION * (q_e - q), 0.0)
            f_w = jnp.where(masks[1], flow[1] * (q_w + q) - DIFFUSION * (q - q_w), 0.0)
            f_n = jnp.where(masks[2], flow[2] * (q + q_n) - DIFFUSION * (q_n - q), 0.0)
            f_s = jnp.where(masks[3], flow[3] * (q_s + q) - DIFFUSION * (q - q_s), 0.0)
            vflux = jnp.where(wet_below, (full_ref[below] - q) * inv_space, 0.0)
            vertical = (vflux - above) * inv_th
            out_ref[k] = jnp.where(wet, q + (f_w - f_e + f_s - f_n) + vertical, 0.0)
            fluxes.append(vflux)
        return tuple(fluxes)

    def step(i, carry):
        for j in range(TILES_PER_STEP):
            at = i * TILES_PER_STEP + j
            for odd in range(2):
                carry = level(2 * at + odd, odd, at, carry)
        return carry

    lax.fori_loop(0, levels // 2 // TILES_PER_STEP, step, (zero, zero))


def slab_kernel(levels, info_ref, own_ref, q_ref, r_ref, st_ref, sum_ref, surf_ref, slope_ref, we_s, wn_s, fac_s, inv_s, r_s, d_s):
    odd_group = jnp.full((GROUP, 128), info_ref[3] // GROUP % 2, jnp.int32) == 1

    def rows(i):
        own, q, r = (ref[pl.ds(i, GROUP, stride=24), :] for ref in (own_ref, q_ref, r_ref))
        return jnp.concatenate([jnp.where(odd_group, q, r), own, jnp.where(odd_group, r, q)], axis=0)

    here = GROUP + info_ref[3] % GROUP
    right, left = here + 1, here - 1
    heights, tu = [], [None] * 8
    for p in range(8):
        packed = rows(16 + p % 4)
        at = 64 * (p // 4)
        heights.append(jnp.concatenate([rows(p), roll_lane(packed, -8 - at)], axis=1))
        r_s[p] = jnp.concatenate([rows(8 + p), roll_lane(packed, -24 - at)], axis=1)
        if p in (0, 7):
            tu[p] = jnp.concatenate([rows(20 if p == 0 else 21), roll_lane(packed, -40 - at)], axis=1)
    r_s[0] = r_s[0] + jnp.where(heights[0] > 0.0, (0.5 * DIVERGENCE) * roll_sub(tu[7], 1), 0.0)
    r_s[7] = r_s[7] - jnp.where(heights[7] > 0.0, (0.5 * DIVERGENCE) * roll_sub(tu[0], -1), 0.0)
    for p in range(8):
        h = heights[p]
        h_e = heights[p + 1] if p < 7 else roll_sub(heights[0], -1)
        we_s[p] = jnp.minimum(h, h_e) * (1.0 / levels)
        wn_s[p] = jnp.minimum(h, roll_lane(h, -1)) * (1.0 / levels)
    for p in range(8):
        w_w = we_s[p - 1] if p > 0 else roll_sub(we_s[7], 1)
        wn = wn_s[p]
        diag = STORAGE + we_s[p] + w_w + wn + roll_lane(wn, 1)
        if p > 0:
            diag = diag + w_w * fac_s[p - 1]
        inv = 1.0 / diag
        inv_s[p] = inv
        fac_s[p] = -we_s[p] * inv

    mid = 0.5 * (SPECTRUM_HIGH + SPECTRUM_LOW)
    half = 0.5 * (SPECTRUM_HIGH - SPECTRUM_LOW)
    ratio = mid / half

    def residuals():
        d, last = d_s[0], d_s[7]
        edge = we_s[7] * (roll_sub(d, -1) - last)
        f_w = roll_sub(edge, 1)
        for p in range(8):
            d_e = d_s[p + 1] if p < 7 else None
            f_e = we_s[p] * (d_e - d) if p < 7 else edge
            f_n = wn_s[p] * (roll_lane(d, -1) - d)
            yield r_s[p] - STORAGE * d + ((f_e - f_w) + (f_n - roll_lane(f_n, 1)))
            f_w, d = f_e, d_e

    def step(scale_old, scale_new, first):
        y = []
        for p, r in enumerate((r_s[p] for p in range(8)) if first else residuals()):
            if not first:
                r_s[p] = r
            y.append((r + we_s[p - 1] * y[p - 1] if p > 0 else r) * inv_s[p])
        x = None
        for p in range(7, -1, -1):
            x = y[p] if x is None else y[p] - fac_s[p] * x
            d_s[p] = x * scale_new if first else scale_old * d_s[p] + scale_new * x
        own = jnp.concatenate([d_s[p, pl.ds(here, 1), :] for p in range(8)], axis=0)
        return own, d_s[0, pl.ds(right, 1), :], d_s[7, pl.ds(left, 1), :]

    found = step(0.0, 1.0 / mid, True)
    rho = 1.0 / ratio
    for _ in range(ITERS - 1):
        rho_next = 1.0 / (2.0 * ratio - rho)
        found = [a + b for a, b in zip(found, step(rho_next * rho, 2.0 * rho_next / half, False))]
        rho = rho_next
    total = jnp.zeros((GROUP, 128), F32)
    for r in residuals():
        r = r[GROUP : 2 * GROUP, 0:128]
        total = total + r * r
    sum_ref[...] = jnp.sum(jnp.sum(total, axis=0, keepdims=True), axis=1, keepdims=True) + jnp.zeros((1, 128), F32)

    both, x_e, x_w = found
    x, x_g = both[:, 0:128], both[:, 128:256]
    sub = subs()
    x_e = jnp.broadcast_to(x_e[:, 0:128], (8, 128))
    x_w = jnp.broadcast_to(x_w[:, 0:128], (8, 128))
    x_h = jnp.where(sub < 4, x_e, x_w)
    x, x_g, x_h = x + st_ref[0], x_g + st_ref[1], x_h + st_ref[2]
    e, w, n, s = around(x, x_g, x_h)
    surf_ref[...] = x
    slope_ref[0] = (0.5 * GRAVITY) * (e - w)
    slope_ref[1] = (0.5 * GRAVITY) * (n - s)


def velocity_kernel(us_ref, vs_ref, d_ref, m_ref, slope_ref, nu_ref, nv_ref):
    depth = (d_ref[...] * m_ref[...]).astype(F32)
    slope_x, slope_y = slope_ref[0], slope_ref[1]
    for k in range(us_ref.shape[0]):
        wet = depth > k + 0.5
        nu_ref[k] = jnp.where(wet, us_ref[k] - slope_x, 0.0)
        nv_ref[k] = jnp.where(wet, vs_ref[k] - slope_y, 0.0)


def call(kernel, name, outs, in_specs, scratch=()):
    return pl.pallas_call(
        kernel,
        name=name,
        out_shape=outs,
        in_specs=in_specs,
        out_specs=jax.tree.map(lambda _: VMEM, outs),
        scratch_shapes=list(scratch),
        compiler_params=pltpu.CompilerParams(vmem_limit_bytes=48 << 20),
    )


def from_all(x, axes):
    size = 1
    for axis in axes:
        size *= lax.axis_size(axis)
    copies = jnp.broadcast_to(x[None], (size, *x.shape))
    return lax.all_to_all(copies, axes, 0, 0, tiled=True)


def per_device(lon_size, lat_size, temp, salt, u, v, strata, sea, thickness, elevation, drive):
    levels = temp.shape[0]
    lon, lat = lax.axis_index(LON), lax.axis_index("lat")
    top = lat_size - 1
    info = jnp.stack(
        [1 - lat % 2, (lat == top).astype(jnp.int32), lat, lon, jnp.int32(lat_size), jnp.int32(levels)]
    ).astype(jnp.int32)
    pairs_a = [(i, i ^ 1) for i in range(lat_size)]
    pairs_b = []
    for a in range(lon_size):
        for i in range(1, top, 2):
            pairs_b += [(a * lat_size + i, a * lat_size + i + 1), (a * lat_size + i + 1, a * lat_size + i)]
        pairs_b.append((a * lat_size + top, (lon_size - 1 - a) * lat_size + top))

    def lat_swap(x):
        return lax.ppermute(x, "lat", pairs_a), lax.ppermute(x, (*LON, "lat"), pairs_b)

    def tiles(n, kind=F32):
        return jax.ShapeDtypeStruct((n, 8, 128), kind)

    field, flat = tiles(levels), (8, 128)
    message, packed = tiles(levels + 2), tiles(levels // 2 + 1)
    own = (temp, salt, u, v, strata, sea, elevation, drive)

    edges = call(
        lat_pack_kernel,
        "lat_pack",
        packed,
        [pl.BlockSpec(memory_space=pltpu.HBM)] * 8,
        [pltpu.VMEM(field.shape, F32)] * 4
        + [pltpu.VMEM(flat, jnp.int32)] * 2
        + [pltpu.VMEM(flat, F32)] * 2
        + [pltpu.SemaphoreType.DMA((8,))],
    )(*[pltpu.with_memory_space_constraint(x, pltpu.HBM) for x in own])
    got_a, got_b = lat_swap(edges)
    ghost, pair_q, pair_r = call(lon_pack_kernel, "lon_pack", (packed, message, message), [SMEM] + [VMEM] * 10)(
        info, *own, got_a, got_b
    )
    pair_q = lax.ppermute(pair_q, LON, [(i, i ^ 1) for i in range(lon_size)])
    pair_r = lax.ppermute(pair_r, LON, [(i, (i + 1 if i % 2 else i - 1) % lon_size) for i in range(lon_size)])
    u_star, v_star, chunk, start = call(
        momentum_kernel, "momentum", (field, field, tiles(3), tiles(3)), [SMEM, SMEM] + [VMEM] * 11
    )(info, thickness, *own, ghost, pair_q, pair_r)
    group = from_all(chunk, ("lon_lo",)).reshape(GROUP * 24, 128)
    group, after = lax.optimization_barrier((group, chunk))
    groups = lon_size // GROUP
    group_q = lax.ppermute(group, "lon_hi", [(i, i ^ 1) for i in range(groups)])
    group_r = lax.ppermute(group, "lon_hi", [(i, (i + 1 if i % 2 else i - 1) % groups) for i in range(groups)])
    new_temp, new_salt = call(tracer_kernel, "tracers", (field, field), [SMEM] * 2 + [VMEM] * 10)(
        info, thickness, temp, salt, u, v, strata, sea, ghost, pair_q, pair_r, after
    )
    group_q, group_r, new_temp, new_salt = lax.optimization_barrier((group_q, group_r, new_temp, new_salt))
    total, surface, slope = call(
        functools.partial(slab_kernel, levels),
        "slab",
        (jax.ShapeDtypeStruct((1, 128), F32), jax.ShapeDtypeStruct((8, 128), F32), tiles(2)),
        [SMEM] + [VMEM] * 4,
        [pltpu.VMEM((8, 3 * GROUP, 256), F32)] * 6,
    )(info, group, group_q, group_r, start)
    total = jnp.sum(from_all(total, ("lon_hi", "lat")), axis=0)
    cells = lon_size * 8 * lat_size * 128
    rms = jnp.sqrt(total[0, 0] / cells + EPSILON)
    new_u, new_v = call(velocity_kernel, "velocity", (field, field), [VMEM] * 5)(u_star, v_star, strata, sea, slope)
    return (new_temp, new_salt, new_u, new_v, surface, rms)


def solution(mesh):
    lon_size, lat_size = mesh.shape["lon"], mesh.shape["lat"]
    finer = Mesh(mesh.devices.reshape(lon_size // GROUP, GROUP, lat_size), (*LON, "lat"))
    cube, flat = P(None, LON, "lat"), P(LON, "lat")
    return jax.shard_map(
        functools.partial(per_device, lon_size, lat_size),
        mesh=finer,
        in_specs=(cube, cube, cube, cube, flat, flat, P(), flat, flat),
        out_specs=(cube, cube, cube, cube, flat, P()),
        check_vma=False,
    )
```

```python
import functools

import jax
import jax.numpy as jnp
from jax import lax
from jax.experimental import pallas as pl
from jax.experimental.pallas import tpu as pltpu
from jax.sharding import Mesh
from jax.sharding import PartitionSpec as P

DIFFUSION = 0.15
MIXING = 0.1
EXPANSION = 0.2
CONTRACTION = 0.15
PRESSURE_SCALE = 0.02
CORIOLIS = 0.5
FRICTION = 0.01
DIVERGENCE = 0.3
STORAGE = 0.1
SPECTRUM_LOW = 0.1
SPECTRUM_HIGH = 1.9
GRAVITY = 0.3
EPSILON = 1e-06
ITERS = 4
TILES_PER_STEP = 4
GROUP = 8
LON = ("lon_hi", "lon_lo")
F32 = jnp.float32

VMEM = pl.BlockSpec(memory_space=pltpu.VMEM)
SMEM = pl.BlockSpec(memory_space=pltpu.SMEM)


def lanes(shape=(8, 128)):
    return lax.broadcasted_iota(jnp.int32, shape, 1)


def subs(shape=(8, 128)):
    return lax.broadcasted_iota(jnp.int32, shape, 0)


def roll_lane(x, shift):
    return pltpu.roll(x, shift % x.shape[1], 1)


def roll_sub(x, shift):
    return pltpu.roll(x, shift % x.shape[0], 0)


def north(x, ghost):
    return roll_lane(jnp.where(lanes() == 0, ghost, x), -1)


def south(x, ghost):
    return roll_lane(jnp.where(lanes() == 127, ghost, x), 1)


def east(x, ghost):
    return roll_sub(jnp.where(subs() == 0, ghost, x), -1)


def west(x, ghost):
    return roll_sub(jnp.where(subs() == 7, ghost, x), 1)


def around(x, lat_ghost, lon_ghost):
    return (east(x, lon_ghost), west(x, lon_ghost), north(x, lat_ghost), south(x, lat_ghost))


def one_of(index, values):
    found = index == values[0]
    for value in values[1:]:
        found = found | (index == value)
    return found


def lat_field(x, f, odd):
    return roll_lane(x, 16 * f + 8 + 64 * odd)


def from_lat_group(x, f, odd):
    return roll_lane(x, -(16 * f + 8 + 64 * odd))


def group_of(lane):
    return lane // 16


def lat_pack_kernel(t_hbm, s_hbm, u_hbm, v_hbm, d_hbm, m_hbm, z_hbm, f_hbm, out_ref, t_ref, s_ref, u_ref, v_ref, d_ref, m_ref, z_ref, f_ref, sem):
    levels = t_ref.shape[0]
    pairs = (
        (t_hbm, t_ref), (s_hbm, s_ref), (u_hbm, u_ref), (v_hbm, v_ref), (d_hbm, d_ref), (m_hbm, m_ref), (z_hbm, z_ref), (f_hbm, f_ref),
    )
    copies = [pltpu.make_async_copy(src, dst, sem.at[i]) for i, (src, dst) in enumerate(pairs)]
    for copy in copies:
        copy.start()
    for copy in copies:
        copy.wait()
    group = group_of(lanes())

    def put(out, fields, odd):
        for f, x in enumerate(fields):
            out = jnp.where(group == f + 4 * odd, lat_field(x, f, odd), out)
        return out

    zero = jnp.zeros((8, 128), F32)
    for j in range(levels // 2):
        out = zero
        for odd in range(2):
            k = 2 * j + odd
            out = put(out, (u_ref[k], v_ref[k], t_ref[k], s_ref[k]), odd)
        out_ref[j] = out
    sea = m_ref[...].astype(F32)
    depth = (d_ref[...] * m_ref[...]).astype(F32)
    out_ref[levels // 2] = put(zero, (depth, sea * z_ref[...], sea * f_ref[...]), 0)


def lon_rows_kernel(info_ref, t_ref, s_ref, u_ref, v_ref, d_ref, m_ref, z_ref, f_ref, q_ref, r_ref):
    levels = t_ref.shape[0]
    sub = subs()
    odd_lon = jnp.full((8, 128), info_ref[3] % 2, jnp.int32) == 1

    def put(k, u, v, t, s):
        v4, t2, s6 = roll_sub(v, 4), roll_sub(t, 2), roll_sub(s, 6)
        x = jnp.where((sub >= 4) & (sub <= 5), v4, u)
        x = jnp.where(sub == 2, t2, x)
        to_west = jnp.where(sub == 6, s6, x)
        x = jnp.where((sub >= 2) & (sub <= 3), v4, u)
        x = jnp.where(sub == 1, t2, x)
        to_east = jnp.where(sub == 5, s6, x)
        q_ref[k] = jnp.where(odd_lon, to_west, to_east)
        r_ref[k] = jnp.where(odd_lon, to_east, to_west)

    for k in range(levels):
        put(k, u_ref[k], v_ref[k], t_ref[k], s_ref[k])
    sea = m_ref[...].astype(F32)
    depth, start = (d_ref[...] * m_ref[...]).astype(F32), sea * z_ref[...]
    put(levels, depth, start, sea * f_ref[...], start)
    put(levels + 1, depth, start, start, start)


def corners_kernel(info_ref, a_ref, b_ref, q_in, r_in, g_ref, q_ref, r_ref):
    del q_in, r_in
    count = a_ref.shape[0]
    lane = lanes()
    is_even, is_top, odd_lon = info_ref[0], info_ref[1], info_ref[3] % 2
    from_north = lane % 16 >= 8
    flow_sign = jnp.where(group_of(lane) % 4 < 2, -1.0, 1.0).astype(F32)

    @pl.when(is_even == 1)
    def _():
        for j in range(count):
            g_ref[j] = jnp.where(from_north, a_ref[j], b_ref[j])

    @pl.when((is_even == 0) & (is_top == 0))
    def _():
        for j in range(count):
            g_ref[j] = jnp.where(from_north, b_ref[j], a_ref[j])

    @pl.when(is_top == 1)
    def _():
        for j in range(count):
            rows = jnp.concatenate([b_ref[j, 7 - i : 8 - i, :] for i in range(8)], axis=0)
            turned = roll_lane(rows, 1)
            for i in range(1, 7):
                turned = jnp.where(lane % 16 == 8 + i, roll_lane(rows, 1 + 2 * i), turned)
            if j < count - 1:
                turned = turned * flow_sign
            g_ref[j] = jnp.where(from_north, turned, a_ref[j])

    def put(west_ref, east_ref):
        for k in range(2 * count):
            odd = k % 2
            west_ref[k, 3:4, :] = g_ref[k // 2, odd : odd + 1, :]
            east_ref[k, 0:1, :] = g_ref[k // 2, 7 - odd : 8 - odd, :]

    @pl.when(odd_lon == 1)
    def _():
        put(q_ref, r_ref)

    @pl.when(odd_lon == 0)
    def _():
        put(r_ref, q_ref)


def lon_masks(info_ref):
    sub = subs()
    odd_lon = jnp.full((8, 128), info_ref[3] % 2, jnp.int32) == 1
    return [x != odd_lon for x in (one_of(sub, (0, 1, 4, 5)), sub == 2, sub == 6, sub == 3)]


def lon_ghost(q, r, masks):
    return jnp.where(masks[0], q, r)


def lon_tracers(q, r, masks):
    return roll_sub(jnp.where(masks[1], q, r), -2), roll_sub(jnp.where(masks[2], q, r), -6)


def corner_group(q_ref, r_ref, j, masks):
    sub = subs()
    x = jnp.where(masks[3], q_ref[2 * j], r_ref[2 * j])
    y = jnp.where(masks[3], q_ref[2 * j + 1], r_ref[2 * j + 1])
    return jnp.where(sub == 0, roll_sub(x, -3), jnp.where(sub == 7, roll_sub(x, -1), roll_sub(y, -2)))


LAT_PARTNER = (1, 0, 3, 2)
LON_PARTNER = (2, 3, 0, 1)


def ext_east(x):
    return [east(x[i], x[LON_PARTNER[i]]) for i in range(len(x))]


def ext_north(x):
    return [north(x[i], x[LAT_PARTNER[i]]) for i in range(len(x))]


def lap(x, mask_e, mask_n, tiles):
    f_e = [jnp.where(m, y - c, 0.0) for m, y, c in zip(mask_e, ext_east(x), x)]
    f_n = [jnp.where(m, y - c, 0.0) for m, y, c in zip(mask_n, ext_north(x), x)]
    out = []
    for i in tiles:
        out.append(f_e[i] - west(f_e[i], f_e[LON_PARTNER[i]]) + (f_n[i] - south(f_n[i], f_n[LAT_PARTNER[i]])))
    return out


def floats(i):
    return i.astype(F32)


def momentum_kernel(
    info_ref, th_ref, t_ref, s_ref, u_ref, v_ref, d_ref, m_ref, z_ref, f_ref, g_ref, q_ref, r_ref, us_ref, vs_ref, chunk_ref, st_ref
):
    levels = t_ref.shape[0]
    lane, sub = lanes(), subs()
    edges = lon_masks(info_ref)
    last = levels // 2
    sea = m_ref[...].astype(F32)
    corner = corner_group(q_ref, r_ref, last, edges)
    edge = lon_ghost(q_ref[levels], r_ref[levels], edges)
    depth = [(d_ref[...] * m_ref[...]).astype(F32), from_lat_group(g_ref[last], 0, 0), edge, from_lat_group(corner, 0, 0)]
    low_e = [jnp.minimum(x, y) for x, y in zip(depth, ext_east(depth))]
    low_n = [jnp.minimum(x, y) for x, y in zip(depth, ext_north(depth))]
    lat_index = (lane + info_ref[2] * 128).astype(F32)
    ghost_index = lat_index + jnp.where(lane < 64, 128.0, -128.0)
    lats = 128.0 * info_ref[4].astype(F32)
    ghost_index = jnp.where(ghost_index >= lats, 2.0 * lats - 1.0 - ghost_index, ghost_index)
    coriolis = [CORIOLIS * (2.0 * (x + 0.5) / lats - 1.0) for x in (lat_index, ghost_index)]
    zero = jnp.zeros((8, 128), F32)
    both = (0, 1)

    def level(k, odd, j, corners, carry):
        p, h, tu, tv = carry
        th = th_ref[k]
        kf = floats(k) + 0.5
        g, q_in, r_in = g_ref[j], q_ref[k], r_ref[k]
        u_h = lon_ghost(q_in, r_in, edges)
        t_h, s_h = lon_tracers(q_in, r_in, edges)
        u = [u_ref[k], from_lat_group(g, 0, odd), u_h, from_lat_group(corners, 0, odd)]
        v = [v_ref[k], from_lat_group(g, 1, odd), roll_sub(u_h, 4), from_lat_group(corners, 1, odd)]
        t = [t_ref[k], from_lat_group(g, 2, odd), t_h, from_lat_group(corners, 2, odd)]
        s = [s_ref[k], from_lat_group(g, 3, odd), s_h, from_lat_group(corners, 3, odd)]
        mask_e, mask_n, wet = [[x > kf for x in xs] for xs in (low_e, low_n, depth)]
        drag_u = lap(lap(u, mask_e, mask_n, range(4)), mask_e, mask_n, both)
        drag_v = lap(lap(v, mask_e, mask_n, range(4)), mask_e, mask_n, both)
        p = [c + jnp.where(m, (CONTRACTION * b - EXPANSION * a) * th, 0.0) for c, m, a, b in zip(p, wet, t, s)]
        h = [c + jnp.where(m, th, 0.0) for c, m in zip(h, wet)]
        f_e = [jnp.where(m, y - c, 0.0) for m, y, c in zip(mask_e, ext_east(p), p)]
        f_n = [jnp.where(m, y - c, 0.0) for m, y, c in zip(mask_n, ext_north(p), p)]
        us, vs = [], []
        for i in both:
            grad_x = f_e[i] + west(f_e[i], f_e[LON_PARTNER[i]])
            grad_y = f_n[i] + south(f_n[i], f_n[LAT_PARTNER[i]])
            x = u[i] + coriolis[i] * v[i] - (0.5 * PRESSURE_SCALE) * grad_x - FRICTION * drag_u[i]
            y = v[i] - coriolis[i] * u[i] - (0.5 * PRESSURE_SCALE) * grad_y - FRICTION * drag_v[i]
            us.append(jnp.where(wet[i], x, 0.0))
            vs.append(jnp.where(wet[i], y, 0.0))
        us_ref[k] = us[0]
        vs_ref[k] = vs[0]
        return (p, h, [a + th * b for a, b in zip(tu, us)], [a + th * b for a, b in zip(tv, vs)])

    def step(i, carry):
        for j in range(TILES_PER_STEP):
            at = i * TILES_PER_STEP + j
            corners = corner_group(q_ref, r_ref, at, edges)
            for odd in range(2):
                carry = level(2 * at + odd, odd, at, corners, carry)
        return carry

    _, h, tu, tv = lax.fori_loop(0, last // TILES_PER_STEP, step, ([zero] * 4, [zero] * 4, [zero] * 2, [zero] * 2))
    start = [sea * z_ref[...], from_lat_group(g_ref[last], 1, 0), roll_sub(edge, 4), from_lat_group(corner, 1, 0)]
    drive = [sea * f_ref[...], from_lat_group(g_ref[last], 2, 0)]
    weight_e = [jnp.minimum(x, y) * (1.0 / levels) for x, y in zip(h, ext_east(h))]
    weight_n = [jnp.minimum(x, y) * (1.0 / levels) for x, y in zip(h, ext_north(h))]
    flux_e = [x * (y - c) for x, y, c in zip(weight_e, ext_east(start), start)]
    flux_n = [x * (y - c) for x, y, c in zip(weight_n, ext_north(start), start)]
    rights = []
    for i in both:
        spread = flux_e[i] - west(flux_e[i], flux_e[LON_PARTNER[i]]) + (flux_n[i] - south(flux_n[i], flux_n[LAT_PARTNER[i]]))
        base = drive[i] - (STORAGE * start[i] - spread)
        tu_e = jnp.where(sub == 7, 0.0, roll_sub(tu[i], -1))
        tu_w = jnp.where(sub == 0, 0.0, roll_sub(tu[i], 1))
        tv_n, tv_s = north(tv[i], tv[1 - i]), south(tv[i], tv[1 - i])
        rights.append(base - jnp.where(h[i] > 0.0, (0.5 * DIVERGENCE) * ((tu_e - tu_w) + (tv_n - tv_s)), 0.0))
    halo = jnp.where(lane < 16, roll_lane(h[1], 8), jnp.where(lane < 32, roll_lane(rights[1], 24), roll_lane(tu[1], 40)))
    halo = jnp.where(lane < 64, halo, roll_lane(roll_sub(halo, 4), 64))
    halo = jnp.where(sub < 4, halo, jnp.where(sub == 4, roll_sub(tu[0], 4), roll_sub(tu[0], -2)))
    chunk_ref[0] = h[0]
    chunk_ref[1] = rights[0]
    chunk_ref[2] = halo
    for i in range(3):
        st_ref[i] = start[i]


def tracer_kernel(info_ref, th_ref, t_ref, s_ref, u_ref, v_ref, d_ref, m_ref, g_ref, q_ref, r_ref, after_ref, nt_ref, ns_ref):
    del after_ref
    levels = t_ref.shape[0]
    edges = lon_masks(info_ref)
    depth = (d_ref[...] * m_ref[...]).astype(F32)
    depth_g = from_lat_group(g_ref[levels // 2], 0, 0)
    depth_h = lon_ghost(q_ref[levels], r_ref[levels], edges)
    low = [jnp.minimum(depth, n) for n in around(depth, depth_g, depth_h)]
    zero = jnp.zeros((8, 128), F32)

    def level(k, odd, j, carry):
        above_t, above_s = carry
        kf = floats(k) + 0.5
        below = jnp.minimum(k + 1, levels - 1)
        th, th_below = th_ref[k], th_ref[below]
        u, v, t, s = u_ref[k], v_ref[k], t_ref[k], s_ref[k]
        g, q_in, r_in = g_ref[j], q_ref[k], r_ref[k]
        u_h = lon_ghost(q_in, r_in, edges)
        t_h, s_h = lon_tracers(q_in, r_in, edges)
        v_g = from_lat_group(g, 1, odd)
        wet = depth > kf
        wet_below = (depth > kf + 1.0) & (k + 1 < levels)
        inv_space = 1.0 / jnp.full((8, 128), 0.5 * (th + th_below), F32)
        inv_th = MIXING / jnp.full((8, 128), th, F32)
        flow = [0.25 * x for x in (u + east(u, u_h), west(u, u_h) + u, v + north(v, v_g), south(v, v_g) + v)]
        masks = [x > kf for x in low]
        fluxes = []
        for q, q_g, q_h, full_ref, above, out_ref in (
            (t, from_lat_group(g, 2, odd), t_h, t_ref, above_t, nt_ref),
            (s, from_lat_group(g, 3, odd), s_h, s_ref, above_s, ns_ref),
        ):
            q_e, q_w, q_n, q_s = around(q, q_g, q_h)
            f_e = jnp.where(masks[0], flow[0] * (q + q_e) - DIFFUSION * (q_e - q), 0.0)
            f_w = jnp.where(masks[1], flow[1] * (q_w + q) - DIFFUSION * (q - q_w), 0.0)
            f_n = jnp.where(masks[2], flow[2] * (q + q_n) - DIFFUSION * (q_n - q), 0.0)
            f_s = jnp.where(masks[3], flow[3] * (q_s + q) - DIFFUSION * (q - q_s), 0.0)
            vflux = jnp.where(wet_below, (full_ref[below] - q) * inv_space, 0.0)
            vertical = (vflux - above) * inv_th
            out_ref[k] = jnp.where(wet, q + (f_w - f_e + f_s - f_n) + vertical, 0.0)
            fluxes.append(vflux)
        return tuple(fluxes)

    def step(i, carry):
        for j in range(TILES_PER_STEP):
            at = i * TILES_PER_STEP + j
            for odd in range(2):
                carry = level(2 * at + odd, odd, at, carry)
        return carry

    lax.fori_loop(0, levels // 2 // TILES_PER_STEP, step, (zero, zero))


def slab_kernel(levels, info_ref, own_ref, q_ref, r_ref, st_ref, sum_ref, surf_ref, slope_ref, we_s, wn_s, fac_s, inv_s, r_s, d_s):
    odd_group = jnp.full((GROUP, 128), info_ref[3] // GROUP % 2, jnp.int32) == 1

    def rows(i):
        own, q, r = (ref[pl.ds(i, GROUP, stride=24), :] for ref in (own_ref, q_ref, r_ref))
        return jnp.concatenate([jnp.where(odd_group, q, r), own, jnp.where(odd_group, r, q)], axis=0)

    here = GROUP + info_ref[3] % GROUP
    right, left = here + 1, here - 1
    heights, tu = [], [None] * 8
    for p in range(8):
        packed = rows(16 + p % 4)
        at = 64 * (p // 4)
        heights.append(jnp.concatenate([rows(p), roll_lane(packed, -8 - at)], axis=1))
        r_s[p] = jnp.concatenate([rows(8 + p), roll_lane(packed, -24 - at)], axis=1)
        if p in (0, 7):
            tu[p] = jnp.concatenate([rows(20 if p == 0 else 21), roll_lane(packed, -40 - at)], axis=1)
    r_s[0] = r_s[0] + jnp.where(heights[0] > 0.0, (0.5 * DIVERGENCE) * roll_sub(tu[7], 1), 0.0)
    r_s[7] = r_s[7] - jnp.where(heights[7] > 0.0, (0.5 * DIVERGENCE) * roll_sub(tu[0], -1), 0.0)
    for p in range(8):
        h = heights[p]
        h_e = heights[p + 1] if p < 7 else roll_sub(heights[0], -1)
        we_s[p] = jnp.minimum(h, h_e) * (1.0 / levels)
        wn_s[p] = jnp.minimum(h, roll_lane(h, -1)) * (1.0 / levels)
    for p in range(8):
        w_w = we_s[p - 1] if p > 0 else roll_sub(we_s[7], 1)
        wn = wn_s[p]
        diag = STORAGE + we_s[p] + w_w + wn + roll_lane(wn, 1)
        if p > 0:
            diag = diag + w_w * fac_s[p - 1]
        inv = 1.0 / diag
        inv_s[p] = inv
        fac_s[p] = -we_s[p] * inv

    mid = 0.5 * (SPECTRUM_HIGH + SPECTRUM_LOW)
    half = 0.5 * (SPECTRUM_HIGH - SPECTRUM_LOW)
    ratio = mid / half

    def residuals():
        d, last = d_s[0], d_s[7]
        edge = we_s[7] * (roll_sub(d, -1) - last)
        f_w = roll_sub(edge, 1)
        for p in range(8):
            d_e = d_s[p + 1] if p < 7 else None
            f_e = we_s[p] * (d_e - d) if p < 7 else edge
            f_n = wn_s[p] * (roll_lane(d, -1) - d)
            yield r_s[p] - STORAGE * d + ((f_e - f_w) + (f_n - roll_lane(f_n, 1)))
            f_w, d = f_e, d_e

    def step(scale_old, scale_new, first):
        y = []
        for p, r in enumerate((r_s[p] for p in range(8)) if first else residuals()):
            if not first:
                r_s[p] = r
            y.append((r + we_s[p - 1] * y[p - 1] if p > 0 else r) * inv_s[p])
        x = None
        for p in range(7, -1, -1):
            x = y[p] if x is None else y[p] - fac_s[p] * x
            d_s[p] = x * scale_new if first else scale_old * d_s[p] + scale_new * x
        own = jnp.concatenate([d_s[p, pl.ds(here, 1), :] for p in range(8)], axis=0)
        return own, d_s[0, pl.ds(right, 1), :], d_s[7, pl.ds(left, 1), :]

    found = step(0.0, 1.0 / mid, True)
    rho = 1.0 / ratio
    for _ in range(ITERS - 1):
        rho_next = 1.0 / (2.0 * ratio - rho)
        found = [a + b for a, b in zip(found, step(rho_next * rho, 2.0 * rho_next / half, False))]
        rho = rho_next
    total = jnp.zeros((GROUP, 128), F32)
    for r in residuals():
        r = r[GROUP : 2 * GROUP, 0:128]
        total = total + r * r
    total = jnp.sum(jnp.sum(total, axis=0, keepdims=True), axis=1, keepdims=True) + jnp.zeros((1, 128), F32)
    for i in range(sum_ref.shape[0]):
        sum_ref[i] = total

    both, x_e, x_w = found
    x, x_g = both[:, 0:128], both[:, 128:256]
    sub = subs()
    x_e = jnp.broadcast_to(x_e[:, 0:128], (8, 128))
    x_w = jnp.broadcast_to(x_w[:, 0:128], (8, 128))
    x_h = jnp.where(sub < 4, x_e, x_w)
    x, x_g, x_h = x + st_ref[0], x_g + st_ref[1], x_h + st_ref[2]
    e, w, n, s = around(x, x_g, x_h)
    surf_ref[...] = x
    slope_ref[0] = (0.5 * GRAVITY) * (e - w)
    slope_ref[1] = (0.5 * GRAVITY) * (n - s)


def velocity_kernel(us_ref, vs_ref, d_ref, m_ref, slope_ref, nu_ref, nv_ref):
    depth = (d_ref[...] * m_ref[...]).astype(F32)
    slope_x, slope_y = slope_ref[0], slope_ref[1]
    for k in range(us_ref.shape[0]):
        wet = depth > k + 0.5
        nu_ref[k] = jnp.where(wet, us_ref[k] - slope_x, 0.0)
        nv_ref[k] = jnp.where(wet, vs_ref[k] - slope_y, 0.0)


def call(kernel, name, outs, in_specs, scratch=(), aliases=None):
    return pl.pallas_call(
        kernel,
        name=name,
        out_shape=outs,
        in_specs=in_specs,
        out_specs=jax.tree.map(lambda _: VMEM, outs),
        scratch_shapes=list(scratch),
        input_output_aliases=aliases or {},
        compiler_params=pltpu.CompilerParams(vmem_limit_bytes=48 << 20),
    )


def from_all(x, axes):
    size = 1
    for axis in axes:
        size *= lax.axis_size(axis)
    copies = jnp.broadcast_to(x[None], (size, *x.shape))
    return lax.all_to_all(copies, axes, 0, 0, tiled=True)


def per_device(lon_size, lat_size, temp, salt, u, v, strata, sea, thickness, elevation, drive):
    levels = temp.shape[0]
    lon, lat = lax.axis_index(LON), lax.axis_index("lat")
    top = lat_size - 1
    info = jnp.stack(
        [1 - lat % 2, (lat == top).astype(jnp.int32), lat, lon, jnp.int32(lat_size), jnp.int32(levels)]
    ).astype(jnp.int32)
    pairs_a = [(i, i ^ 1) for i in range(lat_size)]
    pairs_b = []
    for a in range(lon_size):
        for i in range(1, top, 2):
            pairs_b += [(a * lat_size + i, a * lat_size + i + 1), (a * lat_size + i + 1, a * lat_size + i)]
        pairs_b.append((a * lat_size + top, (lon_size - 1 - a) * lat_size + top))

    def lat_swap(x):
        return lax.ppermute(x, "lat", pairs_a), lax.ppermute(x, (*LON, "lat"), pairs_b)

    def tiles(n, kind=F32):
        return jax.ShapeDtypeStruct((n, 8, 128), kind)

    field, flat = tiles(levels), (8, 128)
    message, packed = tiles(levels + 2), tiles(levels // 2 + 1)
    own = (temp, salt, u, v, strata, sea, elevation, drive)

    edges = call(
        lat_pack_kernel,
        "lat_pack",
        packed,
        [pl.BlockSpec(memory_space=pltpu.HBM)] * 8,
        [pltpu.VMEM(field.shape, F32)] * 4
        + [pltpu.VMEM(flat, jnp.int32)] * 2
        + [pltpu.VMEM(flat, F32)] * 2
        + [pltpu.SemaphoreType.DMA((8,))],
    )(*[pltpu.with_memory_space_constraint(x, pltpu.HBM) for x in own])
    got_a, got_b = lat_swap(edges)
    rows_q, rows_r = call(lon_rows_kernel, "lon_rows", (message, message), [SMEM] + [VMEM] * 8)(info, *own)
    ghost, pair_q, pair_r = call(
        corners_kernel, "corners", (packed, message, message), [SMEM] + [VMEM] * 4, aliases={3: 1, 4: 2}
    )(info, got_a, got_b, rows_q, rows_r)
    pair_q = lax.ppermute(pair_q, LON, [(i, i ^ 1) for i in range(lon_size)])
    pair_r = lax.ppermute(pair_r, LON, [(i, (i + 1 if i % 2 else i - 1) % lon_size) for i in range(lon_size)])
    u_star, v_star, chunk, start = call(
        momentum_kernel, "momentum", (field, field, tiles(3), tiles(3)), [SMEM, SMEM] + [VMEM] * 11
    )(info, thickness, *own, ghost, pair_q, pair_r)
    group = from_all(chunk, ("lon_lo",)).reshape(GROUP * 24, 128)
    group, after = lax.optimization_barrier((group, chunk))
    groups = lon_size // GROUP
    group_q = lax.ppermute(group, "lon_hi", [(i, i ^ 1) for i in range(groups)])
    group_r = lax.ppermute(group, "lon_hi", [(i, (i + 1 if i % 2 else i - 1) % groups) for i in range(groups)])
    new_temp, new_salt = call(tracer_kernel, "tracers", (field, field), [SMEM] * 2 + [VMEM] * 10)(
        info, thickness, temp, salt, u, v, strata, sea, ghost, pair_q, pair_r, after
    )
    group_q, group_r, new_temp, new_salt = lax.optimization_barrier((group_q, group_r, new_temp, new_salt))
    sums, surface, slope = call(
        functools.partial(slab_kernel, levels),
        "slab",
        (jax.ShapeDtypeStruct((groups * lat_size, 1, 128), F32), jax.ShapeDtypeStruct((8, 128), F32), tiles(2)),
        [SMEM] + [VMEM] * 4,
        [pltpu.VMEM((8, 3 * GROUP, 256), F32)] * 6,
    )(info, group, group_q, group_r, start)
    sums = lax.all_to_all(sums, ("lon_hi", "lat"), 0, 0, tiled=True)
    total = jnp.sum(sums, axis=0)
    cells = lon_size * 8 * lat_size * 128
    rms = jnp.sqrt(total[0, 0] / cells + EPSILON)
    new_u, new_v = call(velocity_kernel, "velocity", (field, field), [VMEM] * 5)(u_star, v_star, strata, sea, slope)
    return (new_temp, new_salt, new_u, new_v, surface, rms)


def solution(mesh):
    lon_size, lat_size = mesh.shape["lon"], mesh.shape["lat"]
    finer = Mesh(mesh.devices.reshape(lon_size // GROUP, GROUP, lat_size), (*LON, "lat"))
    cube, flat = P(None, LON, "lat"), P(LON, "lat")
    return jax.shard_map(
        functools.partial(per_device, lon_size, lat_size),
        mesh=finer,
        in_specs=(cube, cube, cube, cube, flat, flat, P(), flat, flat),
        out_specs=(cube, cube, cube, cube, flat, P()),
        check_vma=False,
    )
```

```python
import functools

import jax
import jax.numpy as jnp
from jax import lax
from jax.experimental import pallas as pl
from jax.experimental.pallas import tpu as pltpu
from jax.sharding import Mesh
from jax.sharding import PartitionSpec as P

DIFFUSION = 0.15
MIXING = 0.1
EXPANSION = 0.2
CONTRACTION = 0.15
PRESSURE_SCALE = 0.02
CORIOLIS = 0.5
FRICTION = 0.01
DIVERGENCE = 0.3
STORAGE = 0.1
SPECTRUM_LOW = 0.1
SPECTRUM_HIGH = 1.9
GRAVITY = 0.3
EPSILON = 1e-06
ITERS = 4
TILES_PER_STEP = 4
GROUP = 8
LON = ("lon_hi", "lon_lo")
F32 = jnp.float32

VMEM = pl.BlockSpec(memory_space=pltpu.VMEM)
SMEM = pl.BlockSpec(memory_space=pltpu.SMEM)


def lanes(shape=(8, 128)):
    return lax.broadcasted_iota(jnp.int32, shape, 1)


def subs(shape=(8, 128)):
    return lax.broadcasted_iota(jnp.int32, shape, 0)


def roll_lane(x, shift):
    return pltpu.roll(x, shift % x.shape[1], 1)


def roll_sub(x, shift):
    return pltpu.roll(x, shift % x.shape[0], 0)


def north(x, ghost):
    return roll_lane(jnp.where(lanes() == 0, ghost, x), -1)


def south(x, ghost):
    return roll_lane(jnp.where(lanes() == 127, ghost, x), 1)


def east(x, ghost):
    return roll_sub(jnp.where(subs() == 0, ghost, x), -1)


def west(x, ghost):
    return roll_sub(jnp.where(subs() == 7, ghost, x), 1)


def around(x, lat_ghost, lon_ghost):
    return (east(x, lon_ghost), west(x, lon_ghost), north(x, lat_ghost), south(x, lat_ghost))


def one_of(index, values):
    found = index == values[0]
    for value in values[1:]:
        found = found | (index == value)
    return found


def lat_field(x, f, odd):
    return roll_lane(x, 16 * f + 8 + 64 * odd)


def from_lat_group(x, f, odd):
    return roll_lane(x, -(16 * f + 8 + 64 * odd))


def group_of(lane):
    return lane // 16


def lat_pack_kernel(t_hbm, s_hbm, u_hbm, v_hbm, d_hbm, m_hbm, z_hbm, f_hbm, out_ref, t_ref, s_ref, u_ref, v_ref, d_ref, m_ref, z_ref, f_ref, sem):
    levels = t_ref.shape[0]
    half = levels // 2
    fields = ((t_hbm, t_ref), (s_hbm, s_ref), (u_hbm, u_ref), (v_hbm, v_ref))
    parts = [[(src.at[i : i + half], dst.at[i : i + half]) for src, dst in fields] for i in (0, half)]
    parts.append([(d_hbm, d_ref), (m_hbm, m_ref), (z_hbm, z_ref), (f_hbm, f_ref)])
    copies = [[pltpu.make_async_copy(*p, sem.at[i, j]) for j, p in enumerate(part)] for i, part in enumerate(parts)]
    for part in copies:
        for copy in part:
            copy.start()
    group = group_of(lanes())

    def put(out, fields, odd):
        for f, x in enumerate(fields):
            out = jnp.where(group == f + 4 * odd, lat_field(x, f, odd), out)
        return out

    zero = jnp.zeros((8, 128), F32)
    for j in range(levels // 2):
        if j % (half // 2) == 0:
            for copy in copies[j // (half // 2)]:
                copy.wait()
        out = zero
        for odd in range(2):
            k = 2 * j + odd
            out = put(out, (u_ref[k], v_ref[k], t_ref[k], s_ref[k]), odd)
        out_ref[j] = out
    for copy in copies[2]:
        copy.wait()
    sea = m_ref[...].astype(F32)
    depth = (d_ref[...] * m_ref[...]).astype(F32)
    out_ref[levels // 2] = put(zero, (depth, sea * z_ref[...], sea * f_ref[...]), 0)


def lon_rows_kernel(info_ref, t_ref, s_ref, u_ref, v_ref, d_ref, m_ref, z_ref, f_ref, q_ref, r_ref):
    levels = t_ref.shape[0]
    sub = subs()
    odd_lon = jnp.full((8, 128), info_ref[3] % 2, jnp.int32) == 1

    def put(k, u, v, t, s):
        v4, t2, s6 = roll_sub(v, 4), roll_sub(t, 2), roll_sub(s, 6)
        x = jnp.where((sub >= 4) & (sub <= 5), v4, u)
        x = jnp.where(sub == 2, t2, x)
        to_west = jnp.where(sub == 6, s6, x)
        x = jnp.where((sub >= 2) & (sub <= 3), v4, u)
        x = jnp.where(sub == 1, t2, x)
        to_east = jnp.where(sub == 5, s6, x)
        q_ref[k] = jnp.where(odd_lon, to_west, to_east)
        r_ref[k] = jnp.where(odd_lon, to_east, to_west)

    for k in range(levels):
        put(k, u_ref[k], v_ref[k], t_ref[k], s_ref[k])
    sea = m_ref[...].astype(F32)
    depth, start = (d_ref[...] * m_ref[...]).astype(F32), sea * z_ref[...]
    put(levels, depth, start, sea * f_ref[...], start)
    put(levels + 1, depth, start, start, start)


def turn_rows(x):
    sub = subs()
    x = roll_sub(x, 4)
    x = jnp.where(sub // 2 % 2 == 0, roll_sub(x, -2), roll_sub(x, 2))
    return jnp.where(sub % 2 == 0, roll_sub(x, -1), roll_sub(x, 1))


def corners_kernel(info_ref, a_ref, b_ref, r_in, q_in, g_ref, r_ref, q_ref):
    del q_in, r_in
    count = a_ref.shape[0]
    lane = lanes()
    is_even, is_top, odd_lon = info_ref[0], info_ref[1], info_ref[3] % 2
    from_north = lane % 16 >= 8
    flow_sign = jnp.where(group_of(lane) % 4 < 2, -1.0, 1.0).astype(F32)

    @pl.when(is_even == 1)
    def _():
        for j in range(count):
            g_ref[j] = jnp.where(from_north, a_ref[j], b_ref[j])

    @pl.when((is_even == 0) & (is_top == 0))
    def _():
        for j in range(count):
            g_ref[j] = jnp.where(from_north, b_ref[j], a_ref[j])

    @pl.when(is_top == 1)
    def _():
        for j in range(count):
            rows = turn_rows(b_ref[j])
            turned = roll_lane(rows, 1)
            for i in range(1, 7):
                turned = jnp.where(lane % 16 == 8 + i, roll_lane(rows, 1 + 2 * i), turned)
            if j < count - 1:
                turned = turned * flow_sign
            g_ref[j] = jnp.where(from_north, turned, a_ref[j])

    def put(west_ref, east_ref):
        for k in range(2 * count):
            odd = k % 2
            west_ref[k, 3:4, :] = g_ref[k // 2, odd : odd + 1, :]
            east_ref[k, 0:1, :] = g_ref[k // 2, 7 - odd : 8 - odd, :]

    @pl.when(odd_lon == 1)
    def _():
        put(q_ref, r_ref)

    @pl.when(odd_lon == 0)
    def _():
        put(r_ref, q_ref)


def lon_masks(info_ref):
    sub = subs()
    odd_lon = jnp.full((8, 128), info_ref[3] % 2, jnp.int32) == 1
    return [x != odd_lon for x in (one_of(sub, (0, 1, 4, 5)), sub == 2, sub == 6, sub == 3)]


def lon_ghost(q, r, masks):
    return jnp.where(masks[0], q, r)


def lon_tracers(q, r, masks):
    return roll_sub(jnp.where(masks[1], q, r), -2), roll_sub(jnp.where(masks[2], q, r), -6)


def corner_group(q_ref, r_ref, j, masks):
    sub = subs()
    x = jnp.where(masks[3], q_ref[2 * j], r_ref[2 * j])
    y = jnp.where(masks[3], q_ref[2 * j + 1], r_ref[2 * j + 1])
    return jnp.where(sub == 0, roll_sub(x, -3), jnp.where(sub == 7, roll_sub(x, -1), roll_sub(y, -2)))


LAT_PARTNER = (1, 0, 3, 2)
LON_PARTNER = (2, 3, 0, 1)


def ext_east(x):
    return [east(x[i], x[LON_PARTNER[i]]) for i in range(len(x))]


def ext_north(x):
    return [north(x[i], x[LAT_PARTNER[i]]) for i in range(len(x))]


def lap(x, mask_e, mask_n, tiles):
    f_e = [jnp.where(m, y - c, 0.0) for m, y, c in zip(mask_e, ext_east(x), x)]
    f_n = [jnp.where(m, y - c, 0.0) for m, y, c in zip(mask_n, ext_north(x), x)]
    out = []
    for i in tiles:
        out.append(f_e[i] - west(f_e[i], f_e[LON_PARTNER[i]]) + (f_n[i] - south(f_n[i], f_n[LAT_PARTNER[i]])))
    return out


def floats(i):
    return i.astype(F32)


def momentum_kernel(
    info_ref, th_ref, t_ref, s_ref, u_ref, v_ref, d_ref, m_ref, z_ref, f_ref, g_ref, r_ref, q_ref, us_ref, vs_ref, chunk_ref, st_ref
):
    levels = t_ref.shape[0]
    lane, sub = lanes(), subs()
    edges = lon_masks(info_ref)
    last = levels // 2
    sea = m_ref[...].astype(F32)
    corner = corner_group(q_ref, r_ref, last, edges)
    edge = lon_ghost(q_ref[levels], r_ref[levels], edges)
    depth = [(d_ref[...] * m_ref[...]).astype(F32), from_lat_group(g_ref[last], 0, 0), edge, from_lat_group(corner, 0, 0)]
    low_e = [jnp.minimum(x, y) for x, y in zip(depth, ext_east(depth))]
    low_n = [jnp.minimum(x, y) for x, y in zip(depth, ext_north(depth))]
    lat_index = (lane + info_ref[2] * 128).astype(F32)
    ghost_index = lat_index + jnp.where(lane < 64, 128.0, -128.0)
    lats = 128.0 * info_ref[4].astype(F32)
    ghost_index = jnp.where(ghost_index >= lats, 2.0 * lats - 1.0 - ghost_index, ghost_index)
    coriolis = [CORIOLIS * (2.0 * (x + 0.5) / lats - 1.0) for x in (lat_index, ghost_index)]
    zero = jnp.zeros((8, 128), F32)
    both = (0, 1)

    def level(k, odd, j, corners, carry):
        p, h, tu, tv = carry
        th = th_ref[k]
        kf = floats(k) + 0.5
        g, q_in, r_in = g_ref[j], q_ref[k], r_ref[k]
        u_h = lon_ghost(q_in, r_in, edges)
        t_h, s_h = lon_tracers(q_in, r_in, edges)
        u = [u_ref[k], from_lat_group(g, 0, odd), u_h, from_lat_group(corners, 0, odd)]
        v = [v_ref[k], from_lat_group(g, 1, odd), roll_sub(u_h, 4), from_lat_group(corners, 1, odd)]
        t = [t_ref[k], from_lat_group(g, 2, odd), t_h, from_lat_group(corners, 2, odd)]
        s = [s_ref[k], from_lat_group(g, 3, odd), s_h, from_lat_group(corners, 3, odd)]
        mask_e, mask_n, wet = [[x > kf for x in xs] for xs in (low_e, low_n, depth)]
        drag_u = lap(lap(u, mask_e, mask_n, range(4)), mask_e, mask_n, both)
        drag_v = lap(lap(v, mask_e, mask_n, range(4)), mask_e, mask_n, both)
        p = [c + jnp.where(m, (CONTRACTION * b - EXPANSION * a) * th, 0.0) for c, m, a, b in zip(p, wet, t, s)]
        h = [c + jnp.where(m, th, 0.0) for c, m in zip(h, wet)]
        f_e = [jnp.where(m, y - c, 0.0) for m, y, c in zip(mask_e, ext_east(p), p)]
        f_n = [jnp.where(m, y - c, 0.0) for m, y, c in zip(mask_n, ext_north(p), p)]
        us, vs = [], []
        for i in both:
            grad_x = f_e[i] + west(f_e[i], f_e[LON_PARTNER[i]])
            grad_y = f_n[i] + south(f_n[i], f_n[LAT_PARTNER[i]])
            x = u[i] + coriolis[i] * v[i] - (0.5 * PRESSURE_SCALE) * grad_x - FRICTION * drag_u[i]
            y = v[i] - coriolis[i] * u[i] - (0.5 * PRESSURE_SCALE) * grad_y - FRICTION * drag_v[i]
            us.append(jnp.where(wet[i], x, 0.0))
            vs.append(jnp.where(wet[i], y, 0.0))
        us_ref[k] = us[0]
        vs_ref[k] = vs[0]
        return (p, h, [a + th * b for a, b in zip(tu, us)], [a + th * b for a, b in zip(tv, vs)])

    def step(i, carry):
        for j in range(TILES_PER_STEP):
            at = i * TILES_PER_STEP + j
            corners = corner_group(q_ref, r_ref, at, edges)
            for odd in range(2):
                carry = level(2 * at + odd, odd, at, corners, carry)
        return carry

    _, h, tu, tv = lax.fori_loop(0, last // TILES_PER_STEP, step, ([zero] * 4, [zero] * 4, [zero] * 2, [zero] * 2))
    start = [sea * z_ref[...], from_lat_group(g_ref[last], 1, 0), roll_sub(edge, 4), from_lat_group(corner, 1, 0)]
    drive = [sea * f_ref[...], from_lat_group(g_ref[last], 2, 0)]
    weight_e = [jnp.minimum(x, y) * (1.0 / levels) for x, y in zip(h, ext_east(h))]
    weight_n = [jnp.minimum(x, y) * (1.0 / levels) for x, y in zip(h, ext_north(h))]
    flux_e = [x * (y - c) for x, y, c in zip(weight_e, ext_east(start), start)]
    flux_n = [x * (y - c) for x, y, c in zip(weight_n, ext_north(start), start)]
    rights = []
    for i in both:
        spread = flux_e[i] - west(flux_e[i], flux_e[LON_PARTNER[i]]) + (flux_n[i] - south(flux_n[i], flux_n[LAT_PARTNER[i]]))
        base = drive[i] - (STORAGE * start[i] - spread)
        tu_e = jnp.where(sub == 7, 0.0, roll_sub(tu[i], -1))
        tu_w = jnp.where(sub == 0, 0.0, roll_sub(tu[i], 1))
        tv_n, tv_s = north(tv[i], tv[1 - i]), south(tv[i], tv[1 - i])
        rights.append(base - jnp.where(h[i] > 0.0, (0.5 * DIVERGENCE) * ((tu_e - tu_w) + (tv_n - tv_s)), 0.0))
    halo = jnp.where(lane < 16, roll_lane(h[1], 8), jnp.where(lane < 32, roll_lane(rights[1], 24), roll_lane(tu[1], 40)))
    halo = jnp.where(lane < 64, halo, roll_lane(roll_sub(halo, 4), 64))
    halo = jnp.where(sub < 4, halo, jnp.where(sub == 4, roll_sub(tu[0], 4), roll_sub(tu[0], -2)))
    chunk_ref[0] = h[0]
    chunk_ref[1] = rights[0]
    chunk_ref[2] = halo
    for i in range(3):
        st_ref[i] = start[i]


def tracer_kernel(info_ref, th_ref, t_ref, s_ref, u_ref, v_ref, d_ref, m_ref, g_ref, q_ref, r_ref, after_ref, nt_ref, ns_ref):
    del after_ref
    levels = t_ref.shape[0]
    edges = lon_masks(info_ref)
    depth = (d_ref[...] * m_ref[...]).astype(F32)
    depth_g = from_lat_group(g_ref[levels // 2], 0, 0)
    depth_h = lon_ghost(q_ref[levels], r_ref[levels], edges)
    low = [jnp.minimum(depth, n) for n in around(depth, depth_g, depth_h)]
    zero = jnp.zeros((8, 128), F32)

    def level(k, odd, j, carry):
        above_t, above_s = carry
        kf = floats(k) + 0.5
        below = jnp.minimum(k + 1, levels - 1)
        th, th_below = th_ref[k], th_ref[below]
        u, v, t, s = u_ref[k], v_ref[k], t_ref[k], s_ref[k]
        g, q_in, r_in = g_ref[j], q_ref[k], r_ref[k]
        u_h = lon_ghost(q_in, r_in, edges)
        t_h, s_h = lon_tracers(q_in, r_in, edges)
        v_g = from_lat_group(g, 1, odd)
        wet = depth > kf
        wet_below = (depth > kf + 1.0) & (k + 1 < levels)
        inv_space = 1.0 / jnp.full((8, 128), 0.5 * (th + th_below), F32)
        inv_th = MIXING / jnp.full((8, 128), th, F32)
        flow = [0.25 * x for x in (u + east(u, u_h), west(u, u_h) + u, v + north(v, v_g), south(v, v_g) + v)]
        masks = [x > kf for x in low]
        fluxes = []
        for q, q_g, q_h, full_ref, above, out_ref in (
            (t, from_lat_group(g, 2, odd), t_h, t_ref, above_t, nt_ref),
            (s, from_lat_group(g, 3, odd), s_h, s_ref, above_s, ns_ref),
        ):
            q_e, q_w, q_n, q_s = around(q, q_g, q_h)
            f_e = jnp.where(masks[0], flow[0] * (q + q_e) - DIFFUSION * (q_e - q), 0.0)
            f_w = jnp.where(masks[1], flow[1] * (q_w + q) - DIFFUSION * (q - q_w), 0.0)
            f_n = jnp.where(masks[2], flow[2] * (q + q_n) - DIFFUSION * (q_n - q), 0.0)
            f_s = jnp.where(masks[3], flow[3] * (q_s + q) - DIFFUSION * (q - q_s), 0.0)
            vflux = jnp.where(wet_below, (full_ref[below] - q) * inv_space, 0.0)
            vertical = (vflux - above) * inv_th
            out_ref[k] = jnp.where(wet, q + (f_w - f_e + f_s - f_n) + vertical, 0.0)
            fluxes.append(vflux)
        return tuple(fluxes)

    def step(i, carry):
        for j in range(TILES_PER_STEP):
            at = i * TILES_PER_STEP + j
            for odd in range(2):
                carry = level(2 * at + odd, odd, at, carry)
        return carry

    lax.fori_loop(0, levels // 2 // TILES_PER_STEP, step, (zero, zero))


def slab_kernel(levels, info_ref, own_ref, q_ref, r_ref, st_ref, sum_ref, surf_ref, slope_ref, we_s, wn_s, fac_s, inv_s, r_s, d_s, z_s):
    odd_group = jnp.full((GROUP, 128), info_ref[3] // GROUP % 2, jnp.int32) == 1

    def rows(i):
        own, q, r = (ref[pl.ds(i, GROUP, stride=24), :] for ref in (own_ref, q_ref, r_ref))
        return jnp.concatenate([jnp.where(odd_group, q, r), own, jnp.where(odd_group, r, q)], axis=0)

    here = GROUP + info_ref[3] % GROUP
    right, left = here + 1, here - 1
    heights, tu = [], [None] * 8
    for p in range(8):
        packed = rows(16 + p % 4)
        at = 64 * (p // 4)
        heights.append(jnp.concatenate([rows(p), roll_lane(packed, -8 - at)], axis=1))
        r_s[p] = jnp.concatenate([rows(8 + p), roll_lane(packed, -24 - at)], axis=1)
        if p in (0, 7):
            tu[p] = jnp.concatenate([rows(20 if p == 0 else 21), roll_lane(packed, -40 - at)], axis=1)
    r_s[0] = r_s[0] + jnp.where(heights[0] > 0.0, (0.5 * DIVERGENCE) * roll_sub(tu[7], 1), 0.0)
    r_s[7] = r_s[7] - jnp.where(heights[7] > 0.0, (0.5 * DIVERGENCE) * roll_sub(tu[0], -1), 0.0)
    for p in range(8):
        h = heights[p]
        h_e = heights[p + 1] if p < 7 else roll_sub(heights[0], -1)
        we_s[p] = jnp.minimum(h, h_e) * (1.0 / levels)
        wn_s[p] = jnp.minimum(h, roll_lane(h, -1)) * (1.0 / levels)
    for p in range(8):
        w_w = we_s[p - 1] if p > 0 else roll_sub(we_s[7], 1)
        wn = wn_s[p]
        diag = STORAGE + we_s[p] + w_w + wn + roll_lane(wn, 1)
        if p > 0:
            diag = diag + w_w * fac_s[p - 1]
        inv = 1.0 / diag
        inv_s[p] = inv
        fac_s[p] = -we_s[p] * inv

    mid = 0.5 * (SPECTRUM_HIGH + SPECTRUM_LOW)
    half = 0.5 * (SPECTRUM_HIGH - SPECTRUM_LOW)
    ratio = mid / half

    def residuals():
        d, last = d_s[0], d_s[7]
        edge = we_s[7] * (roll_sub(d, -1) - last)
        f_w = roll_sub(edge, 1)
        for p in range(8):
            d_e = d_s[p + 1] if p < 7 else None
            f_e = we_s[p] * (d_e - d) if p < 7 else edge
            f_n = wn_s[p] * (roll_lane(d, -1) - d)
            yield r_s[p] - STORAGE * d + ((f_e - f_w) + (f_n - roll_lane(f_n, 1)))
            f_w, d = f_e, d_e

    def step(scale_old, scale_new, first):
        y = []
        for p, r in enumerate((r_s[p] for p in range(8)) if first else residuals()):
            if not first:
                r_s[p] = r
            y.append((r + we_s[p - 1] * y[p - 1] if p > 0 else r) * inv_s[p])
        x = None
        for p in range(7, -1, -1):
            x = y[p] if x is None else y[p] - fac_s[p] * x
            d = x * scale_new if first else scale_old * d_s[p] + scale_new * x
            d_s[p] = d
            z_s[p] = d if first else z_s[p] + d

    step(0.0, 1.0 / mid, True)
    rho = 1.0 / ratio
    for _ in range(ITERS - 1):
        rho_next = 1.0 / (2.0 * ratio - rho)
        step(rho_next * rho, 2.0 * rho_next / half, False)
        rho = rho_next
    total = jnp.zeros((GROUP, 128), F32)
    for r in residuals():
        r = r[GROUP : 2 * GROUP, 0:128]
        total = total + r * r
    total = jnp.sum(jnp.sum(total, axis=0, keepdims=True), axis=1, keepdims=True) + jnp.zeros((1, 128), F32)
    for i in range(sum_ref.shape[0]):
        sum_ref[i] = total

    both = jnp.concatenate([z_s[p, pl.ds(here, 1), :] for p in range(8)], axis=0)
    x_e, x_w = z_s[0, pl.ds(right, 1), :], z_s[7, pl.ds(left, 1), :]
    x, x_g = both[:, 0:128], both[:, 128:256]
    sub = subs()
    x_e = jnp.broadcast_to(x_e[:, 0:128], (8, 128))
    x_w = jnp.broadcast_to(x_w[:, 0:128], (8, 128))
    x_h = jnp.where(sub < 4, x_e, x_w)
    x, x_g, x_h = x + st_ref[0], x_g + st_ref[1], x_h + st_ref[2]
    e, w, n, s = around(x, x_g, x_h)
    surf_ref[...] = x
    slope_ref[0] = (0.5 * GRAVITY) * (e - w)
    slope_ref[1] = (0.5 * GRAVITY) * (n - s)


def velocity_kernel(us_ref, vs_ref, d_ref, m_ref, slope_ref, nu_ref, nv_ref):
    depth = (d_ref[...] * m_ref[...]).astype(F32)
    slope_x, slope_y = slope_ref[0], slope_ref[1]
    for k in range(us_ref.shape[0]):
        wet = depth > k + 0.5
        nu_ref[k] = jnp.where(wet, us_ref[k] - slope_x, 0.0)
        nv_ref[k] = jnp.where(wet, vs_ref[k] - slope_y, 0.0)


def call(kernel, name, outs, in_specs, scratch=(), aliases=None):
    return pl.pallas_call(
        kernel,
        name=name,
        out_shape=outs,
        in_specs=in_specs,
        out_specs=jax.tree.map(lambda _: VMEM, outs),
        scratch_shapes=list(scratch),
        input_output_aliases=aliases or {},
        compiler_params=pltpu.CompilerParams(vmem_limit_bytes=48 << 20),
    )


def from_all(x, axes):
    size = 1
    for axis in axes:
        size *= lax.axis_size(axis)
    copies = jnp.broadcast_to(x[None], (size, *x.shape))
    return lax.all_to_all(copies, axes, 0, 0, tiled=True)


def per_device(lon_size, lat_size, temp, salt, u, v, strata, sea, thickness, elevation, drive):
    levels = temp.shape[0]
    lon, lat = lax.axis_index(LON), lax.axis_index("lat")
    top = lat_size - 1
    info = jnp.stack(
        [1 - lat % 2, (lat == top).astype(jnp.int32), lat, lon, jnp.int32(lat_size), jnp.int32(levels)]
    ).astype(jnp.int32)
    pairs_a = [(i, i ^ 1) for i in range(lat_size)]
    pairs_b = []
    for a in range(lon_size):
        for i in range(1, top, 2):
            pairs_b += [(a * lat_size + i, a * lat_size + i + 1), (a * lat_size + i + 1, a * lat_size + i)]
        pairs_b.append((a * lat_size + top, (lon_size - 1 - a) * lat_size + top))

    def lat_swap(x):
        return lax.ppermute(x, "lat", pairs_a), lax.ppermute(x, (*LON, "lat"), pairs_b)

    def tiles(n, kind=F32):
        return jax.ShapeDtypeStruct((n, 8, 128), kind)

    field, flat = tiles(levels), (8, 128)
    message, packed = tiles(levels + 2), tiles(levels // 2 + 1)
    own = (temp, salt, u, v, strata, sea, elevation, drive)

    edges = call(
        lat_pack_kernel,
        "lat_pack",
        packed,
        [pl.BlockSpec(memory_space=pltpu.HBM)] * 8,
        [pltpu.VMEM(field.shape, F32)] * 4
        + [pltpu.VMEM(flat, jnp.int32)] * 2
        + [pltpu.VMEM(flat, F32)] * 2
        + [pltpu.SemaphoreType.DMA((3, 4))],
    )(*[pltpu.with_memory_space_constraint(x, pltpu.HBM) for x in own])
    got_a, got_b = lat_swap(edges)
    rows_q, rows_r = call(lon_rows_kernel, "lon_rows", (message, message), [SMEM] + [VMEM] * 8)(info, *own)
    ghost, pair_r, pair_q = call(
        corners_kernel, "corners", (packed, message, message), [SMEM] + [VMEM] * 4, aliases={3: 1, 4: 2}
    )(info, got_a, got_b, rows_r, rows_q)
    pair_r = lax.ppermute(pair_r, LON, [(i, (i + 1 if i % 2 else i - 1) % lon_size) for i in range(lon_size)])
    pair_q = lax.ppermute(pair_q, LON, [(i, i ^ 1) for i in range(lon_size)])
    u_star, v_star, chunk, start = call(
        momentum_kernel, "momentum", (field, field, tiles(3), tiles(3)), [SMEM, SMEM] + [VMEM] * 11
    )(info, thickness, *own, ghost, pair_r, pair_q)
    group = from_all(chunk, ("lon_lo",)).reshape(GROUP * 24, 128)
    group, after = lax.optimization_barrier((group, chunk))
    groups = lon_size // GROUP
    group_q = lax.ppermute(group, "lon_hi", [(i, i ^ 1) for i in range(groups)])
    group_r = lax.ppermute(group, "lon_hi", [(i, (i + 1 if i % 2 else i - 1) % groups) for i in range(groups)])
    new_temp, new_salt = call(tracer_kernel, "tracers", (field, field), [SMEM] * 2 + [VMEM] * 10)(
        info, thickness, temp, salt, u, v, strata, sea, ghost, pair_q, pair_r, after
    )
    group_q, group_r, new_temp, new_salt = lax.optimization_barrier((group_q, group_r, new_temp, new_salt))
    sums, surface, slope = call(
        functools.partial(slab_kernel, levels),
        "slab",
        (jax.ShapeDtypeStruct((groups * lat_size, 1, 128), F32), jax.ShapeDtypeStruct((8, 128), F32), tiles(2)),
        [SMEM] + [VMEM] * 4,
        [pltpu.VMEM((8, 3 * GROUP, 256), F32)] * 7,
    )(info, group, group_q, group_r, start)
    sums = lax.all_to_all(sums, ("lon_hi", "lat"), 0, 0, tiled=True)
    total = jnp.sum(sums, axis=0)
    cells = lon_size * 8 * lat_size * 128
    rms = jnp.sqrt(total[0, 0] / cells + EPSILON)
    new_u, new_v = call(velocity_kernel, "velocity", (field, field), [VMEM] * 5)(u_star, v_star, strata, sea, slope)
    return (new_temp, new_salt, new_u, new_v, surface, rms)


def solution(mesh):
    lon_size, lat_size = mesh.shape["lon"], mesh.shape["lat"]
    finer = Mesh(mesh.devices.reshape(lon_size // GROUP, GROUP, lat_size), (*LON, "lat"))
    cube, flat = P(None, LON, "lat"), P(LON, "lat")
    return jax.shard_map(
        functools.partial(per_device, lon_size, lat_size),
        mesh=finer,
        in_specs=(cube, cube, cube, cube, flat, flat, P(), flat, flat),
        out_specs=(cube, cube, cube, cube, flat, P()),
        check_vma=False,
    )
```

```python
import functools

import jax
import jax.numpy as jnp
from jax import lax
from jax.experimental import pallas as pl
from jax.experimental.pallas import tpu as pltpu
from jax.sharding import Mesh
from jax.sharding import PartitionSpec as P

DIFFUSION = 0.15
MIXING = 0.1
EXPANSION = 0.2
CONTRACTION = 0.15
PRESSURE_SCALE = 0.02
CORIOLIS = 0.5
FRICTION = 0.01
DIVERGENCE = 0.3
STORAGE = 0.1
SPECTRUM_LOW = 0.1
SPECTRUM_HIGH = 1.9
GRAVITY = 0.3
EPSILON = 1e-06
ITERS = 4
TILES_PER_STEP = 4
GROUP = 8
LON = ("lon_hi", "lon_lo")
F32 = jnp.float32

VMEM = pl.BlockSpec(memory_space=pltpu.VMEM)


def place():
    return lax.axis_index(LON[0]) * GROUP + lax.axis_index(LON[1]), lax.axis_index("lat")


def lanes(shape=(8, 128)):
    return lax.broadcasted_iota(jnp.int32, shape, 1)


def subs(shape=(8, 128)):
    return lax.broadcasted_iota(jnp.int32, shape, 0)


def roll_lane(x, shift):
    return pltpu.roll(x, shift % x.shape[1], 1)


def roll_sub(x, shift):
    return pltpu.roll(x, shift % x.shape[0], 0)


def north(x, ghost):
    return roll_lane(jnp.where(lanes() == 0, ghost, x), -1)


def south(x, ghost):
    return roll_lane(jnp.where(lanes() == 127, ghost, x), 1)


def east(x, ghost):
    return roll_sub(jnp.where(subs() == 0, ghost, x), -1)


def west(x, ghost):
    return roll_sub(jnp.where(subs() == 7, ghost, x), 1)


def around(x, lat_ghost, lon_ghost):
    return (east(x, lon_ghost), west(x, lon_ghost), north(x, lat_ghost), south(x, lat_ghost))


def one_of(index, values):
    found = index == values[0]
    for value in values[1:]:
        found = found | (index == value)
    return found


def lat_field(x, f, odd):
    return roll_lane(x, 16 * f + 8 + 64 * odd)


def from_lat_group(x, f, odd):
    return roll_lane(x, -(16 * f + 8 + 64 * odd))


def group_of(lane):
    return lane // 16


def lat_pack_kernel(t_hbm, s_hbm, u_hbm, v_hbm, d_hbm, m_hbm, z_hbm, f_hbm, out_ref, t_ref, s_ref, u_ref, v_ref, d_ref, m_ref, z_ref, f_ref, sem):
    levels = t_ref.shape[0]
    half = levels // 2
    fields = ((t_hbm, t_ref), (s_hbm, s_ref), (u_hbm, u_ref), (v_hbm, v_ref))
    parts = [[(src.at[i : i + half], dst.at[i : i + half]) for src, dst in fields] for i in (0, half)]
    parts.append([(d_hbm, d_ref), (m_hbm, m_ref), (z_hbm, z_ref), (f_hbm, f_ref)])
    copies = [[pltpu.make_async_copy(*p, sem.at[i, j]) for j, p in enumerate(part)] for i, part in enumerate(parts)]
    for part in copies:
        for copy in part:
            copy.start()
    group = group_of(lanes())

    def put(out, fields, odd):
        for f, x in enumerate(fields):
            out = jnp.where(group == f + 4 * odd, lat_field(x, f, odd), out)
        return out

    zero = jnp.zeros((8, 128), F32)
    for j in range(levels // 2):
        if j % (half // 2) == 0:
            for copy in copies[j // (half // 2)]:
                copy.wait()
        out = zero
        for odd in range(2):
            k = 2 * j + odd
            out = put(out, (u_ref[k], v_ref[k], t_ref[k], s_ref[k]), odd)
        out_ref[j] = out
    for copy in copies[2]:
        copy.wait()
    sea = m_ref[...].astype(F32)
    depth = (d_ref[...] * m_ref[...]).astype(F32)
    out_ref[levels // 2] = put(zero, (depth, sea * z_ref[...], sea * f_ref[...]), 0)


def lon_rows_kernel(t_ref, s_ref, u_ref, v_ref, d_ref, m_ref, z_ref, f_ref, q_ref, r_ref):
    levels = t_ref.shape[0]
    sub = subs()
    odd_lon = jnp.full((8, 128), place()[0] % 2, jnp.int32) == 1

    def put(k, u, v, t, s):
        v4, t2, s6 = roll_sub(v, 4), roll_sub(t, 2), roll_sub(s, 6)
        x = jnp.where((sub >= 4) & (sub <= 5), v4, u)
        x = jnp.where(sub == 2, t2, x)
        to_west = jnp.where(sub == 6, s6, x)
        x = jnp.where((sub >= 2) & (sub <= 3), v4, u)
        x = jnp.where(sub == 1, t2, x)
        to_east = jnp.where(sub == 5, s6, x)
        q_ref[k] = jnp.where(odd_lon, to_west, to_east)
        r_ref[k] = jnp.where(odd_lon, to_east, to_west)

    for k in range(levels):
        put(k, u_ref[k], v_ref[k], t_ref[k], s_ref[k])
    sea = m_ref[...].astype(F32)
    depth, start = (d_ref[...] * m_ref[...]).astype(F32), sea * z_ref[...]
    put(levels, depth, start, sea * f_ref[...], start)
    put(levels + 1, depth, start, start, start)


def turn_rows(x):
    sub = subs()
    x = roll_sub(x, 4)
    x = jnp.where(sub // 2 % 2 == 0, roll_sub(x, -2), roll_sub(x, 2))
    return jnp.where(sub % 2 == 0, roll_sub(x, -1), roll_sub(x, 1))


def corners_kernel(top, a_ref, b_ref, r_in, q_in, g_ref, r_ref, q_ref):
    del q_in, r_in
    count = a_ref.shape[0]
    lane = lanes()
    lon, lat = place()
    is_even, odd_lon = 1 - lat % 2, lon % 2
    from_north = lane % 16 >= 8
    flow_sign = jnp.where(group_of(lane) % 4 < 2, -1.0, 1.0).astype(F32)

    sub = subs()
    odd_block = jnp.full((8, 128), odd_lon, jnp.int32) == 1
    west_row, east_row = sub == 3, sub == 0
    in_q = (west_row & odd_block) | (east_row & ~odd_block)
    in_r = (east_row & odd_block) | (west_row & ~odd_block)

    def put(j, g):
        g_ref[j] = g
        for odd in range(2):
            rows = jnp.where(west_row, roll_sub(g, 3 - odd), roll_sub(g, 1 + odd))
            k = 2 * j + odd
            q_ref[k] = jnp.where(in_q, rows, q_ref[k])
            r_ref[k] = jnp.where(in_r, rows, r_ref[k])

    @pl.when(lat != top)
    def _():
        from_a = from_north == (jnp.full((8, 128), is_even, jnp.int32) == 1)
        for j in range(count):
            put(j, jnp.where(from_a, a_ref[j], b_ref[j]))

    @pl.when(lat == top)
    def _():
        for j in range(count):
            rows = turn_rows(b_ref[j])
            turned = roll_lane(rows, 1)
            for i in range(1, 7):
                turned = jnp.where(lane % 16 == 8 + i, roll_lane(rows, 1 + 2 * i), turned)
            if j < count - 1:
                turned = turned * flow_sign
            put(j, jnp.where(from_north, turned, a_ref[j]))


def lon_masks():
    sub = subs()
    odd_lon = jnp.full((8, 128), place()[0] % 2, jnp.int32) == 1
    return [x != odd_lon for x in (one_of(sub, (0, 1, 4, 5)), sub == 2, sub == 6, sub == 3)]


def lon_ghost(q, r, masks):
    return jnp.where(masks[0], q, r)


def lon_tracers(q, r, masks):
    return roll_sub(jnp.where(masks[1], q, r), -2), roll_sub(jnp.where(masks[2], q, r), -6)


def corner_group(q_ref, r_ref, j, masks):
    sub = subs()
    x = jnp.where(masks[3], q_ref[2 * j], r_ref[2 * j])
    y = jnp.where(masks[3], q_ref[2 * j + 1], r_ref[2 * j + 1])
    return jnp.where(sub == 0, roll_sub(x, -3), jnp.where(sub == 7, roll_sub(x, -1), roll_sub(y, -2)))


LAT_PARTNER = (1, 0, 3, 2)
LON_PARTNER = (2, 3, 0, 1)


def ext_east(x):
    return [east(x[i], x[LON_PARTNER[i]]) for i in range(len(x))]


def ext_north(x):
    return [north(x[i], x[LAT_PARTNER[i]]) for i in range(len(x))]


def lap(x, mask_e, mask_n, tiles):
    f_e = [jnp.where(m, y - c, 0.0) for m, y, c in zip(mask_e, ext_east(x), x)]
    f_n = [jnp.where(m, y - c, 0.0) for m, y, c in zip(mask_n, ext_north(x), x)]
    out = []
    for i in tiles:
        out.append(f_e[i] - west(f_e[i], f_e[LON_PARTNER[i]]) + (f_n[i] - south(f_n[i], f_n[LAT_PARTNER[i]])))
    return out


def floats(i):
    return i.astype(F32)


def momentum_kernel(
    lat_size, th_ref, t_ref, s_ref, u_ref, v_ref, d_ref, m_ref, z_ref, f_ref, g_ref, r_ref, q_ref, us_ref, vs_ref, chunk_ref, st_ref
):
    levels = t_ref.shape[0]
    lane, sub = lanes(), subs()
    edges = lon_masks()
    last = levels // 2
    sea = m_ref[...].astype(F32)
    corner = corner_group(q_ref, r_ref, last, edges)
    edge = lon_ghost(q_ref[levels], r_ref[levels], edges)
    depth = [(d_ref[...] * m_ref[...]).astype(F32), from_lat_group(g_ref[last], 0, 0), edge, from_lat_group(corner, 0, 0)]
    low_e = [jnp.minimum(x, y) for x, y in zip(depth, ext_east(depth))]
    low_n = [jnp.minimum(x, y) for x, y in zip(depth, ext_north(depth))]
    lat_index = (lane + place()[1] * 128).astype(F32)
    ghost_index = lat_index + jnp.where(lane < 64, 128.0, -128.0)
    lats = 128.0 * lat_size
    ghost_index = jnp.where(ghost_index >= lats, 2.0 * lats - 1.0 - ghost_index, ghost_index)
    coriolis = [CORIOLIS * (2.0 * (x + 0.5) / lats - 1.0) for x in (lat_index, ghost_index)]
    zero = jnp.zeros((8, 128), F32)
    both = (0, 1)

    def level(k, odd, j, corners, carry):
        p, h, tu, tv = carry
        th = th_ref[k]
        kf = floats(k) + 0.5
        g, q_in, r_in = g_ref[j], q_ref[k], r_ref[k]
        u_h = lon_ghost(q_in, r_in, edges)
        t_h, s_h = lon_tracers(q_in, r_in, edges)
        u = [u_ref[k], from_lat_group(g, 0, odd), u_h, from_lat_group(corners, 0, odd)]
        v = [v_ref[k], from_lat_group(g, 1, odd), roll_sub(u_h, 4), from_lat_group(corners, 1, odd)]
        t = [t_ref[k], from_lat_group(g, 2, odd), t_h, from_lat_group(corners, 2, odd)]
        s = [s_ref[k], from_lat_group(g, 3, odd), s_h, from_lat_group(corners, 3, odd)]
        mask_e, mask_n, wet = [[x > kf for x in xs] for xs in (low_e, low_n, depth)]
        drag_u = lap(lap(u, mask_e, mask_n, range(4)), mask_e, mask_n, both)
        drag_v = lap(lap(v, mask_e, mask_n, range(4)), mask_e, mask_n, both)
        p = [c + jnp.where(m, (CONTRACTION * b - EXPANSION * a) * th, 0.0) for c, m, a, b in zip(p, wet, t, s)]
        h = [c + jnp.where(m, th, 0.0) for c, m in zip(h, wet)]
        f_e = [jnp.where(m, y - c, 0.0) for m, y, c in zip(mask_e, ext_east(p), p)]
        f_n = [jnp.where(m, y - c, 0.0) for m, y, c in zip(mask_n, ext_north(p), p)]
        us, vs = [], []
        for i in both:
            grad_x = f_e[i] + west(f_e[i], f_e[LON_PARTNER[i]])
            grad_y = f_n[i] + south(f_n[i], f_n[LAT_PARTNER[i]])
            x = u[i] + coriolis[i] * v[i] - (0.5 * PRESSURE_SCALE) * grad_x - FRICTION * drag_u[i]
            y = v[i] - coriolis[i] * u[i] - (0.5 * PRESSURE_SCALE) * grad_y - FRICTION * drag_v[i]
            us.append(jnp.where(wet[i], x, 0.0))
            vs.append(jnp.where(wet[i], y, 0.0))
        us_ref[k] = us[0]
        vs_ref[k] = vs[0]
        return (p, h, [a + th * b for a, b in zip(tu, us)], [a + th * b for a, b in zip(tv, vs)])

    def step(i, carry):
        for j in range(TILES_PER_STEP):
            at = i * TILES_PER_STEP + j
            corners = corner_group(q_ref, r_ref, at, edges)
            for odd in range(2):
                carry = level(2 * at + odd, odd, at, corners, carry)
        return carry

    _, h, tu, tv = lax.fori_loop(0, last // TILES_PER_STEP, step, ([zero] * 4, [zero] * 4, [zero] * 2, [zero] * 2))
    start = [sea * z_ref[...], from_lat_group(g_ref[last], 1, 0), roll_sub(edge, 4), from_lat_group(corner, 1, 0)]
    drive = [sea * f_ref[...], from_lat_group(g_ref[last], 2, 0)]
    weight_e = [jnp.minimum(x, y) * (1.0 / levels) for x, y in zip(h, ext_east(h))]
    weight_n = [jnp.minimum(x, y) * (1.0 / levels) for x, y in zip(h, ext_north(h))]
    flux_e = [x * (y - c) for x, y, c in zip(weight_e, ext_east(start), start)]
    flux_n = [x * (y - c) for x, y, c in zip(weight_n, ext_north(start), start)]
    rights = []
    for i in both:
        spread = flux_e[i] - west(flux_e[i], flux_e[LON_PARTNER[i]]) + (flux_n[i] - south(flux_n[i], flux_n[LAT_PARTNER[i]]))
        base = drive[i] - (STORAGE * start[i] - spread)
        tu_e = jnp.where(sub == 7, 0.0, roll_sub(tu[i], -1))
        tu_w = jnp.where(sub == 0, 0.0, roll_sub(tu[i], 1))
        tv_n, tv_s = north(tv[i], tv[1 - i]), south(tv[i], tv[1 - i])
        rights.append(base - jnp.where(h[i] > 0.0, (0.5 * DIVERGENCE) * ((tu_e - tu_w) + (tv_n - tv_s)), 0.0))
    halo = jnp.where(lane < 16, roll_lane(h[1], 8), jnp.where(lane < 32, roll_lane(rights[1], 24), roll_lane(tu[1], 40)))
    halo = jnp.where(lane < 64, halo, roll_lane(roll_sub(halo, 4), 64))
    halo = jnp.where(sub < 4, halo, jnp.where(sub == 4, roll_sub(tu[0], 4), roll_sub(tu[0], -2)))
    chunk_ref[0] = h[0]
    chunk_ref[1] = rights[0]
    chunk_ref[2] = halo
    for i in range(3):
        st_ref[i] = start[i]


def tracer_kernel(th_ref, t_ref, s_ref, u_ref, v_ref, d_ref, m_ref, g_ref, q_ref, r_ref, after_ref, nt_ref, ns_ref):
    del after_ref
    levels = t_ref.shape[0]
    edges = lon_masks()
    depth = (d_ref[...] * m_ref[...]).astype(F32)
    depth_g = from_lat_group(g_ref[levels // 2], 0, 0)
    depth_h = lon_ghost(q_ref[levels], r_ref[levels], edges)
    low = [jnp.minimum(depth, n) for n in around(depth, depth_g, depth_h)]
    zero = jnp.zeros((8, 128), F32)

    def level(k, odd, j, carry):
        above_t, above_s = carry
        kf = floats(k) + 0.5
        below = jnp.minimum(k + 1, levels - 1)
        th, th_below = th_ref[k], th_ref[below]
        u, v, t, s = u_ref[k], v_ref[k], t_ref[k], s_ref[k]
        g, q_in, r_in = g_ref[j], q_ref[k], r_ref[k]
        u_h = lon_ghost(q_in, r_in, edges)
        t_h, s_h = lon_tracers(q_in, r_in, edges)
        v_g = from_lat_group(g, 1, odd)
        wet = depth > kf
        wet_below = (depth > kf + 1.0) & (k + 1 < levels)
        inv_space = 1.0 / (0.5 * (th + th_below))
        inv_th = MIXING / th
        flow = [0.25 * x for x in (u + east(u, u_h), west(u, u_h) + u, v + north(v, v_g), south(v, v_g) + v)]
        masks = [x > kf for x in low]
        fluxes = []
        for q, q_g, q_h, full_ref, above, out_ref in (
            (t, from_lat_group(g, 2, odd), t_h, t_ref, above_t, nt_ref),
            (s, from_lat_group(g, 3, odd), s_h, s_ref, above_s, ns_ref),
        ):
            q_e, q_w, q_n, q_s = around(q, q_g, q_h)
            f_e = jnp.where(masks[0], flow[0] * (q + q_e) - DIFFUSION * (q_e - q), 0.0)
            f_w = jnp.where(masks[1], flow[1] * (q_w + q) - DIFFUSION * (q - q_w), 0.0)
            f_n = jnp.where(masks[2], flow[2] * (q + q_n) - DIFFUSION * (q_n - q), 0.0)
            f_s = jnp.where(masks[3], flow[3] * (q_s + q) - DIFFUSION * (q - q_s), 0.0)
            vflux = jnp.where(wet_below, (full_ref[below] - q) * inv_space, 0.0)
            vertical = (vflux - above) * inv_th
            out_ref[k] = jnp.where(wet, q + (f_w - f_e + f_s - f_n) + vertical, 0.0)
            fluxes.append(vflux)
        return tuple(fluxes)

    def step(i, carry):
        for j in range(TILES_PER_STEP):
            at = i * TILES_PER_STEP + j
            for odd in range(2):
                carry = level(2 * at + odd, odd, at, carry)
        return carry

    lax.fori_loop(0, levels // 2 // TILES_PER_STEP, step, (zero, zero))


def slab_kernel(levels, own_ref, q_ref, r_ref, st_ref, sum_ref, surf_ref, slope_ref, we_s, wn_s, fac_s, inv_s, r_s, d_s, z_s):
    odd_group = jnp.full((GROUP, 128), lax.axis_index(LON[0]) % 2, jnp.int32) == 1

    def rows(i):
        own, q, r = (ref[pl.ds(i, GROUP, stride=24), :] for ref in (own_ref, q_ref, r_ref))
        return jnp.concatenate([jnp.where(odd_group, q, r), own, jnp.where(odd_group, r, q)], axis=0)

    here = GROUP + lax.axis_index(LON[1])
    right, left = here + 1, here - 1
    heights, tu = [], [None] * 8
    for p in range(8):
        packed = rows(16 + p % 4)
        at = 64 * (p // 4)
        heights.append(jnp.concatenate([rows(p), roll_lane(packed, -8 - at)], axis=1))
        r_s[p] = jnp.concatenate([rows(8 + p), roll_lane(packed, -24 - at)], axis=1)
        if p in (0, 7):
            tu[p] = jnp.concatenate([rows(20 if p == 0 else 21), roll_lane(packed, -40 - at)], axis=1)
    r_s[0] = r_s[0] + jnp.where(heights[0] > 0.0, (0.5 * DIVERGENCE) * roll_sub(tu[7], 1), 0.0)
    r_s[7] = r_s[7] - jnp.where(heights[7] > 0.0, (0.5 * DIVERGENCE) * roll_sub(tu[0], -1), 0.0)
    for p in range(8):
        h = heights[p]
        h_e = heights[p + 1] if p < 7 else roll_sub(heights[0], -1)
        we_s[p] = jnp.minimum(h, h_e) * (1.0 / levels)
        wn_s[p] = jnp.minimum(h, roll_lane(h, -1)) * (1.0 / levels)
    for p in range(8):
        w_w = we_s[p - 1] if p > 0 else roll_sub(we_s[7], 1)
        wn = wn_s[p]
        diag = STORAGE + we_s[p] + w_w + wn + roll_lane(wn, 1)
        if p > 0:
            diag = diag + w_w * fac_s[p - 1]
        inv = 1.0 / diag
        inv_s[p] = inv
        fac_s[p] = -we_s[p] * inv

    mid = 0.5 * (SPECTRUM_HIGH + SPECTRUM_LOW)
    half = 0.5 * (SPECTRUM_HIGH - SPECTRUM_LOW)
    ratio = mid / half

    def residuals():
        d, last = d_s[0], d_s[7]
        edge = we_s[7] * (roll_sub(d, -1) - last)
        f_w = roll_sub(edge, 1)
        for p in range(8):
            d_e = d_s[p + 1] if p < 7 else None
            f_e = we_s[p] * (d_e - d) if p < 7 else edge
            f_n = wn_s[p] * (roll_lane(d, -1) - d)
            yield r_s[p] - STORAGE * d + ((f_e - f_w) + (f_n - roll_lane(f_n, 1)))
            f_w, d = f_e, d_e

    def step(scale_old, scale_new, first):
        y = []
        for p, r in enumerate((r_s[p] for p in range(8)) if first else residuals()):
            if not first:
                r_s[p] = r
            y.append((r + we_s[p - 1] * y[p - 1] if p > 0 else r) * inv_s[p])
        x = None
        for p in range(7, -1, -1):
            x = y[p] if x is None else y[p] - fac_s[p] * x
            d = x * scale_new if first else scale_old * d_s[p] + scale_new * x
            d_s[p] = d
            z_s[p] = d if first else z_s[p] + d

    step(0.0, 1.0 / mid, True)
    rho = 1.0 / ratio
    for _ in range(ITERS - 1):
        rho_next = 1.0 / (2.0 * ratio - rho)
        step(rho_next * rho, 2.0 * rho_next / half, False)
        rho = rho_next
    total = jnp.zeros((GROUP, 128), F32)
    for r in residuals():
        r = r[GROUP : 2 * GROUP, 0:128]
        total = total + r * r
    total = jnp.sum(jnp.sum(total, axis=0, keepdims=True), axis=1, keepdims=True) + jnp.zeros((1, 128), F32)
    for i in range(sum_ref.shape[0]):
        sum_ref[i] = total

    both = jnp.concatenate([z_s[p, pl.ds(here, 1), :] for p in range(8)], axis=0)
    x_e, x_w = z_s[0, pl.ds(right, 1), :], z_s[7, pl.ds(left, 1), :]
    x, x_g = both[:, 0:128], both[:, 128:256]
    sub = subs()
    x_e = jnp.broadcast_to(x_e[:, 0:128], (8, 128))
    x_w = jnp.broadcast_to(x_w[:, 0:128], (8, 128))
    x_h = jnp.where(sub < 4, x_e, x_w)
    x, x_g, x_h = x + st_ref[0], x_g + st_ref[1], x_h + st_ref[2]
    e, w, n, s = around(x, x_g, x_h)
    surf_ref[...] = x
    slope_ref[0] = (0.5 * GRAVITY) * (e - w)
    slope_ref[1] = (0.5 * GRAVITY) * (n - s)


def velocity_kernel(us_ref, vs_ref, d_ref, m_ref, slope_ref, nu_ref, nv_ref):
    depth = (d_ref[...] * m_ref[...]).astype(F32)
    slope_x, slope_y = slope_ref[0], slope_ref[1]
    for k in range(us_ref.shape[0]):
        wet = depth > k + 0.5
        nu_ref[k] = jnp.where(wet, us_ref[k] - slope_x, 0.0)
        nv_ref[k] = jnp.where(wet, vs_ref[k] - slope_y, 0.0)


def call(kernel, name, outs, in_specs, scratch=(), aliases=None):
    return pl.pallas_call(
        kernel,
        name=name,
        out_shape=outs,
        in_specs=in_specs,
        out_specs=jax.tree.map(lambda _: VMEM, outs),
        scratch_shapes=list(scratch),
        input_output_aliases=aliases or {},
        compiler_params=pltpu.CompilerParams(vmem_limit_bytes=48 << 20),
    )


def from_all(x, axes):
    size = 1
    for axis in axes:
        size *= lax.axis_size(axis)
    copies = jnp.broadcast_to(x[None], (size, *x.shape))
    return lax.all_to_all(copies, axes, 0, 0, tiled=True)


def per_device(lon_size, lat_size, temp, salt, u, v, strata, sea, thickness, elevation, drive):
    levels = temp.shape[0]
    top = lat_size - 1
    pairs_a = [(i, i ^ 1) for i in range(lat_size)]
    pairs_b = []
    for a in range(lon_size):
        for i in range(1, top, 2):
            pairs_b += [(a * lat_size + i, a * lat_size + i + 1), (a * lat_size + i + 1, a * lat_size + i)]
        pairs_b.append((a * lat_size + top, (lon_size - 1 - a) * lat_size + top))

    def lat_swap(x):
        return lax.ppermute(x, "lat", pairs_a), lax.ppermute(x, (*LON, "lat"), pairs_b)

    def tiles(n, kind=F32):
        return jax.ShapeDtypeStruct((n, 8, 128), kind)

    field, flat = tiles(levels), (8, 128)
    message, packed = tiles(levels + 2), tiles(levels // 2 + 1)
    own = (temp, salt, u, v, strata, sea, elevation, drive)

    edges = call(
        lat_pack_kernel,
        "lat_pack",
        packed,
        [pl.BlockSpec(memory_space=pltpu.HBM)] * 8,
        [pltpu.VMEM(field.shape, F32)] * 4
        + [pltpu.VMEM(flat, jnp.int32)] * 2
        + [pltpu.VMEM(flat, F32)] * 2
        + [pltpu.SemaphoreType.DMA((3, 4))],
    )(*[pltpu.with_memory_space_constraint(x, pltpu.HBM) for x in own])
    got_a, got_b = lat_swap(edges)
    thick = jnp.broadcast_to(thickness[:, None, None], field.shape)
    rows_q, rows_r = call(lon_rows_kernel, "lon_rows", (message, message), [VMEM] * 8)(*own)
    corners = functools.partial(corners_kernel, top)
    ghost, pair_r, pair_q = call(corners, "corners", (packed, message, message), [VMEM] * 4, aliases={2: 1, 3: 2})(
        got_a, got_b, rows_r, rows_q
    )
    pair_r = lax.ppermute(pair_r, LON, [(i, (i + 1 if i % 2 else i - 1) % lon_size) for i in range(lon_size)])
    pair_q = lax.ppermute(pair_q, LON, [(i, i ^ 1) for i in range(lon_size)])
    u_star, v_star, chunk, start = call(
        functools.partial(momentum_kernel, lat_size), "momentum", (field, field, tiles(3), tiles(3)), [VMEM] * 12
    )(thick, *own, ghost, pair_r, pair_q)
    group = from_all(chunk, ("lon_lo",)).reshape(GROUP * 24, 128)
    group, after = lax.optimization_barrier((group, chunk))
    groups = lon_size // GROUP
    group_q = lax.ppermute(group, "lon_hi", [(i, i ^ 1) for i in range(groups)])
    group_r = lax.ppermute(group, "lon_hi", [(i, (i + 1 if i % 2 else i - 1) % groups) for i in range(groups)])
    new_temp, new_salt = call(tracer_kernel, "tracers", (field, field), [VMEM] * 11)(
        thick, temp, salt, u, v, strata, sea, ghost, pair_q, pair_r, after
    )
    group_q, group_r, new_temp, new_salt = lax.optimization_barrier((group_q, group_r, new_temp, new_salt))
    sums, surface, slope = call(
        functools.partial(slab_kernel, levels),
        "slab",
        (jax.ShapeDtypeStruct((groups * lat_size, 1, 128), F32), jax.ShapeDtypeStruct((8, 128), F32), tiles(2)),
        [VMEM] * 4,
        [pltpu.VMEM((8, 3 * GROUP, 256), F32)] * 7,
    )(group, group_q, group_r, start)
    sums = lax.all_to_all(sums, ("lon_hi", "lat"), 0, 0, tiled=True)
    total = jnp.sum(sums, axis=0)
    cells = lon_size * 8 * lat_size * 128
    rms = jnp.sqrt(total[0, 0] / cells + EPSILON)
    new_u, new_v = call(velocity_kernel, "velocity", (field, field), [VMEM] * 5)(u_star, v_star, strata, sea, slope)
    return (new_temp, new_salt, new_u, new_v, surface, rms)


def solution(mesh):
    lon_size, lat_size = mesh.shape["lon"], mesh.shape["lat"]
    finer = Mesh(mesh.devices.reshape(lon_size // GROUP, GROUP, lat_size), (*LON, "lat"))
    cube, flat = P(None, LON, "lat"), P(LON, "lat")
    return jax.shard_map(
        functools.partial(per_device, lon_size, lat_size),
        mesh=finer,
        in_specs=(cube, cube, cube, cube, flat, flat, P(), flat, flat),
        out_specs=(cube, cube, cube, cube, flat, P()),
        check_vma=False,
    )
```

```python
import functools

import jax
import jax.numpy as jnp
from jax import lax
from jax.experimental import pallas as pl
from jax.experimental.pallas import tpu as pltpu
from jax.sharding import Mesh
from jax.sharding import PartitionSpec as P

DIFFUSION = 0.15
MIXING = 0.1
EXPANSION = 0.2
CONTRACTION = 0.15
PRESSURE_SCALE = 0.02
CORIOLIS = 0.5
FRICTION = 0.01
DIVERGENCE = 0.3
STORAGE = 0.1
SPECTRUM_LOW = 0.1
SPECTRUM_HIGH = 1.9
GRAVITY = 0.3
EPSILON = 1e-06
ITERS = 4
TILES_PER_STEP = 4
GROUP = 8
LON = ("lon_hi", "lon_lo")
F32 = jnp.float32

VMEM = pl.BlockSpec(memory_space=pltpu.VMEM)


def place():
    return lax.axis_index(LON[0]) * GROUP + lax.axis_index(LON[1]), lax.axis_index("lat")


def lanes(shape=(8, 128)):
    return lax.broadcasted_iota(jnp.int32, shape, 1)


def subs(shape=(8, 128)):
    return lax.broadcasted_iota(jnp.int32, shape, 0)


def roll_lane(x, shift):
    return pltpu.roll(x, shift % x.shape[1], 1)


def roll_sub(x, shift):
    return pltpu.roll(x, shift % x.shape[0], 0)


def north(x, ghost):
    return roll_lane(jnp.where(lanes() == 0, ghost, x), -1)


def south(x, ghost):
    return roll_lane(jnp.where(lanes() == 127, ghost, x), 1)


def east(x, ghost):
    return roll_sub(jnp.where(subs() == 0, ghost, x), -1)


def west(x, ghost):
    return roll_sub(jnp.where(subs() == 7, ghost, x), 1)


def around(x, lat_ghost, lon_ghost):
    return (east(x, lon_ghost), west(x, lon_ghost), north(x, lat_ghost), south(x, lat_ghost))


def one_of(index, values):
    found = index == values[0]
    for value in values[1:]:
        found = found | (index == value)
    return found


def lat_field(x, f, odd):
    return roll_lane(x, 16 * f + 8 + 64 * odd)


def from_lat_group(x, f, odd):
    return roll_lane(x, -(16 * f + 8 + 64 * odd))


def group_of(lane):
    return lane // 16


def lat_pack_kernel(t_hbm, s_hbm, u_hbm, v_hbm, d_hbm, m_hbm, z_hbm, f_hbm, out_ref, t_ref, s_ref, u_ref, v_ref, d_ref, m_ref, z_ref, f_ref, sem):
    levels = t_ref.shape[0]
    half = levels // 2
    fields = ((t_hbm, t_ref), (s_hbm, s_ref), (u_hbm, u_ref), (v_hbm, v_ref))
    parts = [[(src.at[i : i + half], dst.at[i : i + half]) for src, dst in fields] for i in (0, half)]
    parts.append([(d_hbm, d_ref), (m_hbm, m_ref), (z_hbm, z_ref), (f_hbm, f_ref)])
    copies = [[pltpu.make_async_copy(*p, sem.at[i, j]) for j, p in enumerate(part)] for i, part in enumerate(parts)]
    for part in copies:
        for copy in part:
            copy.start()
    group = group_of(lanes())

    def put(out, fields, odd):
        for f, x in enumerate(fields):
            out = jnp.where(group == f + 4 * odd, lat_field(x, f, odd), out)
        return out

    zero = jnp.zeros((8, 128), F32)
    for j in range(levels // 2):
        if j % (half // 2) == 0:
            for copy in copies[j // (half // 2)]:
                copy.wait()
        out = zero
        for odd in range(2):
            k = 2 * j + odd
            out = put(out, (u_ref[k], v_ref[k], t_ref[k], s_ref[k]), odd)
        out_ref[j] = out
    for copy in copies[2]:
        copy.wait()
    sea = m_ref[...].astype(F32)
    depth = (d_ref[...] * m_ref[...]).astype(F32)
    out_ref[levels // 2] = put(zero, (depth, sea * z_ref[...], sea * f_ref[...]), 0)


def lon_rows_kernel(t_ref, s_ref, u_ref, v_ref, d_ref, m_ref, z_ref, f_ref, q_ref, r_ref):
    levels = t_ref.shape[0]
    sub = subs()
    odd_lon = jnp.full((8, 128), place()[0] % 2, jnp.int32) == 1

    def put(k, u, v, t, s):
        v4, t2, s6 = roll_sub(v, 4), roll_sub(t, 2), roll_sub(s, 6)
        x = jnp.where((sub >= 4) & (sub <= 5), v4, u)
        x = jnp.where(sub == 2, t2, x)
        to_west = jnp.where(sub == 6, s6, x)
        x = jnp.where((sub >= 2) & (sub <= 3), v4, u)
        x = jnp.where(sub == 1, t2, x)
        to_east = jnp.where(sub == 5, s6, x)
        q_ref[k] = jnp.where(odd_lon, to_west, to_east)
        r_ref[k] = jnp.where(odd_lon, to_east, to_west)

    for k in range(levels):
        put(k, u_ref[k], v_ref[k], t_ref[k], s_ref[k])
    sea = m_ref[...].astype(F32)
    depth, start = (d_ref[...] * m_ref[...]).astype(F32), sea * z_ref[...]
    put(levels, depth, start, sea * f_ref[...], start)
    put(levels + 1, depth, start, start, start)


def turn_rows(x):
    sub = subs()
    x = roll_sub(x, 4)
    x = jnp.where(sub // 2 % 2 == 0, roll_sub(x, -2), roll_sub(x, 2))
    return jnp.where(sub % 2 == 0, roll_sub(x, -1), roll_sub(x, 1))


def corners_kernel(top, a_ref, b_ref, r_in, q_in, g_ref, r_ref, q_ref):
    del q_in, r_in
    count = a_ref.shape[0]
    lane = lanes()
    lon, lat = place()
    is_even, odd_lon = 1 - lat % 2, lon % 2
    from_north = lane % 16 >= 8
    flow_sign = jnp.where(group_of(lane) % 4 < 2, -1.0, 1.0).astype(F32)

    sub = subs()
    odd_block = jnp.full((8, 128), odd_lon, jnp.int32) == 1
    west_row, east_row = sub == 3, sub == 0
    in_q = (west_row & odd_block) | (east_row & ~odd_block)
    in_r = (east_row & odd_block) | (west_row & ~odd_block)

    def put(j, g):
        g_ref[j] = g
        for odd in range(2):
            rows = jnp.where(west_row, roll_sub(g, 3 - odd), roll_sub(g, 1 + odd))
            k = 2 * j + odd
            q_ref[k] = jnp.where(in_q, rows, q_ref[k])
            r_ref[k] = jnp.where(in_r, rows, r_ref[k])

    @pl.when(lat != top)
    def _():
        from_a = from_north == (jnp.full((8, 128), is_even, jnp.int32) == 1)
        for j in range(count):
            put(j, jnp.where(from_a, a_ref[j], b_ref[j]))

    @pl.when(lat == top)
    def _():
        for j in range(count):
            rows = turn_rows(b_ref[j])
            turned = roll_lane(rows, 1)
            for i in range(1, 7):
                turned = jnp.where(lane % 16 == 8 + i, roll_lane(rows, 1 + 2 * i), turned)
            if j < count - 1:
                turned = turned * flow_sign
            put(j, jnp.where(from_north, turned, a_ref[j]))


def lon_masks():
    sub = subs()
    odd_lon = jnp.full((8, 128), place()[0] % 2, jnp.int32) == 1
    return [x != odd_lon for x in (one_of(sub, (0, 1, 4, 5)), sub == 2, sub == 6, sub == 3)]


def lon_ghost(q, r, masks):
    return jnp.where(masks[0], q, r)


def lon_tracers(q, r, masks):
    return roll_sub(jnp.where(masks[1], q, r), -2), roll_sub(jnp.where(masks[2], q, r), -6)


def corner_group(q_ref, r_ref, j, masks):
    sub = subs()
    x = jnp.where(masks[3], q_ref[2 * j], r_ref[2 * j])
    y = jnp.where(masks[3], q_ref[2 * j + 1], r_ref[2 * j + 1])
    return jnp.where(sub == 0, roll_sub(x, -3), jnp.where(sub == 7, roll_sub(x, -1), roll_sub(y, -2)))


LAT_PARTNER = (1, 0, 3, 2)
LON_PARTNER = (2, 3, 0, 1)


def ext_east(x):
    return [east(x[i], x[LON_PARTNER[i]]) for i in range(len(x))]


def ext_north(x):
    return [north(x[i], x[LAT_PARTNER[i]]) for i in range(len(x))]


def lap(x, mask_e, mask_n, tiles):
    f_e = [jnp.where(m, y - c, 0.0) for m, y, c in zip(mask_e, ext_east(x), x)]
    f_n = [jnp.where(m, y - c, 0.0) for m, y, c in zip(mask_n, ext_north(x), x)]
    out = []
    for i in tiles:
        out.append(f_e[i] - west(f_e[i], f_e[LON_PARTNER[i]]) + (f_n[i] - south(f_n[i], f_n[LAT_PARTNER[i]])))
    return out


def floats(i):
    return i.astype(F32)


def momentum_kernel(
    lat_size, th_ref, t_ref, s_ref, u_ref, v_ref, d_ref, m_ref, z_ref, f_ref, g_ref, r_ref, q_ref, us_ref, vs_ref, chunk_ref, st_ref
):
    levels = t_ref.shape[0]
    lane, sub = lanes(), subs()
    edges = lon_masks()
    last = levels // 2
    sea = m_ref[...].astype(F32)
    corner = corner_group(q_ref, r_ref, last, edges)
    edge = lon_ghost(q_ref[levels], r_ref[levels], edges)
    depth = [(d_ref[...] * m_ref[...]).astype(F32), from_lat_group(g_ref[last], 0, 0), edge, from_lat_group(corner, 0, 0)]
    low_e = [jnp.minimum(x, y) for x, y in zip(depth, ext_east(depth))]
    low_n = [jnp.minimum(x, y) for x, y in zip(depth, ext_north(depth))]
    lat_index = (lane + place()[1] * 128).astype(F32)
    ghost_index = lat_index + jnp.where(lane < 64, 128.0, -128.0)
    lats = 128.0 * lat_size
    ghost_index = jnp.where(ghost_index >= lats, 2.0 * lats - 1.0 - ghost_index, ghost_index)
    coriolis = [CORIOLIS * (2.0 * (x + 0.5) / lats - 1.0) for x in (lat_index, ghost_index)]
    zero = jnp.zeros((8, 128), F32)
    both = (0, 1)

    def level(k, odd, j, corners, carry):
        p, h, tu, tv = carry
        th = th_ref[k]
        kf = floats(k) + 0.5
        g, q_in, r_in = g_ref[j], q_ref[k], r_ref[k]
        u_h = lon_ghost(q_in, r_in, edges)
        t_h, s_h = lon_tracers(q_in, r_in, edges)
        u = [u_ref[k], from_lat_group(g, 0, odd), u_h, from_lat_group(corners, 0, odd)]
        v = [v_ref[k], from_lat_group(g, 1, odd), roll_sub(u_h, 4), from_lat_group(corners, 1, odd)]
        t = [t_ref[k], from_lat_group(g, 2, odd), t_h, from_lat_group(corners, 2, odd)]
        s = [s_ref[k], from_lat_group(g, 3, odd), s_h, from_lat_group(corners, 3, odd)]
        mask_e, mask_n, wet = [[x > kf for x in xs] for xs in (low_e, low_n, depth)]
        drag_u = lap(lap(u, mask_e, mask_n, range(4)), mask_e, mask_n, both)
        drag_v = lap(lap(v, mask_e, mask_n, range(4)), mask_e, mask_n, both)
        p = [c + jnp.where(m, (CONTRACTION * b - EXPANSION * a) * th, 0.0) for c, m, a, b in zip(p, wet, t, s)]
        h = [c + jnp.where(m, th, 0.0) for c, m in zip(h, wet)]
        f_e = [jnp.where(m, y - c, 0.0) for m, y, c in zip(mask_e, ext_east(p), p)]
        f_n = [jnp.where(m, y - c, 0.0) for m, y, c in zip(mask_n, ext_north(p), p)]
        us, vs = [], []
        for i in both:
            grad_x = f_e[i] + west(f_e[i], f_e[LON_PARTNER[i]])
            grad_y = f_n[i] + south(f_n[i], f_n[LAT_PARTNER[i]])
            x = u[i] + coriolis[i] * v[i] - (0.5 * PRESSURE_SCALE) * grad_x - FRICTION * drag_u[i]
            y = v[i] - coriolis[i] * u[i] - (0.5 * PRESSURE_SCALE) * grad_y - FRICTION * drag_v[i]
            us.append(jnp.where(wet[i], x, 0.0))
            vs.append(jnp.where(wet[i], y, 0.0))
        us_ref[k] = us[0]
        vs_ref[k] = vs[0]
        return (p, h, [a + th * b for a, b in zip(tu, us)], [a + th * b for a, b in zip(tv, vs)])

    def step(i, carry):
        for j in range(TILES_PER_STEP):
            at = i * TILES_PER_STEP + j
            corners = corner_group(q_ref, r_ref, at, edges)
            for odd in range(2):
                carry = level(2 * at + odd, odd, at, corners, carry)
        return carry

    _, h, tu, tv = lax.fori_loop(0, last // TILES_PER_STEP, step, ([zero] * 4, [zero] * 4, [zero] * 2, [zero] * 2))
    start = [sea * z_ref[...], from_lat_group(g_ref[last], 1, 0), roll_sub(edge, 4), from_lat_group(corner, 1, 0)]
    drive = [sea * f_ref[...], from_lat_group(g_ref[last], 2, 0)]
    weight_e = [jnp.minimum(x, y) * (1.0 / levels) for x, y in zip(h, ext_east(h))]
    weight_n = [jnp.minimum(x, y) * (1.0 / levels) for x, y in zip(h, ext_north(h))]
    flux_e = [x * (y - c) for x, y, c in zip(weight_e, ext_east(start), start)]
    flux_n = [x * (y - c) for x, y, c in zip(weight_n, ext_north(start), start)]
    rights = []
    for i in both:
        spread = flux_e[i] - west(flux_e[i], flux_e[LON_PARTNER[i]]) + (flux_n[i] - south(flux_n[i], flux_n[LAT_PARTNER[i]]))
        base = drive[i] - (STORAGE * start[i] - spread)
        tu_e = jnp.where(sub == 7, 0.0, roll_sub(tu[i], -1))
        tu_w = jnp.where(sub == 0, 0.0, roll_sub(tu[i], 1))
        tv_n, tv_s = north(tv[i], tv[1 - i]), south(tv[i], tv[1 - i])
        rights.append(base - jnp.where(h[i] > 0.0, (0.5 * DIVERGENCE) * ((tu_e - tu_w) + (tv_n - tv_s)), 0.0))
    halo = jnp.where(lane < 16, roll_lane(h[1], 8), jnp.where(lane < 32, roll_lane(rights[1], 24), roll_lane(tu[1], 40)))
    halo = jnp.where(lane < 64, halo, roll_lane(roll_sub(halo, 4), 64))
    halo = jnp.where(sub < 4, halo, jnp.where(sub == 4, roll_sub(tu[0], 4), roll_sub(tu[0], -2)))
    chunk_ref[0] = h[0]
    chunk_ref[1] = rights[0]
    chunk_ref[2] = halo
    for i in range(3):
        st_ref[i] = start[i]


def tracer_kernel(th_ref, t_ref, s_ref, u_ref, v_ref, d_ref, m_ref, g_ref, q_ref, r_ref, after_ref, nt_ref, ns_ref):
    del after_ref
    levels = t_ref.shape[0]
    edges = lon_masks()
    depth = (d_ref[...] * m_ref[...]).astype(F32)
    depth_g = from_lat_group(g_ref[levels // 2], 0, 0)
    depth_h = lon_ghost(q_ref[levels], r_ref[levels], edges)
    low = [jnp.minimum(depth, n) for n in around(depth, depth_g, depth_h)]
    zero = jnp.zeros((8, 128), F32)

    def level(k, odd, j, carry):
        above_t, above_s = carry
        kf = floats(k) + 0.5
        below = jnp.minimum(k + 1, levels - 1)
        th, th_below = th_ref[k], th_ref[below]
        u, v, t, s = u_ref[k], v_ref[k], t_ref[k], s_ref[k]
        g, q_in, r_in = g_ref[j], q_ref[k], r_ref[k]
        u_h = lon_ghost(q_in, r_in, edges)
        t_h, s_h = lon_tracers(q_in, r_in, edges)
        v_g = from_lat_group(g, 1, odd)
        wet = depth > kf
        wet_below = (depth > kf + 1.0) & (k + 1 < levels)
        inv_space = 1.0 / (0.5 * (th + th_below))
        inv_th = MIXING / th
        flow = [0.25 * x for x in (u + east(u, u_h), west(u, u_h) + u, v + north(v, v_g), south(v, v_g) + v)]
        masks = [x > kf for x in low]
        fluxes = []
        for q, q_g, q_h, full_ref, above, out_ref in (
            (t, from_lat_group(g, 2, odd), t_h, t_ref, above_t, nt_ref),
            (s, from_lat_group(g, 3, odd), s_h, s_ref, above_s, ns_ref),
        ):
            q_e, q_w, q_n, q_s = around(q, q_g, q_h)
            f_e = jnp.where(masks[0], flow[0] * (q + q_e) - DIFFUSION * (q_e - q), 0.0)
            f_w = jnp.where(masks[1], flow[1] * (q_w + q) - DIFFUSION * (q - q_w), 0.0)
            f_n = jnp.where(masks[2], flow[2] * (q + q_n) - DIFFUSION * (q_n - q), 0.0)
            f_s = jnp.where(masks[3], flow[3] * (q_s + q) - DIFFUSION * (q - q_s), 0.0)
            vflux = jnp.where(wet_below, (full_ref[below] - q) * inv_space, 0.0)
            vertical = (vflux - above) * inv_th
            out_ref[k] = jnp.where(wet, q + (f_w - f_e + f_s - f_n) + vertical, 0.0)
            fluxes.append(vflux)
        return tuple(fluxes)

    def step(i, carry):
        for j in range(TILES_PER_STEP):
            at = i * TILES_PER_STEP + j
            for odd in range(2):
                carry = level(2 * at + odd, odd, at, carry)
        return carry

    lax.fori_loop(0, levels // 2 // TILES_PER_STEP, step, (zero, zero))


def slab_kernel(levels, own_ref, q_ref, r_ref, st_ref, sum_ref, flat_ref, we_s, wn_s, fac_s, inv_s, r_s, d_s, z_s):
    odd_group = jnp.full((GROUP, 128), lax.axis_index(LON[0]) % 2, jnp.int32) == 1

    def rows(i):
        own, q, r = (ref[pl.ds(i, GROUP, stride=24), :] for ref in (own_ref, q_ref, r_ref))
        return jnp.concatenate([jnp.where(odd_group, q, r), own, jnp.where(odd_group, r, q)], axis=0)

    here = GROUP + lax.axis_index(LON[1])
    right, left = here + 1, here - 1
    heights, tu = [], [None] * 8
    for p in range(8):
        packed = rows(16 + p % 4)
        at = 64 * (p // 4)
        heights.append(jnp.concatenate([rows(p), roll_lane(packed, -8 - at)], axis=1))
        r_s[p] = jnp.concatenate([rows(8 + p), roll_lane(packed, -24 - at)], axis=1)
        if p in (0, 7):
            tu[p] = jnp.concatenate([rows(20 if p == 0 else 21), roll_lane(packed, -40 - at)], axis=1)
    r_s[0] = r_s[0] + jnp.where(heights[0] > 0.0, (0.5 * DIVERGENCE) * roll_sub(tu[7], 1), 0.0)
    r_s[7] = r_s[7] - jnp.where(heights[7] > 0.0, (0.5 * DIVERGENCE) * roll_sub(tu[0], -1), 0.0)
    for p in range(8):
        h = heights[p]
        h_e = heights[p + 1] if p < 7 else roll_sub(heights[0], -1)
        we_s[p] = jnp.minimum(h, h_e) * (1.0 / levels)
        wn_s[p] = jnp.minimum(h, roll_lane(h, -1)) * (1.0 / levels)
    for p in range(8):
        w_w = we_s[p - 1] if p > 0 else roll_sub(we_s[7], 1)
        wn = wn_s[p]
        diag = STORAGE + we_s[p] + w_w + wn + roll_lane(wn, 1)
        if p > 0:
            diag = diag + w_w * fac_s[p - 1]
        inv = 1.0 / diag
        inv_s[p] = inv
        fac_s[p] = -we_s[p] * inv

    mid = 0.5 * (SPECTRUM_HIGH + SPECTRUM_LOW)
    half = 0.5 * (SPECTRUM_HIGH - SPECTRUM_LOW)
    ratio = mid / half

    def residuals():
        d, last = d_s[0], d_s[7]
        edge = we_s[7] * (roll_sub(d, -1) - last)
        f_w = roll_sub(edge, 1)
        for p in range(8):
            d_e = d_s[p + 1] if p < 7 else None
            f_e = we_s[p] * (d_e - d) if p < 7 else edge
            f_n = wn_s[p] * (roll_lane(d, -1) - d)
            yield r_s[p] - STORAGE * d + ((f_e - f_w) + (f_n - roll_lane(f_n, 1)))
            f_w, d = f_e, d_e

    def step(scale_old, scale_new, first):
        y = []
        for p, r in enumerate((r_s[p] for p in range(8)) if first else residuals()):
            if not first:
                r_s[p] = r
            y.append((r + we_s[p - 1] * y[p - 1] if p > 0 else r) * inv_s[p])
        x = None
        for p in range(7, -1, -1):
            x = y[p] if x is None else y[p] - fac_s[p] * x
            d = x * scale_new if first else scale_old * d_s[p] + scale_new * x
            d_s[p] = d
            z_s[p] = d if first else z_s[p] + d

    step(0.0, 1.0 / mid, True)
    rho = 1.0 / ratio
    for _ in range(ITERS - 1):
        rho_next = 1.0 / (2.0 * ratio - rho)
        step(rho_next * rho, 2.0 * rho_next / half, False)
        rho = rho_next
    total = jnp.zeros((GROUP, 128), F32)
    for r in residuals():
        r = r[GROUP : 2 * GROUP, 0:128]
        total = total + r * r
    total = jnp.sum(jnp.sum(total, axis=0, keepdims=True), axis=1, keepdims=True) + jnp.zeros((1, 128), F32)
    for i in range(sum_ref.shape[0]):
        sum_ref[i] = total

    both = jnp.concatenate([z_s[p, pl.ds(here, 1), :] for p in range(8)], axis=0)
    x_e, x_w = z_s[0, pl.ds(right, 1), :], z_s[7, pl.ds(left, 1), :]
    x, x_g = both[:, 0:128], both[:, 128:256]
    sub = subs()
    x_e = jnp.broadcast_to(x_e[:, 0:128], (8, 128))
    x_w = jnp.broadcast_to(x_w[:, 0:128], (8, 128))
    x_h = jnp.where(sub < 4, x_e, x_w)
    x, x_g, x_h = x + st_ref[0], x_g + st_ref[1], x_h + st_ref[2]
    e, w, n, s = around(x, x_g, x_h)
    flat_ref[0] = (0.5 * GRAVITY) * (e - w)
    flat_ref[1] = (0.5 * GRAVITY) * (n - s)
    flat_ref[2] = x


def velocity_kernel(us_ref, vs_ref, d_ref, m_ref, flat_ref, nu_ref, nv_ref, surf_ref):
    depth = (d_ref[...] * m_ref[...]).astype(F32)
    slope_x, slope_y = flat_ref[0], flat_ref[1]
    surf_ref[...] = flat_ref[2]
    for k in range(us_ref.shape[0]):
        wet = depth > k + 0.5
        nu_ref[k] = jnp.where(wet, us_ref[k] - slope_x, 0.0)
        nv_ref[k] = jnp.where(wet, vs_ref[k] - slope_y, 0.0)


def call(kernel, name, outs, in_specs, scratch=(), aliases=None):
    return pl.pallas_call(
        kernel,
        name=name,
        out_shape=outs,
        in_specs=in_specs,
        out_specs=jax.tree.map(lambda _: VMEM, outs),
        scratch_shapes=list(scratch),
        input_output_aliases=aliases or {},
        compiler_params=pltpu.CompilerParams(vmem_limit_bytes=48 << 20),
    )


def from_all(x, axes):
    size = 1
    for axis in axes:
        size *= lax.axis_size(axis)
    copies = jnp.broadcast_to(x[None], (size, *x.shape))
    return lax.all_to_all(copies, axes, 0, 0, tiled=True)


def per_device(lon_size, lat_size, temp, salt, u, v, strata, sea, thickness, elevation, drive):
    levels = temp.shape[0]
    top = lat_size - 1
    pairs_a = [(i, i ^ 1) for i in range(lat_size)]
    pairs_b = []
    for a in range(lon_size):
        for i in range(1, top, 2):
            pairs_b += [(a * lat_size + i, a * lat_size + i + 1), (a * lat_size + i + 1, a * lat_size + i)]
        pairs_b.append((a * lat_size + top, (lon_size - 1 - a) * lat_size + top))

    def lat_swap(x):
        return lax.ppermute(x, "lat", pairs_a), lax.ppermute(x, (*LON, "lat"), pairs_b)

    def tiles(n, kind=F32):
        return jax.ShapeDtypeStruct((n, 8, 128), kind)

    field, flat = tiles(levels), (8, 128)
    message, packed = tiles(levels + 2), tiles(levels // 2 + 1)
    own = (temp, salt, u, v, strata, sea, elevation, drive)

    flat_int, flat_float = jax.ShapeDtypeStruct(flat, jnp.int32), jax.ShapeDtypeStruct(flat, F32)
    edges, *own = call(
        lat_pack_kernel,
        "lat_pack",
        (packed, *[field] * 4, flat_int, flat_int, flat_float, flat_float),
        [pl.BlockSpec(memory_space=pltpu.HBM)] * 8,
        [pltpu.SemaphoreType.DMA((3, 4))],
    )(*[pltpu.with_memory_space_constraint(x, pltpu.HBM) for x in own])
    temp, salt, u, v, strata, sea = own[:6]
    got_a, got_b = lat_swap(edges)
    thick = jnp.broadcast_to(thickness[:, None, None], field.shape)
    rows_q, rows_r = call(lon_rows_kernel, "lon_rows", (message, message), [VMEM] * 8)(*own)
    corners = functools.partial(corners_kernel, top)
    ghost, pair_r, pair_q = call(corners, "corners", (packed, message, message), [VMEM] * 4, aliases={2: 1, 3: 2})(
        got_a, got_b, rows_r, rows_q
    )
    pair_r = lax.ppermute(pair_r, LON, [(i, (i + 1 if i % 2 else i - 1) % lon_size) for i in range(lon_size)])
    pair_q = lax.ppermute(pair_q, LON, [(i, i ^ 1) for i in range(lon_size)])
    u_star, v_star, chunk, start = call(
        functools.partial(momentum_kernel, lat_size), "momentum", (field, field, tiles(3), tiles(3)), [VMEM] * 12
    )(thick, *own, ghost, pair_r, pair_q)
    group = from_all(chunk, ("lon_lo",)).reshape(GROUP * 24, 128)
    group, after = lax.optimization_barrier((group, chunk))
    groups = lon_size // GROUP
    group_q = lax.ppermute(group, "lon_hi", [(i, i ^ 1) for i in range(groups)])
    group_r = lax.ppermute(group, "lon_hi", [(i, (i + 1 if i % 2 else i - 1) % groups) for i in range(groups)])
    new_temp, new_salt = call(tracer_kernel, "tracers", (field, field), [VMEM] * 11)(
        thick, temp, salt, u, v, strata, sea, ghost, pair_q, pair_r, after
    )
    group_q, group_r, new_temp, new_salt = lax.optimization_barrier((group_q, group_r, new_temp, new_salt))
    sums, solved = call(
        functools.partial(slab_kernel, levels),
        "slab",
        (jax.ShapeDtypeStruct((groups * lat_size, 1, 128), F32), tiles(3)),
        [VMEM] * 4,
        [pltpu.VMEM((8, 3 * GROUP, 256), F32)] * 7,
    )(group, group_q, group_r, start)
    sums = lax.all_to_all(sums, ("lon_hi", "lat"), 0, 0, tiled=True)
    total = jnp.sum(sums, axis=0)
    cells = lon_size * 8 * lat_size * 128
    rms = jnp.sqrt(total[0, 0] / cells + EPSILON)
    new_u, new_v, surface = call(velocity_kernel, "velocity", (field, field, flat_float), [VMEM] * 5)(
        u_star, v_star, strata, sea, solved
    )
    return (new_temp, new_salt, new_u, new_v, surface, rms)


def solution(mesh):
    lon_size, lat_size = mesh.shape["lon"], mesh.shape["lat"]
    finer = Mesh(mesh.devices.reshape(lon_size // GROUP, GROUP, lat_size), (*LON, "lat"))
    cube, flat = P(None, LON, "lat"), P(LON, "lat")
    return jax.shard_map(
        functools.partial(per_device, lon_size, lat_size),
        mesh=finer,
        in_specs=(cube, cube, cube, cube, flat, flat, P(), flat, flat),
        out_specs=(cube, cube, cube, cube, flat, P()),
        check_vma=False,
    )
```

```python
import functools

import jax
import jax.numpy as jnp
from jax import lax
from jax.experimental import pallas as pl
from jax.experimental.pallas import tpu as pltpu
from jax.sharding import Mesh
from jax.sharding import PartitionSpec as P

DIFFUSION = 0.15
MIXING = 0.1
EXPANSION = 0.2
CONTRACTION = 0.15
PRESSURE_SCALE = 0.02
CORIOLIS = 0.5
FRICTION = 0.01
DIVERGENCE = 0.3
STORAGE = 0.1
SPECTRUM_LOW = 0.1
SPECTRUM_HIGH = 1.9
GRAVITY = 0.3
EPSILON = 1e-06
ITERS = 4
TILES_PER_STEP = 4
GROUP = 8
REACH = ITERS + 1
LON = ("lon_hi", "lon_lo")
F32 = jnp.float32

VMEM = pl.BlockSpec(memory_space=pltpu.VMEM)


def place():
    return lax.axis_index(LON[0]) * GROUP + lax.axis_index(LON[1]), lax.axis_index("lat")


def lanes(shape=(8, 128)):
    return lax.broadcasted_iota(jnp.int32, shape, 1)


def subs(shape=(8, 128)):
    return lax.broadcasted_iota(jnp.int32, shape, 0)


def roll_lane(x, shift):
    return pltpu.roll(x, shift % x.shape[1], 1)


def roll_sub(x, shift):
    return pltpu.roll(x, shift % x.shape[0], 0)


def north(x, ghost):
    return roll_lane(jnp.where(lanes() == 0, ghost, x), -1)


def south(x, ghost):
    return roll_lane(jnp.where(lanes() == 127, ghost, x), 1)


def east(x, ghost):
    return roll_sub(jnp.where(subs() == 0, ghost, x), -1)


def west(x, ghost):
    return roll_sub(jnp.where(subs() == 7, ghost, x), 1)


def around(x, lat_ghost, lon_ghost):
    return (east(x, lon_ghost), west(x, lon_ghost), north(x, lat_ghost), south(x, lat_ghost))


def one_of(index, values):
    found = index == values[0]
    for value in values[1:]:
        found = found | (index == value)
    return found


def lat_field(x, f, odd):
    return roll_lane(x, 16 * f + 8 + 64 * odd)


def from_lat_group(x, f, odd):
    return roll_lane(x, -(16 * f + 8 + 64 * odd))


def group_of(lane):
    return lane // 16


def lat_pack_kernel(t_hbm, s_hbm, u_hbm, v_hbm, d_hbm, m_hbm, z_hbm, f_hbm, out_ref, t_ref, s_ref, u_ref, v_ref, d_ref, m_ref, z_ref, f_ref, sem):
    levels = t_ref.shape[0]
    half = levels // 2
    fields = ((t_hbm, t_ref), (s_hbm, s_ref), (u_hbm, u_ref), (v_hbm, v_ref))
    parts = [[(src.at[i : i + half], dst.at[i : i + half]) for src, dst in fields] for i in (0, half)]
    parts.append([(d_hbm, d_ref), (m_hbm, m_ref), (z_hbm, z_ref), (f_hbm, f_ref)])
    copies = [[pltpu.make_async_copy(*p, sem.at[i, j]) for j, p in enumerate(part)] for i, part in enumerate(parts)]
    for part in copies:
        for copy in part:
            copy.start()
    group = group_of(lanes())

    def put(out, fields, odd):
        for f, x in enumerate(fields):
            out = jnp.where(group == f + 4 * odd, lat_field(x, f, odd), out)
        return out

    zero = jnp.zeros((8, 128), F32)
    for j in range(levels // 2):
        if j % (half // 2) == 0:
            for copy in copies[j // (half // 2)]:
                copy.wait()
        out = zero
        for odd in range(2):
            k = 2 * j + odd
            out = put(out, (u_ref[k], v_ref[k], t_ref[k], s_ref[k]), odd)
        out_ref[j] = out
    for copy in copies[2]:
        copy.wait()
    sea = m_ref[...].astype(F32)
    depth = (d_ref[...] * m_ref[...]).astype(F32)
    out_ref[levels // 2] = put(zero, (depth, sea * z_ref[...], sea * f_ref[...]), 0)


def lon_rows_kernel(t_ref, s_ref, u_ref, v_ref, d_ref, m_ref, z_ref, f_ref, q_ref, r_ref):
    levels = t_ref.shape[0]
    sub = subs()
    odd_lon = jnp.full((8, 128), place()[0] % 2, jnp.int32) == 1

    def put(k, u, v, t, s):
        v4, t2, s6 = roll_sub(v, 4), roll_sub(t, 2), roll_sub(s, 6)
        x = jnp.where((sub >= 4) & (sub <= 5), v4, u)
        x = jnp.where(sub == 2, t2, x)
        to_west = jnp.where(sub == 6, s6, x)
        x = jnp.where((sub >= 2) & (sub <= 3), v4, u)
        x = jnp.where(sub == 1, t2, x)
        to_east = jnp.where(sub == 5, s6, x)
        q_ref[k] = jnp.where(odd_lon, to_west, to_east)
        r_ref[k] = jnp.where(odd_lon, to_east, to_west)

    for k in range(levels):
        put(k, u_ref[k], v_ref[k], t_ref[k], s_ref[k])
    sea = m_ref[...].astype(F32)
    depth, start = (d_ref[...] * m_ref[...]).astype(F32), sea * z_ref[...]
    put(levels, depth, start, sea * f_ref[...], start)
    put(levels + 1, depth, start, start, start)


def turn_rows(x):
    sub = subs()
    x = roll_sub(x, 4)
    x = jnp.where(sub // 2 % 2 == 0, roll_sub(x, -2), roll_sub(x, 2))
    return jnp.where(sub % 2 == 0, roll_sub(x, -1), roll_sub(x, 1))


def corners_kernel(top, a_ref, b_ref, r_in, q_in, g_ref, r_ref, q_ref):
    del q_in, r_in
    count = a_ref.shape[0]
    lane = lanes()
    lon, lat = place()
    is_even, odd_lon = 1 - lat % 2, lon % 2
    from_north = lane % 16 >= 8
    flow_sign = jnp.where(group_of(lane) % 4 < 2, -1.0, 1.0).astype(F32)

    sub = subs()
    odd_block = jnp.full((8, 128), odd_lon, jnp.int32) == 1
    west_row, east_row = sub == 3, sub == 0
    in_q = (west_row & odd_block) | (east_row & ~odd_block)
    in_r = (east_row & odd_block) | (west_row & ~odd_block)

    def put(j, g):
        g_ref[j] = g
        for odd in range(2):
            rows = jnp.where(west_row, roll_sub(g, 3 - odd), roll_sub(g, 1 + odd))
            k = 2 * j + odd
            q_ref[k] = jnp.where(in_q, rows, q_ref[k])
            r_ref[k] = jnp.where(in_r, rows, r_ref[k])

    @pl.when(lat != top)
    def _():
        from_a = from_north == (jnp.full((8, 128), is_even, jnp.int32) == 1)
        for j in range(count):
            put(j, jnp.where(from_a, a_ref[j], b_ref[j]))

    @pl.when(lat == top)
    def _():
        for j in range(count):
            rows = turn_rows(b_ref[j])
            turned = roll_lane(rows, 1)
            for i in range(1, 7):
                turned = jnp.where(lane % 16 == 8 + i, roll_lane(rows, 1 + 2 * i), turned)
            if j < count - 1:
                turned = turned * flow_sign
            put(j, jnp.where(from_north, turned, a_ref[j]))


def lon_masks():
    sub = subs()
    odd_lon = jnp.full((8, 128), place()[0] % 2, jnp.int32) == 1
    return [x != odd_lon for x in (one_of(sub, (0, 1, 4, 5)), sub == 2, sub == 6, sub == 3)]


def lon_ghost(q, r, masks):
    return jnp.where(masks[0], q, r)


def lon_tracers(q, r, masks):
    return roll_sub(jnp.where(masks[1], q, r), -2), roll_sub(jnp.where(masks[2], q, r), -6)


def corner_group(q_ref, r_ref, j, masks):
    sub = subs()
    x = jnp.where(masks[3], q_ref[2 * j], r_ref[2 * j])
    y = jnp.where(masks[3], q_ref[2 * j + 1], r_ref[2 * j + 1])
    return jnp.where(sub == 0, roll_sub(x, -3), jnp.where(sub == 7, roll_sub(x, -1), roll_sub(y, -2)))


LAT_PARTNER = (1, 0, 3, 2)
LON_PARTNER = (2, 3, 0, 1)


def ext_east(x):
    return [east(x[i], x[LON_PARTNER[i]]) for i in range(len(x))]


def ext_north(x):
    return [north(x[i], x[LAT_PARTNER[i]]) for i in range(len(x))]


def lap(x, mask_e, mask_n, tiles):
    f_e = [jnp.where(m, y - c, 0.0) for m, y, c in zip(mask_e, ext_east(x), x)]
    f_n = [jnp.where(m, y - c, 0.0) for m, y, c in zip(mask_n, ext_north(x), x)]
    out = []
    for i in tiles:
        out.append(f_e[i] - west(f_e[i], f_e[LON_PARTNER[i]]) + (f_n[i] - south(f_n[i], f_n[LAT_PARTNER[i]])))
    return out


def floats(i):
    return i.astype(F32)


def momentum_kernel(
    lat_size, th_ref, t_ref, s_ref, u_ref, v_ref, d_ref, m_ref, z_ref, f_ref, g_ref, r_ref, q_ref, us_ref, vs_ref, chunk_ref, st_ref
):
    levels = t_ref.shape[0]
    lane, sub = lanes(), subs()
    edges = lon_masks()
    last = levels // 2
    sea = m_ref[...].astype(F32)
    corner = corner_group(q_ref, r_ref, last, edges)
    edge = lon_ghost(q_ref[levels], r_ref[levels], edges)
    depth = [(d_ref[...] * m_ref[...]).astype(F32), from_lat_group(g_ref[last], 0, 0), edge, from_lat_group(corner, 0, 0)]
    low_e = [jnp.minimum(x, y) for x, y in zip(depth, ext_east(depth))]
    low_n = [jnp.minimum(x, y) for x, y in zip(depth, ext_north(depth))]
    lat_index = (lane + place()[1] * 128).astype(F32)
    ghost_index = lat_index + jnp.where(lane < 64, 128.0, -128.0)
    lats = 128.0 * lat_size
    ghost_index = jnp.where(ghost_index >= lats, 2.0 * lats - 1.0 - ghost_index, ghost_index)
    coriolis = [CORIOLIS * (2.0 * (x + 0.5) / lats - 1.0) for x in (lat_index, ghost_index)]
    zero = jnp.zeros((8, 128), F32)
    both = (0, 1)

    def level(k, odd, j, corners, carry):
        p, h, tu, tv = carry
        th = th_ref[k]
        kf = floats(k) + 0.5
        g, q_in, r_in = g_ref[j], q_ref[k], r_ref[k]
        u_h = lon_ghost(q_in, r_in, edges)
        t_h, s_h = lon_tracers(q_in, r_in, edges)
        u = [u_ref[k], from_lat_group(g, 0, odd), u_h, from_lat_group(corners, 0, odd)]
        v = [v_ref[k], from_lat_group(g, 1, odd), roll_sub(u_h, 4), from_lat_group(corners, 1, odd)]
        t = [t_ref[k], from_lat_group(g, 2, odd), t_h, from_lat_group(corners, 2, odd)]
        s = [s_ref[k], from_lat_group(g, 3, odd), s_h, from_lat_group(corners, 3, odd)]
        mask_e, mask_n, wet = [[x > kf for x in xs] for xs in (low_e, low_n, depth)]
        drag_u = lap(lap(u, mask_e, mask_n, range(4)), mask_e, mask_n, both)
        drag_v = lap(lap(v, mask_e, mask_n, range(4)), mask_e, mask_n, both)
        p = [c + jnp.where(m, (CONTRACTION * b - EXPANSION * a) * th, 0.0) for c, m, a, b in zip(p, wet, t, s)]
        h = [c + jnp.where(m, th, 0.0) for c, m in zip(h, wet)]
        f_e = [jnp.where(m, y - c, 0.0) for m, y, c in zip(mask_e, ext_east(p), p)]
        f_n = [jnp.where(m, y - c, 0.0) for m, y, c in zip(mask_n, ext_north(p), p)]
        us, vs = [], []
        for i in both:
            grad_x = f_e[i] + west(f_e[i], f_e[LON_PARTNER[i]])
            grad_y = f_n[i] + south(f_n[i], f_n[LAT_PARTNER[i]])
            x = u[i] + coriolis[i] * v[i] - (0.5 * PRESSURE_SCALE) * grad_x - FRICTION * drag_u[i]
            y = v[i] - coriolis[i] * u[i] - (0.5 * PRESSURE_SCALE) * grad_y - FRICTION * drag_v[i]
            us.append(jnp.where(wet[i], x, 0.0))
            vs.append(jnp.where(wet[i], y, 0.0))
        us_ref[k] = us[0]
        vs_ref[k] = vs[0]
        return (p, h, [a + th * b for a, b in zip(tu, us)], [a + th * b for a, b in zip(tv, vs)])

    def step(i, carry):
        for j in range(TILES_PER_STEP):
            at = i * TILES_PER_STEP + j
            corners = corner_group(q_ref, r_ref, at, edges)
            for odd in range(2):
                carry = level(2 * at + odd, odd, at, corners, carry)
        return carry

    _, h, tu, tv = lax.fori_loop(0, last // TILES_PER_STEP, step, ([zero] * 4, [zero] * 4, [zero] * 2, [zero] * 2))
    start = [sea * z_ref[...], from_lat_group(g_ref[last], 1, 0), roll_sub(edge, 4), from_lat_group(corner, 1, 0)]
    drive = [sea * f_ref[...], from_lat_group(g_ref[last], 2, 0)]
    weight_e = [jnp.minimum(x, y) * (1.0 / levels) for x, y in zip(h, ext_east(h))]
    weight_n = [jnp.minimum(x, y) * (1.0 / levels) for x, y in zip(h, ext_north(h))]
    flux_e = [x * (y - c) for x, y, c in zip(weight_e, ext_east(start), start)]
    flux_n = [x * (y - c) for x, y, c in zip(weight_n, ext_north(start), start)]
    rights = []
    for i in both:
        spread = flux_e[i] - west(flux_e[i], flux_e[LON_PARTNER[i]]) + (flux_n[i] - south(flux_n[i], flux_n[LAT_PARTNER[i]]))
        base = drive[i] - (STORAGE * start[i] - spread)
        tu_e = jnp.where(sub == 7, 0.0, roll_sub(tu[i], -1))
        tu_w = jnp.where(sub == 0, 0.0, roll_sub(tu[i], 1))
        tv_n, tv_s = north(tv[i], tv[1 - i]), south(tv[i], tv[1 - i])
        rights.append(base - jnp.where(h[i] > 0.0, (0.5 * DIVERGENCE) * ((tu_e - tu_w) + (tv_n - tv_s)), 0.0))
    halo = jnp.where(lane < 16, roll_lane(h[1], 8), jnp.where(lane < 32, roll_lane(rights[1], 24), roll_lane(tu[1], 40)))
    halo = jnp.where(lane < 64, halo, roll_lane(roll_sub(halo, 4), 64))
    halo = jnp.where(sub < 4, halo, jnp.where(sub == 4, roll_sub(tu[0], 4), roll_sub(tu[0], -2)))
    chunk_ref[0] = h[0]
    chunk_ref[1] = rights[0]
    chunk_ref[2] = halo
    for i in range(3):
        st_ref[i] = start[i]


def tracer_kernel(th_ref, t_ref, s_ref, u_ref, v_ref, d_ref, m_ref, g_ref, q_ref, r_ref, after_ref, nt_ref, ns_ref):
    del after_ref
    levels = t_ref.shape[0]
    edges = lon_masks()
    depth = (d_ref[...] * m_ref[...]).astype(F32)
    depth_g = from_lat_group(g_ref[levels // 2], 0, 0)
    depth_h = lon_ghost(q_ref[levels], r_ref[levels], edges)
    low = [jnp.minimum(depth, n) for n in around(depth, depth_g, depth_h)]
    zero = jnp.zeros((8, 128), F32)

    def level(k, odd, j, carry):
        above_t, above_s = carry
        kf = floats(k) + 0.5
        below = jnp.minimum(k + 1, levels - 1)
        th, th_below = th_ref[k], th_ref[below]
        u, v, t, s = u_ref[k], v_ref[k], t_ref[k], s_ref[k]
        g, q_in, r_in = g_ref[j], q_ref[k], r_ref[k]
        u_h = lon_ghost(q_in, r_in, edges)
        t_h, s_h = lon_tracers(q_in, r_in, edges)
        v_g = from_lat_group(g, 1, odd)
        wet = depth > kf
        wet_below = (depth > kf + 1.0) & (k + 1 < levels)
        inv_space = 1.0 / (0.5 * (th + th_below))
        inv_th = MIXING / th
        flow = [0.25 * x for x in (u + east(u, u_h), west(u, u_h) + u, v + north(v, v_g), south(v, v_g) + v)]
        masks = [x > kf for x in low]
        fluxes = []
        for q, q_g, q_h, full_ref, above, out_ref in (
            (t, from_lat_group(g, 2, odd), t_h, t_ref, above_t, nt_ref),
            (s, from_lat_group(g, 3, odd), s_h, s_ref, above_s, ns_ref),
        ):
            q_e, q_w, q_n, q_s = around(q, q_g, q_h)
            f_e = jnp.where(masks[0], flow[0] * (q + q_e) - DIFFUSION * (q_e - q), 0.0)
            f_w = jnp.where(masks[1], flow[1] * (q_w + q) - DIFFUSION * (q - q_w), 0.0)
            f_n = jnp.where(masks[2], flow[2] * (q + q_n) - DIFFUSION * (q_n - q), 0.0)
            f_s = jnp.where(masks[3], flow[3] * (q_s + q) - DIFFUSION * (q - q_s), 0.0)
            vflux = jnp.where(wet_below, (full_ref[below] - q) * inv_space, 0.0)
            vertical = (vflux - above) * inv_th
            out_ref[k] = jnp.where(wet, q + (f_w - f_e + f_s - f_n) + vertical, 0.0)
            fluxes.append(vflux)
        return tuple(fluxes)

    def step(i, carry):
        for j in range(TILES_PER_STEP):
            at = i * TILES_PER_STEP + j
            for odd in range(2):
                carry = level(2 * at + odd, odd, at, carry)
        return carry

    lax.fori_loop(0, levels // 2 // TILES_PER_STEP, step, (zero, zero))


def slab_kernel(levels, own_ref, q_ref, r_ref, st_ref, sum_ref, flat_ref, we_s, wn_s, fac_s, inv_s, r_s, d_s, z_s):
    odd_group = jnp.full((GROUP, 128), lax.axis_index(LON[0]) % 2, jnp.int32) == 1

    missing = jnp.zeros((GROUP - REACH, 128), F32)

    def rows(i):
        own = own_ref[pl.ds(i, GROUP, stride=24), :]
        q, r = (ref[pl.ds(i, REACH, stride=24), :] for ref in (q_ref, r_ref))
        west_q, west_r = (jnp.concatenate([missing, x], axis=0) for x in (q, r))
        east_q, east_r = (jnp.concatenate([x, missing], axis=0) for x in (q, r))
        return jnp.concatenate([jnp.where(odd_group, west_q, west_r), own, jnp.where(odd_group, east_r, east_q)], axis=0)

    here = GROUP + lax.axis_index(LON[1])
    right, left = here + 1, here - 1
    heights, tu = [], [None] * 8
    for p in range(8):
        packed = rows(16 + p % 4)
        at = 64 * (p // 4)
        heights.append(jnp.concatenate([rows(p), roll_lane(packed, -8 - at)], axis=1))
        r_s[p] = jnp.concatenate([rows(8 + p), roll_lane(packed, -24 - at)], axis=1)
        if p in (0, 7):
            tu[p] = jnp.concatenate([rows(20 if p == 0 else 21), roll_lane(packed, -40 - at)], axis=1)
    r_s[0] = r_s[0] + jnp.where(heights[0] > 0.0, (0.5 * DIVERGENCE) * roll_sub(tu[7], 1), 0.0)
    r_s[7] = r_s[7] - jnp.where(heights[7] > 0.0, (0.5 * DIVERGENCE) * roll_sub(tu[0], -1), 0.0)
    for p in range(8):
        h = heights[p]
        h_e = heights[p + 1] if p < 7 else roll_sub(heights[0], -1)
        we_s[p] = jnp.minimum(h, h_e) * (1.0 / levels)
        wn_s[p] = jnp.minimum(h, roll_lane(h, -1)) * (1.0 / levels)
    for p in range(8):
        w_w = we_s[p - 1] if p > 0 else roll_sub(we_s[7], 1)
        wn = wn_s[p]
        diag = STORAGE + we_s[p] + w_w + wn + roll_lane(wn, 1)
        if p > 0:
            diag = diag + w_w * fac_s[p - 1]
        inv = 1.0 / diag
        inv_s[p] = inv
        fac_s[p] = -we_s[p] * inv

    mid = 0.5 * (SPECTRUM_HIGH + SPECTRUM_LOW)
    half = 0.5 * (SPECTRUM_HIGH - SPECTRUM_LOW)
    ratio = mid / half

    def residuals():
        d, last = d_s[0], d_s[7]
        edge = we_s[7] * (roll_sub(d, -1) - last)
        f_w = roll_sub(edge, 1)
        for p in range(8):
            d_e = d_s[p + 1] if p < 7 else None
            f_e = we_s[p] * (d_e - d) if p < 7 else edge
            f_n = wn_s[p] * (roll_lane(d, -1) - d)
            yield r_s[p] - STORAGE * d + ((f_e - f_w) + (f_n - roll_lane(f_n, 1)))
            f_w, d = f_e, d_e

    def step(scale_old, scale_new, first):
        y = []
        for p, r in enumerate((r_s[p] for p in range(8)) if first else residuals()):
            if not first:
                r_s[p] = r
            y.append((r + we_s[p - 1] * y[p - 1] if p > 0 else r) * inv_s[p])
        x = None
        for p in range(7, -1, -1):
            x = y[p] if x is None else y[p] - fac_s[p] * x
            d = x * scale_new if first else scale_old * d_s[p] + scale_new * x
            d_s[p] = d
            z_s[p] = d if first else z_s[p] + d

    step(0.0, 1.0 / mid, True)
    rho = 1.0 / ratio
    for _ in range(ITERS - 1):
        rho_next = 1.0 / (2.0 * ratio - rho)
        step(rho_next * rho, 2.0 * rho_next / half, False)
        rho = rho_next
    total = jnp.zeros((GROUP, 128), F32)
    for r in residuals():
        r = r[GROUP : 2 * GROUP, 0:128]
        total = total + r * r
    total = jnp.sum(jnp.sum(total, axis=0, keepdims=True), axis=1, keepdims=True) + jnp.zeros((1, 128), F32)
    for i in range(sum_ref.shape[0]):
        sum_ref[i] = total

    both = jnp.concatenate([z_s[p, pl.ds(here, 1), :] for p in range(8)], axis=0)
    x_e, x_w = z_s[0, pl.ds(right, 1), :], z_s[7, pl.ds(left, 1), :]
    x, x_g = both[:, 0:128], both[:, 128:256]
    sub = subs()
    x_e = jnp.broadcast_to(x_e[:, 0:128], (8, 128))
    x_w = jnp.broadcast_to(x_w[:, 0:128], (8, 128))
    x_h = jnp.where(sub < 4, x_e, x_w)
    x, x_g, x_h = x + st_ref[0], x_g + st_ref[1], x_h + st_ref[2]
    e, w, n, s = around(x, x_g, x_h)
    flat_ref[0] = (0.5 * GRAVITY) * (e - w)
    flat_ref[1] = (0.5 * GRAVITY) * (n - s)
    flat_ref[2] = x


def velocity_kernel(us_ref, vs_ref, d_ref, m_ref, flat_ref, nu_ref, nv_ref, surf_ref):
    depth = (d_ref[...] * m_ref[...]).astype(F32)
    slope_x, slope_y = flat_ref[0], flat_ref[1]
    surf_ref[...] = flat_ref[2]
    for k in range(us_ref.shape[0]):
        wet = depth > k + 0.5
        nu_ref[k] = jnp.where(wet, us_ref[k] - slope_x, 0.0)
        nv_ref[k] = jnp.where(wet, vs_ref[k] - slope_y, 0.0)


def call(kernel, name, outs, in_specs, scratch=(), aliases=None):
    return pl.pallas_call(
        kernel,
        name=name,
        out_shape=outs,
        in_specs=in_specs,
        out_specs=jax.tree.map(lambda _: VMEM, outs),
        scratch_shapes=list(scratch),
        input_output_aliases=aliases or {},
        compiler_params=pltpu.CompilerParams(vmem_limit_bytes=48 << 20),
    )


def from_all(x, axes):
    size = 1
    for axis in axes:
        size *= lax.axis_size(axis)
    copies = jnp.broadcast_to(x[None], (size, *x.shape))
    return lax.all_to_all(copies, axes, 0, 0, tiled=True)


def per_device(lon_size, lat_size, temp, salt, u, v, strata, sea, thickness, elevation, drive):
    levels = temp.shape[0]
    top = lat_size - 1
    pairs_a = [(i, i ^ 1) for i in range(lat_size)]
    pairs_b = []
    for a in range(lon_size):
        for i in range(1, top, 2):
            pairs_b += [(a * lat_size + i, a * lat_size + i + 1), (a * lat_size + i + 1, a * lat_size + i)]
        pairs_b.append((a * lat_size + top, (lon_size - 1 - a) * lat_size + top))

    def lat_swap(x):
        return lax.ppermute(x, "lat", pairs_a), lax.ppermute(x, (*LON, "lat"), pairs_b)

    def tiles(n, kind=F32):
        return jax.ShapeDtypeStruct((n, 8, 128), kind)

    field, flat = tiles(levels), (8, 128)
    message, packed = tiles(levels + 2), tiles(levels // 2 + 1)
    own = (temp, salt, u, v, strata, sea, elevation, drive)

    flat_int, flat_float = jax.ShapeDtypeStruct(flat, jnp.int32), jax.ShapeDtypeStruct(flat, F32)
    edges, *own = call(
        lat_pack_kernel,
        "lat_pack",
        (packed, *[field] * 4, flat_int, flat_int, flat_float, flat_float),
        [pl.BlockSpec(memory_space=pltpu.HBM)] * 8,
        [pltpu.SemaphoreType.DMA((3, 4))],
    )(*[pltpu.with_memory_space_constraint(x, pltpu.HBM) for x in own])
    temp, salt, u, v, strata, sea = own[:6]
    got_a, got_b = lat_swap(edges)
    thick = jnp.broadcast_to(thickness[:, None, None], field.shape)
    rows_q, rows_r = call(lon_rows_kernel, "lon_rows", (message, message), [VMEM] * 8)(*own)
    corners = functools.partial(corners_kernel, top)
    ghost, pair_r, pair_q = call(corners, "corners", (packed, message, message), [VMEM] * 4, aliases={2: 1, 3: 2})(
        got_a, got_b, rows_r, rows_q
    )
    pair_r = lax.ppermute(pair_r, LON, [(i, (i + 1 if i % 2 else i - 1) % lon_size) for i in range(lon_size)])
    pair_q = lax.ppermute(pair_q, LON, [(i, i ^ 1) for i in range(lon_size)])
    u_star, v_star, chunk, start = call(
        functools.partial(momentum_kernel, lat_size), "momentum", (field, field, tiles(3), tiles(3)), [VMEM] * 12
    )(thick, *own, ghost, pair_r, pair_q)
    chunk, odd_group = lax.optimization_barrier((chunk, lax.axis_index("lon_hi") % 2 == 1))
    group = from_all(chunk, ("lon_lo",)).reshape(GROUP * 24, 128)
    groups = lon_size // GROUP
    first, final = group[: REACH * 24], group[(GROUP - REACH) * 24 :]
    group_q, group_r = jnp.where(odd_group, first, final), jnp.where(odd_group, final, first)
    group, group_q, group_r, after = lax.optimization_barrier((group, group_q, group_r, chunk))
    group_q = lax.ppermute(group_q, "lon_hi", [(i, i ^ 1) for i in range(groups)])
    group_r = lax.ppermute(group_r, "lon_hi", [(i, (i + 1 if i % 2 else i - 1) % groups) for i in range(groups)])
    new_temp, new_salt = call(tracer_kernel, "tracers", (field, field), [VMEM] * 11)(
        thick, temp, salt, u, v, strata, sea, ghost, pair_q, pair_r, after
    )
    group_q, group_r, new_temp, new_salt = lax.optimization_barrier((group_q, group_r, new_temp, new_salt))
    sums, solved = call(
        functools.partial(slab_kernel, levels),
        "slab",
        (jax.ShapeDtypeStruct((groups * lat_size, 1, 128), F32), tiles(3)),
        [VMEM] * 4,
        [pltpu.VMEM((8, 3 * GROUP, 256), F32)] * 7,
    )(group, group_q, group_r, start)
    sums = lax.all_to_all(sums, ("lon_hi", "lat"), 0, 0, tiled=True)
    total = jnp.sum(sums, axis=0)
    cells = lon_size * 8 * lat_size * 128
    rms = jnp.sqrt(total[0, 0] / cells + EPSILON)
    new_u, new_v, surface = call(velocity_kernel, "velocity", (field, field, flat_float), [VMEM] * 5)(
        u_star, v_star, strata, sea, solved
    )
    return (new_temp, new_salt, new_u, new_v, surface, rms)


def solution(mesh):
    lon_size, lat_size = mesh.shape["lon"], mesh.shape["lat"]
    finer = Mesh(mesh.devices.reshape(lon_size // GROUP, GROUP, lat_size), (*LON, "lat"))
    cube, flat = P(None, LON, "lat"), P(LON, "lat")
    return jax.shard_map(
        functools.partial(per_device, lon_size, lat_size),
        mesh=finer,
        in_specs=(cube, cube, cube, cube, flat, flat, P(), flat, flat),
        out_specs=(cube, cube, cube, cube, flat, P()),
        check_vma=False,
    )
```

```python
import functools

import jax
import jax.numpy as jnp
from jax import lax
from jax.experimental import pallas as pl
from jax.experimental.pallas import tpu as pltpu
from jax.sharding import Mesh
from jax.sharding import PartitionSpec as P

DIFFUSION = 0.15
MIXING = 0.1
EXPANSION = 0.2
CONTRACTION = 0.15
PRESSURE_SCALE = 0.02
CORIOLIS = 0.5
FRICTION = 0.01
DIVERGENCE = 0.3
STORAGE = 0.1
SPECTRUM_LOW = 0.1
SPECTRUM_HIGH = 1.9
GRAVITY = 0.3
EPSILON = 1e-06
ITERS = 4
TILES_PER_STEP = 4
GROUP = 8
LON = ("lon_hi", "lon_lo")
F32 = jnp.float32

VMEM = pl.BlockSpec(memory_space=pltpu.VMEM)


def place():
    return lax.axis_index(LON[0]) * GROUP + lax.axis_index(LON[1]), lax.axis_index("lat")


def lanes(shape=(8, 128)):
    return lax.broadcasted_iota(jnp.int32, shape, 1)


def subs(shape=(8, 128)):
    return lax.broadcasted_iota(jnp.int32, shape, 0)


def roll_lane(x, shift):
    return pltpu.roll(x, shift % x.shape[1], 1)


def roll_sub(x, shift):
    return pltpu.roll(x, shift % x.shape[0], 0)


def north(x, ghost):
    return roll_lane(jnp.where(lanes() == 0, ghost, x), -1)


def south(x, ghost):
    return roll_lane(jnp.where(lanes() == 127, ghost, x), 1)


def east(x, ghost):
    return roll_sub(jnp.where(subs() == 0, ghost, x), -1)


def west(x, ghost):
    return roll_sub(jnp.where(subs() == 7, ghost, x), 1)


def around(x, lat_ghost, lon_ghost):
    return (east(x, lon_ghost), west(x, lon_ghost), north(x, lat_ghost), south(x, lat_ghost))


def one_of(index, values):
    found = index == values[0]
    for value in values[1:]:
        found = found | (index == value)
    return found


def lat_field(x, f, odd):
    return roll_lane(x, 16 * f + 8 + 64 * odd)


def from_lat_group(x, f, odd):
    return roll_lane(x, -(16 * f + 8 + 64 * odd))


def group_of(lane):
    return lane // 16


def lat_pack_kernel(t_hbm, s_hbm, u_hbm, v_hbm, d_hbm, m_hbm, z_hbm, f_hbm, out_ref, t_ref, s_ref, u_ref, v_ref, d_ref, m_ref, z_ref, f_ref, sem):
    levels = t_ref.shape[0]
    half = levels // 2
    fields = ((t_hbm, t_ref), (s_hbm, s_ref), (u_hbm, u_ref), (v_hbm, v_ref))
    parts = [[(src.at[i : i + half], dst.at[i : i + half]) for src, dst in fields] for i in (0, half)]
    parts.append([(d_hbm, d_ref), (m_hbm, m_ref), (z_hbm, z_ref), (f_hbm, f_ref)])
    copies = [[pltpu.make_async_copy(*p, sem.at[i, j]) for j, p in enumerate(part)] for i, part in enumerate(parts)]
    for part in copies:
        for copy in part:
            copy.start()
    group = group_of(lanes())

    def put(out, fields, odd):
        for f, x in enumerate(fields):
            out = jnp.where(group == f + 4 * odd, lat_field(x, f, odd), out)
        return out

    zero = jnp.zeros((8, 128), F32)
    for j in range(levels // 2):
        if j % (half // 2) == 0:
            for copy in copies[j // (half // 2)]:
                copy.wait()
        out = zero
        for odd in range(2):
            k = 2 * j + odd
            out = put(out, (u_ref[k], v_ref[k], t_ref[k], s_ref[k]), odd)
        out_ref[j] = out
    for copy in copies[2]:
        copy.wait()
    sea = m_ref[...].astype(F32)
    depth = (d_ref[...] * m_ref[...]).astype(F32)
    out_ref[levels // 2] = put(zero, (depth, sea * z_ref[...], sea * f_ref[...]), 0)


def lon_rows_kernel(t_ref, s_ref, u_ref, v_ref, d_ref, m_ref, z_ref, f_ref, q_ref, r_ref):
    levels = t_ref.shape[0]
    sub = subs()
    odd_lon = jnp.full((8, 128), place()[0] % 2, jnp.int32) == 1

    def put(k, u, v, t, s):
        v4, t2, s6 = roll_sub(v, 4), roll_sub(t, 2), roll_sub(s, 6)
        x = jnp.where((sub >= 4) & (sub <= 5), v4, u)
        x = jnp.where(sub == 2, t2, x)
        to_west = jnp.where(sub == 6, s6, x)
        x = jnp.where((sub >= 2) & (sub <= 3), v4, u)
        x = jnp.where(sub == 1, t2, x)
        to_east = jnp.where(sub == 5, s6, x)
        q_ref[k] = jnp.where(odd_lon, to_west, to_east)
        r_ref[k] = jnp.where(odd_lon, to_east, to_west)

    for k in range(levels):
        put(k, u_ref[k], v_ref[k], t_ref[k], s_ref[k])
    sea = m_ref[...].astype(F32)
    depth, start = (d_ref[...] * m_ref[...]).astype(F32), sea * z_ref[...]
    put(levels, depth, start, sea * f_ref[...], start)
    put(levels + 1, depth, start, start, start)


def turn_rows(x):
    sub = subs()
    x = roll_sub(x, 4)
    x = jnp.where(sub // 2 % 2 == 0, roll_sub(x, -2), roll_sub(x, 2))
    return jnp.where(sub % 2 == 0, roll_sub(x, -1), roll_sub(x, 1))


def corners_kernel(top, a_ref, b_ref, r_in, q_in, g_ref, r_ref, q_ref):
    del q_in, r_in
    count = a_ref.shape[0]
    lane = lanes()
    lon, lat = place()
    is_even, odd_lon = 1 - lat % 2, lon % 2
    from_north = lane % 16 >= 8
    flow_sign = jnp.where(group_of(lane) % 4 < 2, -1.0, 1.0).astype(F32)

    sub = subs()
    odd_block = jnp.full((8, 128), odd_lon, jnp.int32) == 1
    west_row, east_row = sub == 3, sub == 0
    in_q = (west_row & odd_block) | (east_row & ~odd_block)
    in_r = (east_row & odd_block) | (west_row & ~odd_block)

    def put(j, g):
        g_ref[j] = g
        for odd in range(2):
            rows = jnp.where(west_row, roll_sub(g, 3 - odd), roll_sub(g, 1 + odd))
            k = 2 * j + odd
            q_ref[k] = jnp.where(in_q, rows, q_ref[k])
            r_ref[k] = jnp.where(in_r, rows, r_ref[k])

    @pl.when(lat != top)
    def _():
        from_a = from_north == (jnp.full((8, 128), is_even, jnp.int32) == 1)
        for j in range(count):
            put(j, jnp.where(from_a, a_ref[j], b_ref[j]))

    @pl.when(lat == top)
    def _():
        for j in range(count):
            rows = turn_rows(b_ref[j])
            turned = roll_lane(rows, 1)
            for i in range(1, 7):
                turned = jnp.where(lane % 16 == 8 + i, roll_lane(rows, 1 + 2 * i), turned)
            if j < count - 1:
                turned = turned * flow_sign
            put(j, jnp.where(from_north, turned, a_ref[j]))


def lon_masks():
    sub = subs()
    odd_lon = jnp.full((8, 128), place()[0] % 2, jnp.int32) == 1
    return [x != odd_lon for x in (one_of(sub, (0, 1, 4, 5)), sub == 2, sub == 6, sub == 3)]


def lon_ghost(q, r, masks):
    return jnp.where(masks[0], q, r)


def lon_tracers(q, r, masks):
    return roll_sub(jnp.where(masks[1], q, r), -2), roll_sub(jnp.where(masks[2], q, r), -6)


def corner_group(q_ref, r_ref, j, masks):
    sub = subs()
    x = jnp.where(masks[3], q_ref[2 * j], r_ref[2 * j])
    y = jnp.where(masks[3], q_ref[2 * j + 1], r_ref[2 * j + 1])
    return jnp.where(sub == 0, roll_sub(x, -3), jnp.where(sub == 7, roll_sub(x, -1), roll_sub(y, -2)))


LAT_PARTNER = (1, 0, 3, 2)
LON_PARTNER = (2, 3, 0, 1)


def ext_east(x):
    return [east(x[i], x[LON_PARTNER[i]]) for i in range(len(x))]


def ext_north(x):
    return [north(x[i], x[LAT_PARTNER[i]]) for i in range(len(x))]


def lap(x, mask_e, mask_n, tiles):
    f_e = [jnp.where(m, y - c, 0.0) for m, y, c in zip(mask_e, ext_east(x), x)]
    f_n = [jnp.where(m, y - c, 0.0) for m, y, c in zip(mask_n, ext_north(x), x)]
    out = []
    for i in tiles:
        out.append(f_e[i] - west(f_e[i], f_e[LON_PARTNER[i]]) + (f_n[i] - south(f_n[i], f_n[LAT_PARTNER[i]])))
    return out


def floats(i):
    return i.astype(F32)


def momentum_kernel(
    lat_size, th_ref, t_ref, s_ref, u_ref, v_ref, d_ref, m_ref, z_ref, f_ref, g_ref, r_ref, q_ref, us_ref, vs_ref, chunk_ref, st_ref
):
    levels = t_ref.shape[0]
    lane, sub = lanes(), subs()
    edges = lon_masks()
    last = levels // 2
    sea = m_ref[...].astype(F32)
    corner = corner_group(q_ref, r_ref, last, edges)
    edge = lon_ghost(q_ref[levels], r_ref[levels], edges)
    depth = [(d_ref[...] * m_ref[...]).astype(F32), from_lat_group(g_ref[last], 0, 0), edge, from_lat_group(corner, 0, 0)]
    low_e = [jnp.minimum(x, y) for x, y in zip(depth, ext_east(depth))]
    low_n = [jnp.minimum(x, y) for x, y in zip(depth, ext_north(depth))]
    lat_index = (lane + place()[1] * 128).astype(F32)
    ghost_index = lat_index + jnp.where(lane < 64, 128.0, -128.0)
    lats = 128.0 * lat_size
    ghost_index = jnp.where(ghost_index >= lats, 2.0 * lats - 1.0 - ghost_index, ghost_index)
    coriolis = [CORIOLIS * (2.0 * (x + 0.5) / lats - 1.0) for x in (lat_index, ghost_index)]
    zero = jnp.zeros((8, 128), F32)
    both = (0, 1)

    def level(k, odd, j, corners, carry):
        p, h, tu, tv = carry
        th = th_ref[k]
        kf = floats(k) + 0.5
        g, q_in, r_in = g_ref[j], q_ref[k], r_ref[k]
        u_h = lon_ghost(q_in, r_in, edges)
        t_h, s_h = lon_tracers(q_in, r_in, edges)
        u = [u_ref[k], from_lat_group(g, 0, odd), u_h, from_lat_group(corners, 0, odd)]
        v = [v_ref[k], from_lat_group(g, 1, odd), roll_sub(u_h, 4), from_lat_group(corners, 1, odd)]
        t = [t_ref[k], from_lat_group(g, 2, odd), t_h, from_lat_group(corners, 2, odd)]
        s = [s_ref[k], from_lat_group(g, 3, odd), s_h, from_lat_group(corners, 3, odd)]
        mask_e, mask_n, wet = [[x > kf for x in xs] for xs in (low_e, low_n, depth)]
        drag_u = lap(lap(u, mask_e, mask_n, range(4)), mask_e, mask_n, both)
        drag_v = lap(lap(v, mask_e, mask_n, range(4)), mask_e, mask_n, both)
        p = [c + jnp.where(m, (CONTRACTION * b - EXPANSION * a) * th, 0.0) for c, m, a, b in zip(p, wet, t, s)]
        h = [c + jnp.where(m, th, 0.0) for c, m in zip(h, wet)]
        f_e = [jnp.where(m, y - c, 0.0) for m, y, c in zip(mask_e, ext_east(p), p)]
        f_n = [jnp.where(m, y - c, 0.0) for m, y, c in zip(mask_n, ext_north(p), p)]
        us, vs = [], []
        for i in both:
            grad_x = f_e[i] + west(f_e[i], f_e[LON_PARTNER[i]])
            grad_y = f_n[i] + south(f_n[i], f_n[LAT_PARTNER[i]])
            x = u[i] + coriolis[i] * v[i] - (0.5 * PRESSURE_SCALE) * grad_x - FRICTION * drag_u[i]
            y = v[i] - coriolis[i] * u[i] - (0.5 * PRESSURE_SCALE) * grad_y - FRICTION * drag_v[i]
            us.append(jnp.where(wet[i], x, 0.0))
            vs.append(jnp.where(wet[i], y, 0.0))
        us_ref[k] = us[0]
        vs_ref[k] = vs[0]
        return (p, h, [a + th * b for a, b in zip(tu, us)], [a + th * b for a, b in zip(tv, vs)])

    def step(i, carry):
        for j in range(TILES_PER_STEP):
            at = i * TILES_PER_STEP + j
            corners = corner_group(q_ref, r_ref, at, edges)
            for odd in range(2):
                carry = level(2 * at + odd, odd, at, corners, carry)
        return carry

    _, h, tu, tv = lax.fori_loop(0, last // TILES_PER_STEP, step, ([zero] * 4, [zero] * 4, [zero] * 2, [zero] * 2))
    start = [sea * z_ref[...], from_lat_group(g_ref[last], 1, 0), roll_sub(edge, 4), from_lat_group(corner, 1, 0)]
    drive = [sea * f_ref[...], from_lat_group(g_ref[last], 2, 0)]
    weight_e = [jnp.minimum(x, y) * (1.0 / levels) for x, y in zip(h, ext_east(h))]
    weight_n = [jnp.minimum(x, y) * (1.0 / levels) for x, y in zip(h, ext_north(h))]
    flux_e = [x * (y - c) for x, y, c in zip(weight_e, ext_east(start), start)]
    flux_n = [x * (y - c) for x, y, c in zip(weight_n, ext_north(start), start)]
    rights = []
    for i in both:
        spread = flux_e[i] - west(flux_e[i], flux_e[LON_PARTNER[i]]) + (flux_n[i] - south(flux_n[i], flux_n[LAT_PARTNER[i]]))
        base = drive[i] - (STORAGE * start[i] - spread)
        tu_e = jnp.where(sub == 7, 0.0, roll_sub(tu[i], -1))
        tu_w = jnp.where(sub == 0, 0.0, roll_sub(tu[i], 1))
        tv_n, tv_s = north(tv[i], tv[1 - i]), south(tv[i], tv[1 - i])
        rights.append(base - jnp.where(h[i] > 0.0, (0.5 * DIVERGENCE) * ((tu_e - tu_w) + (tv_n - tv_s)), 0.0))
    halo = jnp.where(lane < 16, roll_lane(h[1], 8), jnp.where(lane < 32, roll_lane(rights[1], 24), roll_lane(tu[1], 40)))
    halo = jnp.where(lane < 64, halo, roll_lane(roll_sub(halo, 4), 64))
    halo = jnp.where(sub < 4, halo, jnp.where(sub == 4, roll_sub(tu[0], 4), roll_sub(tu[0], -2)))
    chunk_ref[0] = h[0]
    chunk_ref[1] = rights[0]
    chunk_ref[2] = halo
    for i in range(3):
        st_ref[i] = start[i]


def tracer_kernel(th_ref, t_ref, s_ref, u_ref, v_ref, d_ref, m_ref, g_ref, q_ref, r_ref, after_ref, nt_ref, ns_ref):
    del after_ref
    levels = t_ref.shape[0]
    edges = lon_masks()
    depth = (d_ref[...] * m_ref[...]).astype(F32)
    depth_g = from_lat_group(g_ref[levels // 2], 0, 0)
    depth_h = lon_ghost(q_ref[levels], r_ref[levels], edges)
    low = [jnp.minimum(depth, n) for n in around(depth, depth_g, depth_h)]
    zero = jnp.zeros((8, 128), F32)

    def level(k, odd, j, carry):
        above_t, above_s = carry
        kf = floats(k) + 0.5
        below = jnp.minimum(k + 1, levels - 1)
        th, th_below = th_ref[k], th_ref[below]
        u, v, t, s = u_ref[k], v_ref[k], t_ref[k], s_ref[k]
        g, q_in, r_in = g_ref[j], q_ref[k], r_ref[k]
        u_h = lon_ghost(q_in, r_in, edges)
        t_h, s_h = lon_tracers(q_in, r_in, edges)
        v_g = from_lat_group(g, 1, odd)
        wet = depth > kf
        wet_below = (depth > kf + 1.0) & (k + 1 < levels)
        inv_space = 1.0 / (0.5 * (th + th_below))
        inv_th = MIXING / th
        flow = [0.25 * x for x in (u + east(u, u_h), west(u, u_h) + u, v + north(v, v_g), south(v, v_g) + v)]
        masks = [x > kf for x in low]
        fluxes = []
        for q, q_g, q_h, full_ref, above, out_ref in (
            (t, from_lat_group(g, 2, odd), t_h, t_ref, above_t, nt_ref),
            (s, from_lat_group(g, 3, odd), s_h, s_ref, above_s, ns_ref),
        ):
            q_e, q_w, q_n, q_s = around(q, q_g, q_h)
            f_e = jnp.where(masks[0], flow[0] * (q + q_e) - DIFFUSION * (q_e - q), 0.0)
            f_w = jnp.where(masks[1], flow[1] * (q_w + q) - DIFFUSION * (q - q_w), 0.0)
            f_n = jnp.where(masks[2], flow[2] * (q + q_n) - DIFFUSION * (q_n - q), 0.0)
            f_s = jnp.where(masks[3], flow[3] * (q_s + q) - DIFFUSION * (q - q_s), 0.0)
            vflux = jnp.where(wet_below, (full_ref[below] - q) * inv_space, 0.0)
            vertical = (vflux - above) * inv_th
            out_ref[k] = jnp.where(wet, q + (f_w - f_e + f_s - f_n) + vertical, 0.0)
            fluxes.append(vflux)
        return tuple(fluxes)

    def step(i, carry):
        for j in range(TILES_PER_STEP):
            at = i * TILES_PER_STEP + j
            for odd in range(2):
                carry = level(2 * at + odd, odd, at, carry)
        return carry

    lax.fori_loop(0, levels // 2 // TILES_PER_STEP, step, (zero, zero))


def slab_kernel(levels, own_ref, r_ref, q_ref, st_ref, sum_ref, flat_ref, we_s, wn_s, fac_s, inv_s, r_s, d_s, z_s):
    odd_group = jnp.full((GROUP, 128), lax.axis_index(LON[0]) % 2, jnp.int32) == 1

    def rows(i):
        own, q, r = (ref[pl.ds(i, GROUP, stride=24), :] for ref in (own_ref, q_ref, r_ref))
        return jnp.concatenate([jnp.where(odd_group, q, r), own, jnp.where(odd_group, r, q)], axis=0)

    here = GROUP + lax.axis_index(LON[1])
    right, left = here + 1, here - 1
    heights, tu = [], [None] * 8
    for p in range(8):
        packed = rows(16 + p % 4)
        at = 64 * (p // 4)
        heights.append(jnp.concatenate([rows(p), roll_lane(packed, -8 - at)], axis=1))
        r_s[p] = jnp.concatenate([rows(8 + p), roll_lane(packed, -24 - at)], axis=1)
        if p in (0, 7):
            tu[p] = jnp.concatenate([rows(20 if p == 0 else 21), roll_lane(packed, -40 - at)], axis=1)
    r_s[0] = r_s[0] + jnp.where(heights[0] > 0.0, (0.5 * DIVERGENCE) * roll_sub(tu[7], 1), 0.0)
    r_s[7] = r_s[7] - jnp.where(heights[7] > 0.0, (0.5 * DIVERGENCE) * roll_sub(tu[0], -1), 0.0)
    for p in range(8):
        h = heights[p]
        h_e = heights[p + 1] if p < 7 else roll_sub(heights[0], -1)
        we_s[p] = jnp.minimum(h, h_e) * (1.0 / levels)
        wn_s[p] = jnp.minimum(h, roll_lane(h, -1)) * (1.0 / levels)
    for p in range(8):
        w_w = we_s[p - 1] if p > 0 else roll_sub(we_s[7], 1)
        wn = wn_s[p]
        diag = STORAGE + we_s[p] + w_w + wn + roll_lane(wn, 1)
        if p > 0:
            diag = diag + w_w * fac_s[p - 1]
        inv = 1.0 / diag
        inv_s[p] = inv
        fac_s[p] = -we_s[p] * inv

    mid = 0.5 * (SPECTRUM_HIGH + SPECTRUM_LOW)
    half = 0.5 * (SPECTRUM_HIGH - SPECTRUM_LOW)
    ratio = mid / half

    def residuals():
        d, last = d_s[0], d_s[7]
        edge = we_s[7] * (roll_sub(d, -1) - last)
        f_w = roll_sub(edge, 1)
        for p in range(8):
            d_e = d_s[p + 1] if p < 7 else None
            f_e = we_s[p] * (d_e - d) if p < 7 else edge
            f_n = wn_s[p] * (roll_lane(d, -1) - d)
            yield r_s[p] - STORAGE * d + ((f_e - f_w) + (f_n - roll_lane(f_n, 1)))
            f_w, d = f_e, d_e

    def step(scale_old, scale_new, first):
        y = []
        for p, r in enumerate((r_s[p] for p in range(8)) if first else residuals()):
            if not first:
                r_s[p] = r
            y.append((r + we_s[p - 1] * y[p - 1] if p > 0 else r) * inv_s[p])
        x = None
        for p in range(7, -1, -1):
            x = y[p] if x is None else y[p] - fac_s[p] * x
            d = x * scale_new if first else scale_old * d_s[p] + scale_new * x
            d_s[p] = d
            z_s[p] = d if first else z_s[p] + d

    step(0.0, 1.0 / mid, True)
    rho = 1.0 / ratio
    for _ in range(ITERS - 1):
        rho_next = 1.0 / (2.0 * ratio - rho)
        step(rho_next * rho, 2.0 * rho_next / half, False)
        rho = rho_next
    total = jnp.zeros((GROUP, 128), F32)
    for r in residuals():
        r = r[GROUP : 2 * GROUP, 0:128]
        total = total + r * r
    total = jnp.sum(jnp.sum(total, axis=0, keepdims=True), axis=1, keepdims=True) + jnp.zeros((1, 128), F32)
    for i in range(sum_ref.shape[0]):
        sum_ref[i] = total

    both = jnp.concatenate([z_s[p, pl.ds(here, 1), :] for p in range(8)], axis=0)
    x_e, x_w = z_s[0, pl.ds(right, 1), :], z_s[7, pl.ds(left, 1), :]
    x, x_g = both[:, 0:128], both[:, 128:256]
    sub = subs()
    x_e = jnp.broadcast_to(x_e[:, 0:128], (8, 128))
    x_w = jnp.broadcast_to(x_w[:, 0:128], (8, 128))
    x_h = jnp.where(sub < 4, x_e, x_w)
    x, x_g, x_h = x + st_ref[0], x_g + st_ref[1], x_h + st_ref[2]
    e, w, n, s = around(x, x_g, x_h)
    flat_ref[0] = (0.5 * GRAVITY) * (e - w)
    flat_ref[1] = (0.5 * GRAVITY) * (n - s)
    flat_ref[2] = x


def velocity_kernel(us_ref, vs_ref, d_ref, m_ref, flat_ref, nu_ref, nv_ref, surf_ref):
    depth = (d_ref[...] * m_ref[...]).astype(F32)
    slope_x, slope_y = flat_ref[0], flat_ref[1]
    surf_ref[...] = flat_ref[2]
    for k in range(us_ref.shape[0]):
        wet = depth > k + 0.5
        nu_ref[k] = jnp.where(wet, us_ref[k] - slope_x, 0.0)
        nv_ref[k] = jnp.where(wet, vs_ref[k] - slope_y, 0.0)


def call(kernel, name, outs, in_specs, scratch=(), aliases=None):
    return pl.pallas_call(
        kernel,
        name=name,
        out_shape=outs,
        in_specs=in_specs,
        out_specs=jax.tree.map(lambda _: VMEM, outs),
        scratch_shapes=list(scratch),
        input_output_aliases=aliases or {},
        compiler_params=pltpu.CompilerParams(vmem_limit_bytes=48 << 20),
    )


def from_all(x, axes):
    size = 1
    for axis in axes:
        size *= lax.axis_size(axis)
    copies = jnp.broadcast_to(x[None], (size, *x.shape))
    return lax.all_to_all(copies, axes, 0, 0, tiled=True)


def per_device(lon_size, lat_size, temp, salt, u, v, strata, sea, thickness, elevation, drive):
    levels = temp.shape[0]
    top = lat_size - 1
    pairs_a = [(i, i ^ 1) for i in range(lat_size)]
    pairs_b = []
    for a in range(lon_size):
        for i in range(1, top, 2):
            pairs_b += [(a * lat_size + i, a * lat_size + i + 1), (a * lat_size + i + 1, a * lat_size + i)]
        pairs_b.append((a * lat_size + top, (lon_size - 1 - a) * lat_size + top))

    def lat_swap(x):
        return lax.ppermute(x, "lat", pairs_a), lax.ppermute(x, (*LON, "lat"), pairs_b)

    def tiles(n, kind=F32):
        return jax.ShapeDtypeStruct((n, 8, 128), kind)

    field, flat = tiles(levels), (8, 128)
    message, packed = tiles(levels + 2), tiles(levels // 2 + 1)
    own = (temp, salt, u, v, strata, sea, elevation, drive)

    flat_int, flat_float = jax.ShapeDtypeStruct(flat, jnp.int32), jax.ShapeDtypeStruct(flat, F32)
    edges, *own = call(
        lat_pack_kernel,
        "lat_pack",
        (packed, *[field] * 4, flat_int, flat_int, flat_float, flat_float),
        [pl.BlockSpec(memory_space=pltpu.HBM)] * 8,
        [pltpu.SemaphoreType.DMA((3, 4))],
    )(*[pltpu.with_memory_space_constraint(x, pltpu.HBM) for x in own])
    temp, salt, u, v, strata, sea = own[:6]
    got_a, got_b = lat_swap(edges)
    thick = jnp.broadcast_to(thickness[:, None, None], field.shape)
    rows_q, rows_r = call(lon_rows_kernel, "lon_rows", (message, message), [VMEM] * 8)(*own)
    corners = functools.partial(corners_kernel, top)
    ghost, pair_r, pair_q = call(corners, "corners", (packed, message, message), [VMEM] * 4, aliases={2: 1, 3: 2})(
        got_a, got_b, rows_r, rows_q
    )
    pair_r = lax.ppermute(pair_r, LON, [(i, (i + 1 if i % 2 else i - 1) % lon_size) for i in range(lon_size)])
    pair_q = lax.ppermute(pair_q, LON, [(i, i ^ 1) for i in range(lon_size)])
    u_star, v_star, chunk, start = call(
        functools.partial(momentum_kernel, lat_size), "momentum", (field, field, tiles(3), tiles(3)), [VMEM] * 12
    )(thick, *own, ghost, pair_r, pair_q)
    group = from_all(chunk, ("lon_lo",)).reshape(GROUP * 24, 128)
    group, after = lax.optimization_barrier((group, chunk))
    groups = lon_size // GROUP
    group_q = lax.ppermute(group, "lon_hi", [(i, i ^ 1) for i in range(groups)])
    group_r = lax.ppermute(group, "lon_hi", [(i, (i + 1 if i % 2 else i - 1) % groups) for i in range(groups)])
    new_temp, new_salt = call(tracer_kernel, "tracers", (field, field), [VMEM] * 11)(
        thick, temp, salt, u, v, strata, sea, ghost, pair_q, pair_r, after
    )
    group_q, group_r, new_temp, new_salt = lax.optimization_barrier((group_q, group_r, new_temp, new_salt))
    sums, solved = call(
        functools.partial(slab_kernel, levels),
        "slab",
        (jax.ShapeDtypeStruct((groups * lat_size, 1, 128), F32), tiles(3)),
        [VMEM] * 4,
        [pltpu.VMEM((8, 3 * GROUP, 256), F32)] * 7,
    )(group, group_r, group_q, start)
    sums = lax.all_to_all(sums, ("lon_hi", "lat"), 0, 0, tiled=True)
    total = jnp.sum(sums, axis=0)
    cells = lon_size * 8 * lat_size * 128
    rms = jnp.sqrt(total[0, 0] / cells + EPSILON)
    new_u, new_v, surface = call(velocity_kernel, "velocity", (field, field, flat_float), [VMEM] * 5)(
        u_star, v_star, strata, sea, solved
    )
    return (new_temp, new_salt, new_u, new_v, surface, rms)


def solution(mesh):
    lon_size, lat_size = mesh.shape["lon"], mesh.shape["lat"]
    finer = Mesh(mesh.devices.reshape(lon_size // GROUP, GROUP, lat_size), (*LON, "lat"))
    cube, flat = P(None, LON, "lat"), P(LON, "lat")
    return jax.shard_map(
        functools.partial(per_device, lon_size, lat_size),
        mesh=finer,
        in_specs=(cube, cube, cube, cube, flat, flat, P(), flat, flat),
        out_specs=(cube, cube, cube, cube, flat, P()),
        check_vma=False,
    )
```
